128 devices in a mesh: rows: 16 (over y_lo, x, core), band: 8 (over y_hi, z).
Axes of the slice: x: 4, y: 4 (y_hi: 2, y_lo: 2; y = y_hi * 2 + y_lo), z: 4, core: 2. Of those that a mesh axis runs over, the one named last changes fastest.
Arguments:
- pan_image: float32 [768, 12288], P('rows', 'band'), may hold values from -1 to 17
- vnir_bands: float32 [8, 192, 3072], P('band', 'rows'), may hold values from -13 to 13
- swir_bands: float32 [8, 64, 1024], P('band', 'rows'), may hold values from -12 to 12
Outputs:
- joined_vnir: float32 [8, 768, 12288], P(None, 'rows', 'band')
- joined_swir: float32 [8, 192, 3072], P(None, 'rows', 'band')
The draws below stay inside these ranges and needn't reach their ends.
All inputs are finite; a program needn't handle non-finite values.
Results may differ from the reference program's by a relative error of at most 0.00023.
Values sent between devices are 32-bit elements; how exact they have to be, the bound alone decides.
A program may use at most 128 MiB of HBM per device.

```python
import math
import jax
import jax.numpy as jnp
import numpy as np
from jax import lax

BANDS = 8
SWIR_BANDS = 8
RATIO_V = 4
RATIO_S = 3
TAPS_V = 17
TAPS_S = 13
WIDTH = 12288
HEIGHT = 768


def scene_field(key):
    base_key = jax.random.fold_in(key, 11)
    rough_part = jax.random.truncated_normal(jax.random.fold_in(base_key, 1), -3.0, 3.0, (HEIGHT, WIDTH), jnp.float32)
    coarse = jax.random.truncated_normal(jax.random.fold_in(base_key, 2), -3.0, 3.0, (HEIGHT // 4, WIDTH // 4), jnp.float32)
    smooth = jnp.repeat(jnp.repeat(coarse, 4, axis=0), 4, axis=1)
    row_pos = jnp.arange(HEIGHT, dtype=jnp.float32)[:, None] / max(HEIGHT - 1, 1)
    row_ramp = 1.0 + 2.0 * row_pos
    level = -1.0 + 2.0 * row_pos
    return level + row_ramp * (0.3 * rough_part + 0.3 * smooth)


def draw_pan_image(key, part):
    scene = scene_field(key)
    speckle = jax.random.truncated_normal(jax.random.fold_in(key, 31), -3.0, 3.0, (HEIGHT, WIDTH), jnp.float32)
    return 8.0 + scene + 0.3 * speckle


def draw_vnir_bands(key, part):
    scene = scene_field(key)
    factors = jax.random.uniform(jax.random.fold_in(key, 21), (BANDS,), jnp.float32, 0.5, 1.5)
    blocks = scene.reshape(HEIGHT // 4, 4, WIDTH // 4, 4).mean(axis=(1, 3))
    band_noise = jax.random.truncated_normal(jax.random.fold_in(key, 22), -3.0, 3.0, (BANDS, HEIGHT // 4, WIDTH // 4), jnp.float32)
    return factors[:, None, None] * blocks[None] + 0.5 * band_noise


def draw_swir_bands(key, part):
    scene = scene_field(key)
    factors = jax.random.uniform(jax.random.fold_in(key, 41), (SWIR_BANDS,), jnp.float32, 0.3, 1.5)
    blocks = scene.reshape(HEIGHT // 12, 12, WIDTH // 12, 12).mean(axis=(1, 3))
    band_noise = jax.random.truncated_normal(jax.random.fold_in(key, 42), -3.0, 3.0, (SWIR_BANDS, HEIGHT // 12, WIDTH // 12), jnp.float32)
    return factors[:, None, None] * blocks[None] + 0.3 * band_noise


def setup_inputs(seed: int = 0) -> dict:
    splits = jax.random.split(jax.random.key(seed), 4)
    return {
        "pan_image": draw_pan_image(jax.random.fold_in(splits[3], 71), 0),
        "vnir_bands": draw_vnir_bands(jax.random.fold_in(splits[3], 71), 0),
        "swir_bands": draw_swir_bands(jax.random.fold_in(splits[3], 71), 0),
    }


NYQUIST_GAIN = 0.29

def gauss_taps(upscale, kernel_len):
    spread = upscale * math.sqrt(-2.0 * math.log(NYQUIST_GAIN)) / math.pi
    radius = kernel_len // 2
    offsets = np.arange(-radius, radius + 1) * 1.0
    values = np.exp(-offsets ** 2 / (2.0 * spread ** 2))
    return values / values.sum()

def cubic_weight(distance):
    distance = abs(distance)
    if distance <= 1.0:
        return 1.5 * distance ** 3 - 2.5 * distance ** 2 + 1.0
    if distance < 2.0:
        return -0.5 * distance ** 3 + 2.5 * distance ** 2 - 4.0 * distance + 2.0
    return 0.0

def cubic_table(upscale):
    weights = np.zeros((5, upscale))
    for phase_index in range(upscale):
        centre = (phase_index + 0.5) / upscale - 0.5
        first_tap = math.floor(centre)
        fraction = centre - first_tap
        for tap_index in range(-1, 3):
            weights[first_tap + tap_index + 2, phase_index] += cubic_weight(tap_index - fraction)
    return weights

def pad_axis(field, along, margin):
    widths = [(0, 0)] * field.ndim
    widths[along] = (margin, margin)
    return jnp.pad(field, widths)

def filter_axis(padded, kernel, along):
    length = padded.shape[along] - len(kernel) + 1
    running = float(kernel[0]) * lax.slice_in_dim(padded, 0, length, axis=along)
    for offset in range(1, len(kernel)):
        running = running + float(kernel[offset]) * lax.slice_in_dim(padded, offset, offset + length, axis=along)
    return running

def upsample_axis(padded, upscale, along):
    weights = cubic_table(upscale)
    length = padded.shape[along] - 4
    phases = []
    for phase_index in range(upscale):
        running = float(weights[0, phase_index]) * lax.slice_in_dim(padded, 0, length, axis=along)
        for offset in range(1, 5):
            running = running + float(weights[offset, phase_index]) * lax.slice_in_dim(padded, offset, offset + length, axis=along)
        phases.append(running)
    stacked = jnp.stack(phases, axis=along + 1)
    new_shape = padded.shape[:along] + (length * upscale,) + padded.shape[along + 1:]
    return stacked.reshape(new_shape)

def moments(layers):
    flattened = layers.reshape(layers.shape[0], -1)
    products = jnp.dot(flattened.astype(jnp.float32), flattened.T.astype(jnp.float32), precision=lax.Precision.HIGHEST, preferred_element_type=jnp.float32)
    return (products, lax.optimization_barrier(jnp.sum(flattened, axis=1)))

def covariance(products, totals, pixels):
    averages = totals / pixels
    return products / pixels - averages[:, None] * averages[None, :]

def solve_spd(matrix, rhs):
    factor = jnp.linalg.cholesky(matrix)
    lower_sol = lax.linalg.triangular_solve(factor, rhs, left_side=True, lower=True)
    return lax.linalg.triangular_solve(factor, lower_sol, left_side=True, lower=True, transpose_a=True)

def first_gains(products, totals, pixels):
    cov_all = covariance(products, totals, pixels)
    inputs_cov = cov_all[:BANDS, :BANDS]
    cross_cov = cov_all[:BANDS, BANDS:]
    weights = solve_spd(inputs_cov, cross_cov)
    return cross_cov[:, 0] / jnp.sum(cross_cov[:, 0] * weights[:, 0])

def second_fit(products, totals, pixels):
    cov_all = covariance(products, totals, pixels)
    inputs_cov = cov_all[:BANDS, :BANDS]
    cross_cov = cov_all[:BANDS, BANDS:]
    target = lax.optimization_barrier(jnp.mean(cross_cov, axis=1, keepdims=True))
    weights = solve_spd(inputs_cov, target)[:, 0]
    numerators = lax.optimization_barrier(jnp.sum(weights[:, None] * cross_cov, axis=0))
    return (weights, numerators / jnp.sum(weights * target[:, 0]))

def reference(pan_image, vnir_bands, swir_bands):
    kernel_fine = gauss_taps(RATIO_V, TAPS_V)
    kernel_coarse = gauss_taps(RATIO_S, TAPS_S)
    padded = jnp.pad(pan_image, TAPS_V // 2)
    pan_low = filter_axis(filter_axis(padded, kernel_fine, 0), kernel_fine, 1)
    vnir_up = upsample_axis(pad_axis(upsample_axis(pad_axis(vnir_bands, 1, 2), RATIO_V, 1), 2, 2), RATIO_V, 2)
    products, totals = moments(jnp.concatenate([vnir_up, pan_low[None]], axis=0))
    gain_bands = first_gains(products, totals, HEIGHT * WIDTH)
    joined_vnir = vnir_up + gain_bands[:, None, None] * (pan_image - pan_low)[None]
    synthetic = joined_vnir.reshape(BANDS, HEIGHT // RATIO_V, RATIO_V, WIDTH // RATIO_V, RATIO_V).mean(axis=(2, 4))
    synth_pad = pad_axis(pad_axis(synthetic, 1, TAPS_S // 2), 2, TAPS_S // 2)
    synthetic_low = filter_axis(filter_axis(synth_pad, kernel_coarse, 1), kernel_coarse, 2)
    swir_up = upsample_axis(pad_axis(upsample_axis(pad_axis(swir_bands, 1, 2), RATIO_S, 1), 2, 2), RATIO_S, 2)
    products_two, totals_two = moments(jnp.concatenate([synthetic_low, swir_up], axis=0))
    weights, shares = second_fit(products_two, totals_two, HEIGHT // 4 * (WIDTH // 4))
    detail = jnp.einsum('b,bij->ij', weights, synthetic - synthetic_low, precision=lax.Precision.HIGHEST)
    joined_swir = swir_up + shares[:, None, None] * detail[None]
    return (joined_vnir, joined_swir)
```

```python
import functools
import math

import jax
import jax.numpy as jnp
import ml_dtypes
import numpy as np
from jax import lax
from jax.experimental import pallas as pl
from jax.experimental.pallas import tpu as pltpu
from jax.sharding import PartitionSpec as P

F32 = jnp.float32
BF16 = jnp.bfloat16
MESH = pl.DeviceIdType.MESH
VM = pltpu.VMEM

BANDS = 8
STRIPS = 16
BLOCKS = 8
HEIGHT = 768
WIDTH = 12288
N1 = float(HEIGHT * WIDTH)
N2 = float(HEIGHT * WIDTH // 16)
NYQUIST_GAIN = 0.29


def gauss_taps(upscale, kernel_len):
    spread = upscale * math.sqrt(-2.0 * math.log(NYQUIST_GAIN)) / math.pi
    radius = kernel_len // 2
    offsets = np.arange(-radius, radius + 1) * 1.0
    values = np.exp(-(offsets**2) / (2.0 * spread**2))
    return values / values.sum()


def cubic_weight(distance):
    distance = abs(distance)
    if distance <= 1.0:
        return 1.5 * distance**3 - 2.5 * distance**2 + 1.0
    if distance < 2.0:
        return -0.5 * distance**3 + 2.5 * distance**2 - 4.0 * distance + 2.0
    return 0.0


def cubic_table(upscale):
    weights = np.zeros((5, upscale))
    for phase_index in range(upscale):
        centre = (phase_index + 0.5) / upscale - 0.5
        first_tap = math.floor(centre)
        fraction = centre - first_tap
        for tap_index in range(-1, 3):
            weights[first_tap + tap_index + 2, phase_index] += cubic_weight(tap_index - fraction)
    return weights


C4 = cubic_table(4)
C3 = cubic_table(3)
G4 = gauss_taps(4, 17)
G3 = gauss_taps(3, 13)
MEAN_TAPS = C4.mean(axis=1)


def split(matrix):
    high = matrix.astype(np.float32).astype(ml_dtypes.bfloat16)
    low = (matrix - high.astype(np.float64)).astype(ml_dtypes.bfloat16)
    return high, low


def tables():
    up_rows = np.zeros((48, 16))
    for m in range(12):
        for p in range(4):
            for t in range(5):
                up_rows[4 * m + p, m + t] += C4[t, p]
    up_cols = np.zeros((1536, 512))
    for m in range(384):
        for p in range(4):
            for t in range(5):
                up_cols[4 * m + p, (m + t - 2) % 512] += C4[t, p]
    gram_rows = up_rows.T @ up_rows
    gram_cols = up_cols.T @ up_cols
    lanes = np.zeros((16, 512), np.float32)
    at = np.arange(512)
    for t in range(-4, 5):
        lanes[t + 4] = gram_cols[at, (at + t) % 512]
    lanes[9] = up_cols.sum(axis=0)
    row_sum = up_rows.sum(axis=0)

    low = np.zeros((96, 112))
    for f in range(96):
        for t in range(17):
            low[f, f + t] = G4[t]
    mean = np.zeros((24, 112))
    mean_low = np.zeros((24, 112))
    for i in range(24):
        mean[i, 8 + 4 * i : 12 + 4 * i] = 0.25
        mean_low[i] = low[4 * i : 4 * i + 4].mean(axis=0)
    g3_rows = np.zeros((12, 24))
    for i in range(12):
        g3_rows[i, i : i + 13] = G3
    row_stack = []
    for variant in range(3):
        keep = np.ones((24, 1))
        if variant == 0:
            keep[:6] = 0.0
        if variant == 2:
            keep[18:] = 0.0
        row_stack.append(
            np.concatenate(
                [
                    low[24:72],
                    up_rows.T @ low[24:72],
                    mean_low[6:18],
                    g3_rows @ (keep * mean_low),
                    mean[6:18],
                    g3_rows @ (keep * mean),
                ]
            )
        )
    rows_hi, rows_lo = split(np.stack(row_stack))

    low_cols = np.zeros((256, 128))
    for o in range(128):
        for t in range(-8, 9):
            q = o + t
            row = q if 0 <= q < 128 else (q if q >= 128 else 256 + q)
            low_cols[row, o] = G4[t + 8]
    mean_cols = np.zeros((640, 128))
    for f in range(512):
        mean_cols[f, f // 4] = 0.25
    for f in range(32):
        mean_cols[512 + f, f // 4] = 0.25
        mean_cols[512 + 96 + f, 120 + f // 4] = 0.25
    back_cols = np.zeros((640, 128))
    for n in range(128):
        for t in range(5):
            for p in range(4):
                f = 4 * (n - (t - 2)) + p
                row = f if f >= 0 else 640 + f
                back_cols[row, n] += C4[t, p]
    fine = np.zeros((256, 512))
    for m in range(128):
        for p in range(4):
            for t in range(5):
                fine[(m + t - 2) % 256, 4 * m + p] += C4[t, p]
    third = np.zeros((256, 384))
    for m in range(128):
        for p in range(3):
            for t in range(5):
                third[(m + t - 2) % 256, 3 * m + p] += C3[t, p]
    constants = (
        rows_hi,
        rows_lo,
        *split(low_cols),
        mean_cols.astype(ml_dtypes.bfloat16),
        *split(back_cols),
        *split(fine),
        *split(third),
        lanes,
    )
    return constants, gram_rows, row_sum, up_rows


CONSTANTS, GRAM_ROWS, ROW_SUM, UP_ROWS = tables()
NUM_CONST = len(CONSTANTS)


def halves(x):
    high = x.astype(BF16)
    return high, (x - high.astype(F32)).astype(BF16)


def mm(a, b):
    return jnp.dot(a, b, preferred_element_type=F32)


def dot3(x, high, low):
    xh, xl = halves(x)
    return mm(xh, high) + mm(xl, high) + mm(xh, low)


def dot2(x, exact):
    xh, xl = halves(x)
    return mm(xh, exact) + mm(xl, exact)


def lane(shape):
    return lax.broadcasted_iota(jnp.int32, shape, len(shape) - 1)


def edge(next_tile, prev_tile):
    return jnp.where(lane(next_tile.shape) < 64, next_tile, prev_tile)


def shifted(x, t):
    n = x.shape[1]
    return x if t == 0 else pltpu.roll(x, (-t) % n, 1)


def col_filter(x, taps):
    radius = len(taps) // 2
    total = float(taps[radius]) * x
    for t in range(-radius, radius + 1):
        if t:
            total = total + float(taps[t + radius]) * shifted(x, t)
    return total


def pick(e, strip, row, tile):
    return e[strip, tile, pl.ds(row, 8, stride=8), :]


def vnir_row(e, strip, i):
    if i < 8:
        parts = [pick(e, strip, i, t) for t in range(3)] + [pick(e, strip, i, 5)]
    else:
        j = i - 8
        parts = [
            pick(e, strip, j, 3),
            pick(e, strip, 4 + j, 3),
            pick(e, strip, j, 4),
            pltpu.roll(pick(e, strip, j, 5), 64, 1),
        ]
    return jnp.concatenate(parts, axis=1)


def swir_row(e, strip, j):
    return jnp.concatenate(
        [pick(e, strip, 4 + j, 4), pltpu.roll(pick(e, strip, 4 + j, 5), 64, 1)], axis=1
    )


def fold(x):
    total = x[:, 0:128]
    for t in range(1, x.shape[1] // 128):
        total = total + x[:, 128 * t : 128 * t + 128]
    return total


def pack(vs, ss, sb):
    for d in range(BLOCKS):
        left, right = 384 * d - 128, 384 * d + 384

        def halo(ref, rows, at, after, width):
            shape = (rows[1] - rows[0], 128)
            prev = ref[rows[0] : rows[1], at : at + 128] if at >= 0 else jnp.zeros(shape, F32)
            nxt = ref[rows[0] : rows[1], after : after + 128] if after < width else jnp.zeros(shape, F32)
            return edge(nxt, prev)

        for t in range(3):
            sb[d, t] = vs[0:8, 384 * d + 128 * t : 384 * d + 128 * t + 128]
        sb[d, 3, 0:4] = vs[8:12, 384 * d : 384 * d + 128]
        sb[d, 3, 4:8] = vs[8:12, 384 * d + 128 : 384 * d + 256]
        sb[d, 4, 0:4] = vs[8:12, 384 * d + 256 : 384 * d + 384]
        sb[d, 4, 4:8] = ss[0:4, 128 * d : 128 * d + 128]
        sb[d, 5, 0:4] = halo(vs, (8, 12), left, right, 3072)
        sb[d, 5, 4:8] = halo(ss, (0, 4), 128 * d - 128, 128 * d + 128, 1024)
        other = pltpu.roll(sb[d, 5], 64, 1)
        own = halo(vs, (0, 8), left, right, 3072)
        at = lane((8, 128))
        sb[d, 5] = jnp.where((at >= 32) & (at < 96), other, own)


def pan_stage(pan_ext, consts, variant, d_out, ts, dd):
    rows_hi, rows_lo, low_hi, low_lo, mean_c, back_hi, back_lo = consts[:7]
    halo = edge(pan_ext[:, 1664:1792], pan_ext[:, 1536:1664])
    full = jnp.concatenate([pan_ext[:, 0:1536], halo], axis=1)
    fh, fl = halves(full)
    rh, rl = rows_hi[variant], rows_lo[variant]
    q = mm(rh, fh) + mm(rh, fl) + mm(rl, fh)
    top = q[0:88]
    tiles = [top[:, 128 * j : 128 * j + 128] for j in range(13)]
    lhs = jnp.concatenate(
        [
            jnp.concatenate([tiles[j], edge(tiles[(j + 1) % 13], tiles[(j + 12) % 13])], axis=1)
            for j in range(13)
        ],
        axis=0,
    )
    low = dot3(lhs, low_hi[...], low_lo[...])
    low_tile = [low[88 * j : 88 * j + 88] for j in range(13)]
    total = jnp.zeros((8, 128), F32)
    for j in range(12):
        d_out[:, 128 * j : 128 * j + 128] = (
            pan_ext[32:80, 128 * j : 128 * j + 128] - low_tile[j][0:48]
        )
        for k in range(6):
            total = total + low_tile[j][8 * k : 8 * k + 8]
    zero = jnp.zeros((16, 128), F32)
    back = [low_tile[j][48:64] for j in range(12)] + [zero]
    lhs = jnp.concatenate(
        [
            jnp.concatenate(
                back[4 * t : 4 * t + 4] + [edge(back[4 * t + 4], back[(4 * t + 12) % 13])], axis=1
            )
            for t in range(3)
        ],
        axis=0,
    )
    main = dot3(lhs, back_hi[...], back_lo[...])
    rim = dot3(edge(back[0], back[11]), back_hi[512:640], back_lo[512:640])
    for t in range(3):
        ts[:, 128 * t : 128 * t + 128] = main[16 * t : 16 * t + 16]
    ts[:, 384:512] = rim
    diff = [q[88:112, 128 * j : 128 * j + 128] - low_tile[j][64:88] for j in range(13)]
    lhs = jnp.concatenate(
        [jnp.concatenate(diff[4 * t : 4 * t + 4], axis=1) for t in range(3)], axis=0
    )
    main = dot2(lhs, mean_c[0:512])
    for t in range(3):
        dd[0:24, 128 * t : 128 * t + 128] = main[24 * t : 24 * t + 24]
    dd[0:24, 384:512] = dot2(diff[12], mean_c[512:640])
    return total


def column_mask(block):
    at = lane((1, 512))
    left = jnp.where(block == 0, 0.0, 1.0)
    right = jnp.where(block == BLOCKS - 1, 0.0, 1.0)
    return jnp.where(at >= 448, left, jnp.where(at >= 384, right, 1.0))


def front_compute(e, pan_ext, consts, r, c, d_out, ts, dd, xs, ys, lvs, vl, swu, dl, rl):
    third_hi, third_lo, lanes = consts[9:12]
    variant = jnp.where(r == 0, 0, jnp.where(r == STRIPS - 1, 2, 1))
    sums = {}
    sums[10] = pan_stage(pan_ext, consts, variant, d_out, ts, dd)
    for k in range(28):
        strip, i = (0, k + 4) if k < 8 else ((1, k - 8) if k < 20 else (2, k - 20))
        xs[k] = vnir_row(e, strip, i)
    for i in range(16):
        total = None
        for j in range(16):
            if GRAM_ROWS[i, j] != 0.0:
                term = float(GRAM_ROWS[i, j]) * xs[j + 6]
                total = term if total is None else total + term
        y = lanes[4:5, :] * total
        for t in range(-4, 5):
            if t:
                y = y + lanes[t + 4 : t + 5, :] * shifted(total, t)
        ys[i] = y
    acc = [jnp.zeros((8, 128), F32) for _ in range(10)]
    ones = lanes[9:10, :]
    for i in range(16):
        x = xs[i + 6]
        for j in range(8):
            acc[j] = acc[j] + fold(x * ys[i, j : j + 1, :])
        acc[8] = acc[8] + fold(x * ts[i : i + 1, :])
        acc[9] = acc[9] + float(ROW_SUM[i]) * fold(x * ones)
    for k in range(10):
        sums[k] = acc[k]
    up_keep = jnp.where(r == 0, 0.0, 1.0)
    down_keep = jnp.where(r == STRIPS - 1, 0.0, 1.0)
    mask = column_mask(c)
    mean_rows = []
    for i in range(24):
        total = None
        for t in range(5):
            term = float(MEAN_TAPS[t]) * xs[i + t]
            total = term if total is None else total + term
        if i < 6:
            total = total * up_keep
        if i >= 18:
            total = total * down_keep
        mean_rows.append(total)
    for i in range(12):
        total = float(G3[6]) * mean_rows[i + 6]
        for t in range(6):
            total = total + float(G3[t]) * (mean_rows[i + t] + mean_rows[i + 12 - t])
        lowered = col_filter(total, MEAN_TAPS) * mask
        lowered = col_filter(lowered, G3)[:, 0:384]
        lvs[i] = lowered
        vl[i] = col_filter(mean_rows[i + 6], MEAN_TAPS)[:, 0:384] - lowered
    dcol = dd[8:24, :] * mask
    dcol = col_filter(dcol, G3)[:, 0:384]
    low_d = dcol[4:16]
    dl[...] = dd[0:12, 0:384] - low_d
    ts[0:12, 0:384] = low_d
    srow = [
        swir_row(e, *at)
        for at in ((0, 2), (0, 3), (1, 0), (1, 1), (1, 2), (1, 3), (2, 0), (2, 1))
    ]
    up = []
    for m in range(4):
        for p in range(3):
            total = None
            for t in range(5):
                if C3[t, p] != 0.0:
                    term = float(C3[t, p]) * srow[m + t]
                    total = term if total is None else total + term
            up.append(total)
    swu[...] = dot3(jnp.concatenate(up, axis=0), third_hi[...], third_lo[...])
    acc = [jnp.zeros((8, 128), F32) for _ in range(22)]
    for i in range(12):
        lv = lvs[i]
        sw = swu[8 * i : 8 * i + 8, :]
        ld = ts[i : i + 1, 0:384]
        for j in range(8):
            other = lvs[i, j : j + 1, :]
            acc[j] = acc[j] + fold(lv * other)
            acc[8 + j] = acc[8 + j] + fold(sw * other)
        acc[16] = acc[16] + fold(lv * ld)
        acc[17] = acc[17] + fold(sw * ld)
        acc[18] = acc[18] + fold(lv)
        acc[19] = acc[19] + fold(sw)
        acc[20] = acc[20] + fold(ld)
        acc[21] = acc[21] + fold(ld * ld)
    for k in range(22):
        sums[16 + k] = acc[k]
    at = lane((8, 128))
    packed = jnp.zeros((8, 128), F32)
    for k, value in sums.items():
        packed = jnp.where(at == k, jnp.sum(value, axis=1, keepdims=True), packed)
    rl[...] = packed


def upsample(xs, consts, zs, up_out):
    fine_hi, fine_lo = consts[7:9]
    for m in range(12):
        for p in range(4):
            total = None
            for t in range(5):
                if C4[t, p] != 0.0:
                    term = float(C4[t, p]) * xs[m + t + 6]
                    total = term if total is None else total + term
            for tile in range(4):
                zs[tile, pl.ds(4 * m + p, 8, stride=48), :] = total[
                    :, 128 * tile : 128 * tile + 128
                ]

    @pl.loop(0, BANDS)
    def _(b):
        at = pl.ds(pl.multiple_of(b * 48, 48), 48)
        z = [zs[k, at, :] for k in range(4)]
        lhs = jnp.concatenate(
            [
                jnp.concatenate([z[k], edge(z[k + 1], z[(k + 3) % 4])], axis=1)
                for k in range(3)
            ],
            axis=0,
        )
        up = dot3(lhs, fine_hi[...], fine_lo[...])
        for k in range(3):
            up_out[at, 512 * k : 512 * k + 512] = up[48 * k : 48 * k + 48]


def front_kernel(pan, vnir, swir, *rest):
    hbm_consts = rest[:NUM_CONST]
    rt, up_out, d_out, vl, swu, dl = rest[NUM_CONST : NUM_CONST + 6]
    rest = rest[NUM_CONST + 6 :]
    consts = rest[:NUM_CONST]
    (vs, ss, sb, e, pe, xs, ys, ts, dd, lvs, zs, rl, g1, mid, g2) = rest[NUM_CONST : NUM_CONST + 15]
    (csem, lsem, ssem, rsem, fsem, hsem, psem, qsem, g1s, g1r, g2s, g2r) = rest[NUM_CONST + 15 :]
    r = lax.axis_index("rows")
    c = lax.axis_index("band")

    def remote(src, dst, send, recv, row, block):
        return pltpu.make_async_remote_copy(
            src_ref=src, dst_ref=dst, send_sem=send, recv_sem=recv,
            device_id=(row, block), device_id_type=MESH,
        )

    rl8 = lax.rem(r, 8)
    base = r - rl8
    q = base + c
    barrier = pltpu.get_barrier_semaphore()

    def greet(row, block):
        pl.semaphore_signal(barrier, inc=1, device_id=(row, block), device_id_type=MESH)

    first = [(base + lax.rem(rl8 + k, 8), c) for k in range(1, 8)]
    second = []
    for k in range(1, 16):
        q2 = lax.rem(q + k, 16)
        c2 = lax.rem(q2, 8)
        second.append((q2 - c2 + rl8, c2))
    around = [(lax.rem(r + 1, STRIPS), c), (lax.rem(r + STRIPS - 1, STRIPS), c)]
    partners = first + second + around
    for row, block in partners:
        greet(row, block)

    loads = [
        pltpu.make_async_copy(vnir.at[0], vs, lsem.at[0]),
        pltpu.make_async_copy(swir.at[0], ss, lsem.at[1]),
        pltpu.make_async_copy(pan, pe.at[pl.ds(32, 48), pl.ds(0, 1536)], lsem.at[2]),
    ]
    for copy in loads:
        copy.start()
    const_loads = [
        pltpu.make_async_copy(hbm_consts[k], consts[k], csem.at[k]) for k in range(NUM_CONST)
    ]
    for copy in const_loads:
        copy.start()

    @pl.when(r == 0)
    def _():
        pe[0:32, :] = jnp.zeros((32, 1792), F32)
        e[0] = jnp.zeros((6, 64, 128), F32)

    @pl.when(r == STRIPS - 1)
    def _():
        pe[80:112, :] = jnp.zeros((32, 1792), F32)
        e[2] = jnp.zeros((6, 64, 128), F32)

    @pl.when(c == 0)
    def _():
        pe[32:80, 1536:1664] = jnp.zeros((48, 128), F32)

    @pl.when(c == BLOCKS - 1)
    def _():
        pe[32:80, 1664:1792] = jnp.zeros((48, 128), F32)

    loads[0].wait()
    loads[1].wait()
    pack(vs, ss, sb)
    loads[2].wait()
    pl.semaphore_wait(barrier, len(partners))

    def pan_cols(side):
        src = pe.at[pl.ds(32, 48), pl.ds(1408, 128)] if side == 0 else pan_first
        dst = pe.at[pl.ds(32, 48), pl.ds(1536 + 128 * side, 128)]
        block = c + 1 if side == 0 else c - 1
        return remote(src, dst, psem.at[side], qsem.at[side], r, block)

    pan_first = pe.at[pl.ds(32, 48), pl.ds(0, 128)]

    def pan_rows(side):
        src = pe.at[pl.ds(48, 32), pl.ds(0, 1536)] if side == 0 else pe.at[pl.ds(32, 32), pl.ds(0, 1536)]
        dst = pe.at[pl.ds(0, 32), pl.ds(0, 1536)] if side == 0 else pe.at[pl.ds(80, 32), pl.ds(0, 1536)]
        row = r + 1 if side == 0 else r - 1
        return remote(src, dst, psem.at[2 + side], qsem.at[2 + side], row, c)

    def pan_corner(side):
        src = pe.at[pl.ds(48, 32), pl.ds(1536, 256)] if side == 0 else pe.at[pl.ds(32, 32), pl.ds(1536, 256)]
        dst = pe.at[pl.ds(0, 32), pl.ds(1536, 256)] if side == 0 else pe.at[pl.ds(80, 32), pl.ds(1536, 256)]
        row = r + 1 if side == 0 else r - 1
        return remote(src, dst, psem.at[4 + side], qsem.at[4 + side], row, c)

    has_below, has_above = r < STRIPS - 1, r > 0
    has_right, has_left = c < BLOCKS - 1, c > 0

    def when(cond, action):
        @pl.when(cond)
        def _():
            action()

    when(has_right, lambda: pan_cols(0).start())
    when(has_left, lambda: pan_cols(1).start())

    def band_rows(b):
        return pl.ds(pl.multiple_of(b * 8, 8), 8)

    def block_send(k):
        block = lax.rem(c + k, 8)
        return remote(sb.at[block], e.at[1, pl.ds(0, 6), band_rows(c)], ssem.at[k], rsem.at[k], r, block)

    def block_recv(k):
        b = lax.rem(c + 8 - k, 8)
        return remote(sb.at[0], e.at[1, pl.ds(0, 6), band_rows(b)], ssem.at[k], rsem.at[k], r, c)

    def forward(k, side):
        b = lax.rem(c + 8 - k, 8)
        dst = e.at[2 * side, pl.ds(0, 6), band_rows(b)]
        src = sb.at[c] if k == 0 else e.at[1, pl.ds(0, 6), band_rows(b)]
        row = r + 1 if side == 0 else r - 1
        return remote(src, dst, fsem.at[side, k], hsem.at[side, k], row, c)

    order = (4, 3, 5, 2, 6, 1, 7)
    for k in order:
        block_send(k).start()
    own = pltpu.make_async_copy(sb.at[c], e.at[1, pl.ds(0, 6), band_rows(c)], lsem.at[3])
    own.start()
    when(has_below, lambda: forward(0, 0).start())
    when(has_above, lambda: forward(0, 1).start())
    when(has_below, lambda: pan_rows(0).start())
    when(has_above, lambda: pan_rows(1).start())

    when(has_left, lambda: pan_cols(0).wait_recv())
    when(has_right, lambda: pan_cols(1).wait_recv())
    when(has_below, lambda: pan_corner(0).start())
    when(has_above, lambda: pan_corner(1).start())
    for k in (1, 7, 2, 6, 3, 5, 4):
        block_recv(k).wait_recv()
        when(has_below, functools.partial(lambda k: forward(k, 0).start(), k))
        when(has_above, functools.partial(lambda k: forward(k, 1).start(), k))
    own.wait()
    for copy in const_loads:
        copy.wait()
    when(has_above, lambda: (pan_rows(0).wait_recv(), pan_corner(0).wait_recv()))
    when(has_below, lambda: (pan_rows(1).wait_recv(), pan_corner(1).wait_recv()))
    for k in range(8):
        when(has_above, functools.partial(lambda k: forward(k, 0).wait_recv(), k))
        when(has_below, functools.partial(lambda k: forward(k, 1).wait_recv(), k))

    front_compute(e, pe, consts, r, c, d_out, ts, dd, xs, ys, lvs, vl, swu, dl, rl)

    def sum_one(k):
        row, block = first[k - 1]
        return remote(rl, g1.at[rl8], g1s.at[k], g1r.at[k], row, block)

    def sum_one_recv(k):
        return remote(rl, g1.at[lax.rem(rl8 + 8 - k, 8)], g1s.at[k], g1r.at[k], r, c)

    def sum_two(k):
        row, block = second[k - 1]
        return remote(mid, g2.at[q_slot], g2s.at[k], g2r.at[k], row, block)

    def sum_two_recv(k):
        return remote(mid, g2.at[lax.rem(q_slot + 16 - k, 16)], g2s.at[k], g2r.at[k], r, c)

    q_slot = q
    for k in range(1, 8):
        sum_one(k).start()
    g1[rl8] = rl[...]
    for k in range(1, 8):
        sum_one_recv(k).wait_recv()
    total = g1[0]
    for k in range(1, 8):
        total = total + g1[k]
    mid[...] = total
    for k in range(1, 16):
        sum_two(k).start()
    g2[q_slot] = total
    upsample(xs, consts, zs, up_out)
    for k in range(1, 16):
        sum_two_recv(k).wait_recv()
    total = g2[0]
    for k in range(1, 16):
        total = total + g2[k]
    rt[...] = total

    for k in range(1, 8):
        block_send(k).wait_send()
        sum_one(k).wait_send()
    for k in range(1, 16):
        sum_two(k).wait_send()
    when(has_right, lambda: pan_cols(0).wait_send())
    when(has_left, lambda: pan_cols(1).wait_send())
    for side, cond in ((0, has_below), (1, has_above)):
        when(cond, functools.partial(lambda side: (pan_rows(side).wait_send(), pan_corner(side).wait_send()), side))
        for k in range(8):
            when(cond, functools.partial(lambda k, side: forward(k, side).wait_send(), k, side))


def front(pan, vnir, swir):
    return pl.pallas_call(
        front_kernel,
        name="front",
        out_shape=[
            jax.ShapeDtypeStruct((8, 128), F32),
            jax.ShapeDtypeStruct((384, 1536), F32),
            jax.ShapeDtypeStruct((48, 1536), F32),
            jax.ShapeDtypeStruct((12, 8, 384), F32),
            jax.ShapeDtypeStruct((96, 384), F32),
            jax.ShapeDtypeStruct((12, 384), F32),
        ],
        in_specs=[pl.BlockSpec(memory_space=pl.ANY)] * (3 + NUM_CONST),
        out_specs=[pl.BlockSpec(memory_space=VM)] * 6,
        scratch_shapes=[VM(k.shape, BF16 if k.dtype == ml_dtypes.bfloat16 else F32) for k in CONSTANTS]
        + [
            VM((12, 3072), F32),
            VM((4, 1024), F32),
            VM((8, 6, 8, 128), F32),
            VM((3, 6, 64, 128), F32),
            VM((112, 1792), F32),
            VM((28, 8, 512), F32),
            VM((16, 8, 512), F32),
            VM((16, 512), F32),
            VM((24, 512), F32),
            VM((12, 8, 384), F32),
            VM((4, 384, 128), F32),
            VM((8, 128), F32),
            VM((8, 8, 128), F32),
            VM((8, 128), F32),
            VM((16, 8, 128), F32),
            pltpu.SemaphoreType.DMA((NUM_CONST,)),
            pltpu.SemaphoreType.DMA((4,)),
            pltpu.SemaphoreType.DMA((8,)),
            pltpu.SemaphoreType.DMA((8,)),
            pltpu.SemaphoreType.DMA((2, 8)),
            pltpu.SemaphoreType.DMA((2, 8)),
            pltpu.SemaphoreType.DMA((6,)),
            pltpu.SemaphoreType.DMA((6,)),
            pltpu.SemaphoreType.DMA((8,)),
            pltpu.SemaphoreType.DMA((8,)),
            pltpu.SemaphoreType.DMA((16,)),
            pltpu.SemaphoreType.DMA((16,)),
        ],
        compiler_params=pltpu.CompilerParams(
            collective_id=0, has_side_effects=True, vmem_limit_bytes=56 << 20
        ),
    )(pan, vnir, swir, *[jnp.asarray(k) for k in CONSTANTS])


def solve_spd(a, b):
    a = [list(row) for row in a]
    inverse = []
    factor = [[None] * 8 for _ in range(8)]
    for j in range(8):
        inv = 1.0 / a[j][j]
        inverse.append(inv)
        for i in range(j + 1, 8):
            factor[i][j] = a[i][j] * inv
        for i in range(j + 1, 8):
            for k in range(j + 1, i + 1):
                a[i][k] = a[i][k] - factor[i][j] * a[k][j]
    z = list(b)
    for j in range(8):
        for i in range(j + 1, 8):
            z[i] = z[i] - factor[i][j] * z[j]
    z = [z[j] * inverse[j] for j in range(8)]
    for j in range(7, -1, -1):
        for i in range(j):
            z[i] = z[i] - factor[j][i] * z[j]
    return z


def total_of(values):
    total = values[0]
    for value in values[1:]:
        total = total + value
    return total


def solve(rt, cb):
    for k in range(38):
        if k < 11 or k >= 16:
            cb[k] = jnp.broadcast_to(rt[:, k : k + 1], (8, 128))

    def at(k, i):
        return cb[k, i : i + 1, :]

    mean = [at(9, i) * (1.0 / N1) for i in range(8)]
    mean_p = jnp.sum(cb[10], axis=0, keepdims=True) * (1.0 / N1)
    a = [[at(j, i) * (1.0 / N1) - mean[i] * mean[j] for j in range(i + 1)] for i in range(8)]
    b = [at(8, i) * (1.0 / N1) - mean[i] * mean_p for i in range(8)]
    w = solve_spd(a, b)
    scale = 1.0 / total_of([b[i] * w[i] for i in range(8)])
    gain = [b[i] * scale for i in range(8)]
    sum_d = at(36, 0)
    sum_dd = at(37, 0)
    q = [at(32, i) for i in range(8)]
    mean2 = [(at(34, i) + gain[i] * sum_d) * (1.0 / N2) for i in range(8)]
    a2 = [
        [
            (at(16 + j, i) + gain[i] * q[j] + gain[j] * q[i] + gain[i] * gain[j] * sum_dd) * (1.0 / N2)
            - mean2[i] * mean2[j]
            for j in range(i + 1)
        ]
        for i in range(8)
    ]
    swir_mean = cb[35] * (1.0 / N2)
    cross = [
        (cb[24 + i] + gain[i] * cb[33]) * (1.0 / N2) - mean2[i] * swir_mean for i in range(8)
    ]
    y = [jnp.sum(cross[i], axis=0, keepdims=True) * 0.125 for i in range(8)]
    v = solve_spd(a2, y)
    share = total_of([v[i] * cross[i] for i in range(8)]) / total_of([v[i] * y[i] for i in range(8)])
    return gain, v, share


def wide(x, copies):
    return jnp.concatenate([x] * copies, axis=1)


def back_kernel(rt, up, d, vl, swu, dl, joined, joined_swir, cb, gs, out, swir_out, sem):
    gain, v, share = solve(rt, cb)
    for b in range(8):
        gs[b] = jnp.broadcast_to(gain[b], (8, 128))

    @pl.loop(0, BANDS)
    def _(b):
        g = wide(gs[b], 2)
        rows = pl.multiple_of(b * 48, 48)
        for i in range(6):
            for t in range(6):
                at = slice(256 * t, 256 * t + 256)
                out[b, 8 * i : 8 * i + 8, at] = (
                    up[pl.ds(rows + 8 * i, 8), at] + g * d[8 * i : 8 * i + 8, at]
                )
        pltpu.make_async_copy(out.at[b], joined.at[b], sem.at[b]).start()

    row8 = lax.broadcasted_iota(jnp.int32, (8, 128), 0)
    v8 = jnp.zeros((8, 128), F32)
    for b in range(8):
        v8 = jnp.where(row8 == b, jnp.broadcast_to(v[b], (8, 128)), v8)
    v8 = wide(v8, 3)
    vg = wide(total_of([v[b] * gain[b] for b in range(8)]), 3)
    share3 = wide(share, 3)
    for i in range(12):
        detail = jnp.sum(v8 * vl[i], axis=0, keepdims=True) + vg * dl[i : i + 1, :]
        row = swu[8 * i : 8 * i + 8, :] + share3 * detail
        for t in range(3):
            swir_out[t, pl.ds(i, 8, stride=16), :] = row[:, 128 * t : 128 * t + 128]
    for s in range(8):
        for t in range(3):
            joined_swir[s, :, 128 * t : 128 * t + 128] = swir_out[t, 16 * s : 16 * s + 12, :]

    @pl.loop(0, BANDS)
    def _(b):
        pltpu.make_async_copy(out.at[b], joined.at[b], sem.at[b]).wait()


def back(rt, up, d, vl, swu, dl):
    return pl.pallas_call(
        back_kernel,
        name="back",
        out_shape=[
            jax.ShapeDtypeStruct((8, 48, 1536), F32),
            jax.ShapeDtypeStruct((8, 12, 384), F32),
        ],
        in_specs=[pl.BlockSpec(memory_space=VM)] * 6,
        out_specs=[pl.BlockSpec(memory_space=pl.ANY), pl.BlockSpec(memory_space=VM)],
        scratch_shapes=[
            VM((38, 8, 128), F32),
            VM((8, 8, 128), F32),
            VM((8, 48, 1536), F32),
            VM((3, 128, 128), F32),
            pltpu.SemaphoreType.DMA((8,)),
        ],
        compiler_params=pltpu.CompilerParams(vmem_limit_bytes=32 << 20),
    )(rt, up, d, vl, swu, dl)


def local(pan, vnir, swir):
    return tuple(back(*front(pan, vnir, swir)))


def solution(mesh):
    return jax.shard_map(
        local,
        mesh=mesh,
        in_specs=(P("rows", "band"), P("band", "rows", None), P("band", "rows", None)),
        out_specs=(P(None, "rows", "band"), P(None, "rows", "band")),
        check_vma=False,
    )
```

```python
import functools
import math

import jax
import jax.numpy as jnp
import ml_dtypes
import numpy as np
from jax import lax
from jax.experimental import pallas as pl
from jax.experimental.pallas import tpu as pltpu
from jax.sharding import PartitionSpec as P

F32 = jnp.float32
BF16 = jnp.bfloat16
MESH = pl.DeviceIdType.MESH
VM = pltpu.VMEM

BANDS = 8
STRIPS = 16
BLOCKS = 8
HEIGHT = 768
WIDTH = 12288
N1 = float(HEIGHT * WIDTH)
N2 = float(HEIGHT * WIDTH // 16)
NYQUIST_GAIN = 0.29


def gauss_taps(upscale, kernel_len):
    spread = upscale * math.sqrt(-2.0 * math.log(NYQUIST_GAIN)) / math.pi
    radius = kernel_len // 2
    offsets = np.arange(-radius, radius + 1) * 1.0
    values = np.exp(-(offsets**2) / (2.0 * spread**2))
    return values / values.sum()


def cubic_weight(distance):
    distance = abs(distance)
    if distance <= 1.0:
        return 1.5 * distance**3 - 2.5 * distance**2 + 1.0
    if distance < 2.0:
        return -0.5 * distance**3 + 2.5 * distance**2 - 4.0 * distance + 2.0
    return 0.0


def cubic_table(upscale):
    weights = np.zeros((5, upscale))
    for phase_index in range(upscale):
        centre = (phase_index + 0.5) / upscale - 0.5
        first_tap = math.floor(centre)
        fraction = centre - first_tap
        for tap_index in range(-1, 3):
            weights[first_tap + tap_index + 2, phase_index] += cubic_weight(tap_index - fraction)
    return weights


C4 = cubic_table(4)
C3 = cubic_table(3)
G4 = gauss_taps(4, 17)
G3 = gauss_taps(3, 13)
MEAN_TAPS = C4.mean(axis=1)


def split(matrix):
    high = matrix.astype(np.float32).astype(ml_dtypes.bfloat16)
    low = (matrix - high.astype(np.float64)).astype(ml_dtypes.bfloat16)
    return high, low


def tables():
    up_rows = np.zeros((48, 16))
    for m in range(12):
        for p in range(4):
            for t in range(5):
                up_rows[4 * m + p, m + t] += C4[t, p]
    up_cols = np.zeros((1536, 512))
    for m in range(384):
        for p in range(4):
            for t in range(5):
                up_cols[4 * m + p, (m + t - 2) % 512] += C4[t, p]
    gram_rows = up_rows.T @ up_rows
    gram_cols = up_cols.T @ up_cols
    lanes = np.zeros((16, 512), np.float32)
    at = np.arange(512)
    for t in range(-4, 5):
        lanes[t + 4] = gram_cols[at, (at + t) % 512]
    lanes[9] = up_cols.sum(axis=0)
    row_sum = up_rows.sum(axis=0)

    low = np.zeros((96, 112))
    for f in range(96):
        for t in range(17):
            low[f, f + t] = G4[t]
    mean = np.zeros((24, 112))
    mean_low = np.zeros((24, 112))
    for i in range(24):
        mean[i, 8 + 4 * i : 12 + 4 * i] = 0.25
        mean_low[i] = low[4 * i : 4 * i + 4].mean(axis=0)
    g3_rows = np.zeros((12, 24))
    for i in range(12):
        g3_rows[i, i : i + 13] = G3
    row_stack = []
    for variant in range(3):
        keep = np.ones((24, 1))
        if variant == 0:
            keep[:6] = 0.0
        if variant == 2:
            keep[18:] = 0.0
        row_stack.append(
            np.concatenate(
                [
                    low[24:72],
                    up_rows.T @ low[24:72],
                    mean_low[6:18],
                    g3_rows @ (keep * mean_low),
                    mean[6:18],
                    g3_rows @ (keep * mean),
                ]
            )
        )
    rows_hi, rows_lo = split(np.stack(row_stack))

    low_cols = np.zeros((256, 128))
    for o in range(128):
        for t in range(-8, 9):
            q = o + t
            row = q if 0 <= q < 128 else (q if q >= 128 else 256 + q)
            low_cols[row, o] = G4[t + 8]
    mean_cols = np.zeros((640, 128))
    for f in range(512):
        mean_cols[f, f // 4] = 0.25
    for f in range(32):
        mean_cols[512 + f, f // 4] = 0.25
        mean_cols[512 + 96 + f, 120 + f // 4] = 0.25
    back_cols = np.zeros((640, 128))
    for n in range(128):
        for t in range(5):
            for p in range(4):
                f = 4 * (n - (t - 2)) + p
                row = f if f >= 0 else 640 + f
                back_cols[row, n] += C4[t, p]
    fine = np.zeros((256, 512))
    for m in range(128):
        for p in range(4):
            for t in range(5):
                fine[(m + t - 2) % 256, 4 * m + p] += C4[t, p]
    third = np.zeros((256, 384))
    for m in range(128):
        for p in range(3):
            for t in range(5):
                third[(m + t - 2) % 256, 3 * m + p] += C3[t, p]
    constants = (
        rows_hi,
        rows_lo,
        *split(low_cols),
        mean_cols.astype(ml_dtypes.bfloat16),
        *split(back_cols),
        *split(fine),
        *split(third),
        lanes,
    )
    return constants, gram_rows, row_sum, up_rows


CONSTANTS, GRAM_ROWS, ROW_SUM, UP_ROWS = tables()
NUM_CONST = len(CONSTANTS)


def halves(x):
    high = x.astype(BF16)
    return high, (x - high.astype(F32)).astype(BF16)


def mm(a, b):
    return jnp.dot(a, b, preferred_element_type=F32)


def dot3(x, high, low):
    xh, xl = halves(x)
    return mm(xh, high) + mm(xl, high) + mm(xh, low)


def dot2(x, exact):
    xh, xl = halves(x)
    return mm(xh, exact) + mm(xl, exact)


def lane(shape):
    return lax.broadcasted_iota(jnp.int32, shape, len(shape) - 1)


def edge(next_tile, prev_tile):
    return jnp.where(lane(next_tile.shape) < 64, next_tile, prev_tile)


def shifted(x, t):
    n = x.shape[1]
    return x if t == 0 else pltpu.roll(x, (-t) % n, 1)


def col_filter(x, taps):
    radius = len(taps) // 2
    total = float(taps[radius]) * x
    for t in range(-radius, radius + 1):
        if t:
            total = total + float(taps[t + radius]) * shifted(x, t)
    return total


def pick(e, strip, row, tile):
    return e[strip, tile, pl.ds(row, 8, stride=8), :]


def vnir_row(e, strip, i):
    if i < 8:
        parts = [pick(e, strip, i, t) for t in range(3)] + [pick(e, strip, i, 5)]
    else:
        j = i - 8
        parts = [
            pick(e, strip, j, 3),
            pick(e, strip, 4 + j, 3),
            pick(e, strip, j, 4),
            pltpu.roll(pick(e, strip, j, 5), 64, 1),
        ]
    return jnp.concatenate(parts, axis=1)


def swir_row(e, strip, j):
    return jnp.concatenate(
        [pick(e, strip, 4 + j, 4), pltpu.roll(pick(e, strip, 4 + j, 5), 64, 1)], axis=1
    )


def fold(x):
    total = x[:, 0:128]
    for t in range(1, x.shape[1] // 128):
        total = total + x[:, 128 * t : 128 * t + 128]
    return total


def pack(vs, ss, sb):
    at = lane((8, 128))
    zero = jnp.zeros((8, 128), F32)

    def coarse(first, tile):
        return vs[pl.ds(24 * first + tile, 8, stride=24), :] if 0 <= tile < 24 else zero

    def short(tile):
        return ss[0:4, 128 * tile : 128 * tile + 128] if 0 <= tile < 8 else zero[0:4]

    for d in range(BLOCKS):
        for t in range(3):
            sb[d, t] = coarse(0, 3 * d + t)
        sb[d, 3, 0:4] = coarse(8, 3 * d)[0:4]
        sb[d, 3, 4:8] = coarse(8, 3 * d + 1)[0:4]
        sb[d, 4, 0:4] = coarse(8, 3 * d + 2)[0:4]
        sb[d, 4, 4:8] = short(d)
        sb[d, 5, 0:4] = edge(coarse(8, 3 * d + 3), coarse(8, 3 * d - 1))[0:4]
        sb[d, 5, 4:8] = edge(short(d + 1), short(d - 1))
        other = pltpu.roll(sb[d, 5], 64, 1)
        own = edge(coarse(0, 3 * d + 3), coarse(0, 3 * d - 1))
        sb[d, 5] = jnp.where((at >= 32) & (at < 96), other, own)


def pan_stage(pan_ext, consts, variant, d_out, ts, dd):
    rows_hi, rows_lo, low_hi, low_lo, mean_c, back_hi, back_lo = consts[:7]
    halo = edge(pan_ext[:, 1664:1792], pan_ext[:, 1536:1664])
    full = jnp.concatenate([pan_ext[:, 0:1536], halo], axis=1)
    fh, fl = halves(full)
    rh, rl = rows_hi[variant], rows_lo[variant]
    q = mm(rh, fh) + mm(rh, fl) + mm(rl, fh)
    top = q[0:88]
    tiles = [top[:, 128 * j : 128 * j + 128] for j in range(13)]
    lhs = jnp.concatenate(
        [
            jnp.concatenate([tiles[j], edge(tiles[(j + 1) % 13], tiles[(j + 12) % 13])], axis=1)
            for j in range(13)
        ],
        axis=0,
    )
    low = dot3(lhs, low_hi[...], low_lo[...])
    low_tile = [low[88 * j : 88 * j + 88] for j in range(13)]
    total = jnp.zeros((8, 128), F32)
    for j in range(12):
        d_out[:, 128 * j : 128 * j + 128] = (
            pan_ext[32:80, 128 * j : 128 * j + 128] - low_tile[j][0:48]
        )
        for k in range(6):
            total = total + low_tile[j][8 * k : 8 * k + 8]
    zero = jnp.zeros((16, 128), F32)
    back = [low_tile[j][48:64] for j in range(12)] + [zero]
    lhs = jnp.concatenate(
        [
            jnp.concatenate(
                back[4 * t : 4 * t + 4] + [edge(back[4 * t + 4], back[(4 * t + 12) % 13])], axis=1
            )
            for t in range(3)
        ],
        axis=0,
    )
    main = dot3(lhs, back_hi[...], back_lo[...])
    rim = dot3(edge(back[0], back[11]), back_hi[512:640], back_lo[512:640])
    for t in range(3):
        ts[:, 128 * t : 128 * t + 128] = main[16 * t : 16 * t + 16]
    ts[:, 384:512] = rim
    diff = [q[88:112, 128 * j : 128 * j + 128] - low_tile[j][64:88] for j in range(13)]
    lhs = jnp.concatenate(
        [jnp.concatenate(diff[4 * t : 4 * t + 4], axis=1) for t in range(3)], axis=0
    )
    main = dot2(lhs, mean_c[0:512])
    for t in range(3):
        dd[0:24, 128 * t : 128 * t + 128] = main[24 * t : 24 * t + 24]
    dd[0:24, 384:512] = dot2(diff[12], mean_c[512:640])
    return total


def column_mask(block):
    at = lane((1, 512))
    left = jnp.where(block == 0, 0.0, 1.0)
    right = jnp.where(block == BLOCKS - 1, 0.0, 1.0)
    return jnp.where(at >= 448, left, jnp.where(at >= 384, right, 1.0))


def front_compute(e, pan_ext, consts, r, c, d_out, ts, dd, xs, ys, lvs, vl, swu, dl, rl):
    third_hi, third_lo, lanes = consts[9:12]
    variant = jnp.where(r == 0, 0, jnp.where(r == STRIPS - 1, 2, 1))
    sums = {}
    sums[10] = pan_stage(pan_ext, consts, variant, d_out, ts, dd)
    for k in range(28):
        strip, i = (0, k + 4) if k < 8 else ((1, k - 8) if k < 20 else (2, k - 20))
        xs[k] = vnir_row(e, strip, i)
    for i in range(16):
        total = None
        for j in range(16):
            if GRAM_ROWS[i, j] != 0.0:
                term = float(GRAM_ROWS[i, j]) * xs[j + 6]
                total = term if total is None else total + term
        y = lanes[4:5, :] * total
        for t in range(-4, 5):
            if t:
                y = y + lanes[t + 4 : t + 5, :] * shifted(total, t)
        ys[i] = y
    acc = [jnp.zeros((8, 128), F32) for _ in range(10)]
    ones = lanes[9:10, :]
    for i in range(16):
        x = xs[i + 6]
        for j in range(8):
            acc[j] = acc[j] + fold(x * ys[i, j : j + 1, :])
        acc[8] = acc[8] + fold(x * ts[i : i + 1, :])
        acc[9] = acc[9] + float(ROW_SUM[i]) * fold(x * ones)
    for k in range(10):
        sums[k] = acc[k]
    up_keep = jnp.where(r == 0, 0.0, 1.0)
    down_keep = jnp.where(r == STRIPS - 1, 0.0, 1.0)
    mask = column_mask(c)
    mean_rows = []
    for i in range(24):
        total = None
        for t in range(5):
            term = float(MEAN_TAPS[t]) * xs[i + t]
            total = term if total is None else total + term
        if i < 6:
            total = total * up_keep
        if i >= 18:
            total = total * down_keep
        mean_rows.append(total)
    for i in range(12):
        total = float(G3[6]) * mean_rows[i + 6]
        for t in range(6):
            total = total + float(G3[t]) * (mean_rows[i + t] + mean_rows[i + 12 - t])
        lowered = col_filter(total, MEAN_TAPS) * mask
        lowered = col_filter(lowered, G3)[:, 0:384]
        lvs[i] = lowered
        vl[i] = col_filter(mean_rows[i + 6], MEAN_TAPS)[:, 0:384] - lowered
    dcol = dd[8:24, :] * mask
    dcol = col_filter(dcol, G3)[:, 0:384]
    low_d = dcol[4:16]
    dl[...] = dd[0:12, 0:384] - low_d
    ts[0:12, 0:384] = low_d
    srow = [
        swir_row(e, *at)
        for at in ((0, 2), (0, 3), (1, 0), (1, 1), (1, 2), (1, 3), (2, 0), (2, 1))
    ]
    up = []
    for m in range(4):
        for p in range(3):
            total = None
            for t in range(5):
                if C3[t, p] != 0.0:
                    term = float(C3[t, p]) * srow[m + t]
                    total = term if total is None else total + term
            up.append(total)
    swu[...] = dot3(jnp.concatenate(up, axis=0), third_hi[...], third_lo[...])
    acc = [jnp.zeros((8, 128), F32) for _ in range(22)]
    for i in range(12):
        lv = lvs[i]
        sw = swu[8 * i : 8 * i + 8, :]
        ld = ts[i : i + 1, 0:384]
        for j in range(8):
            other = lvs[i, j : j + 1, :]
            acc[j] = acc[j] + fold(lv * other)
            acc[8 + j] = acc[8 + j] + fold(sw * other)
        acc[16] = acc[16] + fold(lv * ld)
        acc[17] = acc[17] + fold(sw * ld)
        acc[18] = acc[18] + fold(lv)
        acc[19] = acc[19] + fold(sw)
        acc[20] = acc[20] + fold(ld)
        acc[21] = acc[21] + fold(ld * ld)
    for k in range(22):
        sums[16 + k] = acc[k]
    at = lane((8, 128))
    packed = jnp.zeros((8, 128), F32)
    for k, value in sums.items():
        packed = jnp.where(at == k, jnp.sum(value, axis=1, keepdims=True), packed)
    rl[...] = packed


def upsample(xs, consts, zs, up_out):
    fine_hi, fine_lo = consts[7:9]
    for m in range(12):
        for p in range(4):
            total = None
            for t in range(5):
                if C4[t, p] != 0.0:
                    term = float(C4[t, p]) * xs[m + t + 6]
                    total = term if total is None else total + term
            for tile in range(4):
                zs[tile, pl.ds(4 * m + p, 8, stride=48), :] = total[
                    :, 128 * tile : 128 * tile + 128
                ]

    @pl.loop(0, BANDS)
    def _(b):
        at = pl.ds(pl.multiple_of(b * 48, 48), 48)
        z = [zs[k, at, :] for k in range(4)]
        lhs = jnp.concatenate(
            [
                jnp.concatenate([z[k], edge(z[k + 1], z[(k + 3) % 4])], axis=1)
                for k in range(3)
            ],
            axis=0,
        )
        up = dot3(lhs, fine_hi[...], fine_lo[...])
        for k in range(3):
            up_out[at, 512 * k : 512 * k + 512] = up[48 * k : 48 * k + 48]


def front_kernel(pan, vnir, swir, *rest):
    hbm_consts = rest[:NUM_CONST]
    rt, up_out, d_out, vl, swu, dl = rest[NUM_CONST : NUM_CONST + 6]
    rest = rest[NUM_CONST + 6 :]
    consts = rest[:NUM_CONST]
    (vs, ss, sb, e, pe, xs, ys, ts, dd, lvs, zs, rl, g1, mid, g2) = rest[NUM_CONST : NUM_CONST + 15]
    (csem, lsem, ssem, rsem, fsem, hsem, psem, qsem, g1s, g1r, g2s, g2r) = rest[NUM_CONST + 15 :]
    r = lax.axis_index("rows")
    c = lax.axis_index("band")

    def remote(src, dst, send, recv, row, block):
        return pltpu.make_async_remote_copy(
            src_ref=src, dst_ref=dst, send_sem=send, recv_sem=recv,
            device_id=(row, block), device_id_type=MESH,
        )

    rl8 = lax.rem(r, 8)
    base = r - rl8
    q = base + c
    barrier = pltpu.get_barrier_semaphore()

    def greet(row, block):
        pl.semaphore_signal(barrier, inc=1, device_id=(row, block), device_id_type=MESH)

    first = [(base + lax.rem(rl8 + k, 8), c) for k in range(1, 8)]
    second = []
    for k in range(1, 16):
        q2 = lax.rem(q + k, 16)
        c2 = lax.rem(q2, 8)
        second.append((q2 - c2 + rl8, c2))
    around = [(lax.rem(r + 1, STRIPS), c), (lax.rem(r + STRIPS - 1, STRIPS), c)]
    partners = first + second + around
    for row, block in partners:
        greet(row, block)

    loads = [
        pltpu.make_async_copy(vnir, vs.at[pl.ds(0, 288)], lsem.at[0]),
        pltpu.make_async_copy(swir.at[0], ss, lsem.at[1]),
        pltpu.make_async_copy(pan, pe.at[pl.ds(32, 48), pl.ds(0, 1536)], lsem.at[2]),
    ]
    for copy in loads:
        copy.start()
    const_loads = [
        pltpu.make_async_copy(hbm_consts[k], consts[k], csem.at[k]) for k in range(NUM_CONST)
    ]
    for copy in const_loads:
        copy.start()

    @pl.when(r == 0)
    def _():
        pe[0:32, :] = jnp.zeros((32, 1792), F32)
        e[0] = jnp.zeros((6, 64, 128), F32)

    @pl.when(r == STRIPS - 1)
    def _():
        pe[80:112, :] = jnp.zeros((32, 1792), F32)
        e[2] = jnp.zeros((6, 64, 128), F32)

    @pl.when(c == 0)
    def _():
        pe[32:80, 1536:1664] = jnp.zeros((48, 128), F32)

    @pl.when(c == BLOCKS - 1)
    def _():
        pe[32:80, 1664:1792] = jnp.zeros((48, 128), F32)

    loads[0].wait()
    loads[1].wait()
    pack(vs, ss, sb)
    loads[2].wait()
    pl.semaphore_wait(barrier, len(partners))

    def pan_cols(side):
        src = pe.at[pl.ds(32, 48), pl.ds(1408, 128)] if side == 0 else pan_first
        dst = pe.at[pl.ds(32, 48), pl.ds(1536 + 128 * side, 128)]
        block = c + 1 if side == 0 else c - 1
        return remote(src, dst, psem.at[side], qsem.at[side], r, block)

    pan_first = pe.at[pl.ds(32, 48), pl.ds(0, 128)]

    def pan_rows(side):
        src = pe.at[pl.ds(48, 32), pl.ds(0, 1536)] if side == 0 else pe.at[pl.ds(32, 32), pl.ds(0, 1536)]
        dst = pe.at[pl.ds(0, 32), pl.ds(0, 1536)] if side == 0 else pe.at[pl.ds(80, 32), pl.ds(0, 1536)]
        row = r + 1 if side == 0 else r - 1
        return remote(src, dst, psem.at[2 + side], qsem.at[2 + side], row, c)

    def pan_corner(side):
        src = pe.at[pl.ds(48, 32), pl.ds(1536, 256)] if side == 0 else pe.at[pl.ds(32, 32), pl.ds(1536, 256)]
        dst = pe.at[pl.ds(0, 32), pl.ds(1536, 256)] if side == 0 else pe.at[pl.ds(80, 32), pl.ds(1536, 256)]
        row = r + 1 if side == 0 else r - 1
        return remote(src, dst, psem.at[4 + side], qsem.at[4 + side], row, c)

    has_below, has_above = r < STRIPS - 1, r > 0
    has_right, has_left = c < BLOCKS - 1, c > 0

    def when(cond, action):
        @pl.when(cond)
        def _():
            action()

    when(has_right, lambda: pan_cols(0).start())
    when(has_left, lambda: pan_cols(1).start())

    def band_rows(b):
        return pl.ds(pl.multiple_of(b * 8, 8), 8)

    def block_send(k):
        block = lax.rem(c + k, 8)
        return remote(sb.at[block], e.at[1, pl.ds(0, 6), band_rows(c)], ssem.at[k], rsem.at[k], r, block)

    def block_recv(k):
        b = lax.rem(c + 8 - k, 8)
        return remote(sb.at[0], e.at[1, pl.ds(0, 6), band_rows(b)], ssem.at[k], rsem.at[k], r, c)

    def forward(k, side):
        b = lax.rem(c + 8 - k, 8)
        dst = e.at[2 * side, pl.ds(0, 6), band_rows(b)]
        src = sb.at[c] if k == 0 else e.at[1, pl.ds(0, 6), band_rows(b)]
        row = r + 1 if side == 0 else r - 1
        return remote(src, dst, fsem.at[side, k], hsem.at[side, k], row, c)

    order = (4, 3, 5, 2, 6, 1, 7)
    for k in order:
        block_send(k).start()
    own = pltpu.make_async_copy(sb.at[c], e.at[1, pl.ds(0, 6), band_rows(c)], lsem.at[3])
    own.start()
    when(has_below, lambda: forward(0, 0).start())
    when(has_above, lambda: forward(0, 1).start())
    when(has_below, lambda: pan_rows(0).start())
    when(has_above, lambda: pan_rows(1).start())

    when(has_left, lambda: pan_cols(0).wait_recv())
    when(has_right, lambda: pan_cols(1).wait_recv())
    when(has_below, lambda: pan_corner(0).start())
    when(has_above, lambda: pan_corner(1).start())
    for k in (1, 7, 2, 6, 3, 5, 4):
        block_recv(k).wait_recv()
        when(has_below, functools.partial(lambda k: forward(k, 0).start(), k))
        when(has_above, functools.partial(lambda k: forward(k, 1).start(), k))
    own.wait()
    for copy in const_loads:
        copy.wait()
    when(has_above, lambda: (pan_rows(0).wait_recv(), pan_corner(0).wait_recv()))
    when(has_below, lambda: (pan_rows(1).wait_recv(), pan_corner(1).wait_recv()))
    for k in range(8):
        when(has_above, functools.partial(lambda k: forward(k, 0).wait_recv(), k))
        when(has_below, functools.partial(lambda k: forward(k, 1).wait_recv(), k))

    front_compute(e, pe, consts, r, c, d_out, ts, dd, xs, ys, lvs, vl, swu, dl, rl)

    def sum_one(k):
        row, block = first[k - 1]
        return remote(rl, g1.at[rl8], g1s.at[k], g1r.at[k], row, block)

    def sum_one_recv(k):
        return remote(rl, g1.at[lax.rem(rl8 + 8 - k, 8)], g1s.at[k], g1r.at[k], r, c)

    def sum_two(k):
        row, block = second[k - 1]
        return remote(mid, g2.at[q_slot], g2s.at[k], g2r.at[k], row, block)

    def sum_two_recv(k):
        return remote(mid, g2.at[lax.rem(q_slot + 16 - k, 16)], g2s.at[k], g2r.at[k], r, c)

    q_slot = q
    for k in range(1, 8):
        sum_one(k).start()
    g1[rl8] = rl[...]
    for k in range(1, 8):
        sum_one_recv(k).wait_recv()
    total = g1[0]
    for k in range(1, 8):
        total = total + g1[k]
    mid[...] = total
    for k in range(1, 16):
        sum_two(k).start()
    g2[q_slot] = total
    upsample(xs, consts, zs, up_out)
    for k in range(1, 16):
        sum_two_recv(k).wait_recv()
    total = g2[0]
    for k in range(1, 16):
        total = total + g2[k]
    rt[...] = total

    for k in range(1, 8):
        block_send(k).wait_send()
        sum_one(k).wait_send()
    for k in range(1, 16):
        sum_two(k).wait_send()
    when(has_right, lambda: pan_cols(0).wait_send())
    when(has_left, lambda: pan_cols(1).wait_send())
    for side, cond in ((0, has_below), (1, has_above)):
        when(cond, functools.partial(lambda side: (pan_rows(side).wait_send(), pan_corner(side).wait_send()), side))
        for k in range(8):
            when(cond, functools.partial(lambda k, side: forward(k, side).wait_send(), k, side))


def front(pan, vnir, swir):
    return pl.pallas_call(
        front_kernel,
        name="front",
        out_shape=[
            VM((8, 128), F32),
            VM((384, 1536), F32),
            VM((48, 1536), F32),
            VM((12, 8, 384), F32),
            VM((96, 384), F32),
            VM((12, 384), F32),
        ],
        in_specs=[pl.BlockSpec(memory_space=pl.ANY)] * (3 + NUM_CONST),
        out_specs=[pl.BlockSpec(memory_space=VM)] * 6,
        scratch_shapes=[VM(k.shape, BF16 if k.dtype == ml_dtypes.bfloat16 else F32) for k in CONSTANTS]
        + [
            VM((384, 128), F32),
            VM((4, 1024), F32),
            VM((8, 6, 8, 128), F32),
            VM((3, 6, 64, 128), F32),
            VM((112, 1792), F32),
            VM((28, 8, 512), F32),
            VM((16, 8, 512), F32),
            VM((16, 512), F32),
            VM((24, 512), F32),
            VM((12, 8, 384), F32),
            VM((4, 384, 128), F32),
            VM((8, 128), F32),
            VM((8, 8, 128), F32),
            VM((8, 128), F32),
            VM((16, 8, 128), F32),
            pltpu.SemaphoreType.DMA((NUM_CONST,)),
            pltpu.SemaphoreType.DMA((4,)),
            pltpu.SemaphoreType.DMA((8,)),
            pltpu.SemaphoreType.DMA((8,)),
            pltpu.SemaphoreType.DMA((2, 8)),
            pltpu.SemaphoreType.DMA((2, 8)),
            pltpu.SemaphoreType.DMA((6,)),
            pltpu.SemaphoreType.DMA((6,)),
            pltpu.SemaphoreType.DMA((8,)),
            pltpu.SemaphoreType.DMA((8,)),
            pltpu.SemaphoreType.DMA((16,)),
            pltpu.SemaphoreType.DMA((16,)),
        ],
        compiler_params=pltpu.CompilerParams(
            collective_id=0, has_side_effects=True, vmem_limit_bytes=56 << 20
        ),
    )(pan, vnir, swir, *[jnp.asarray(k) for k in CONSTANTS])


def solve_spd(a, b):
    a = [list(row) for row in a]
    inverse = []
    factor = [[None] * 8 for _ in range(8)]
    for j in range(8):
        inv = 1.0 / a[j][j]
        inverse.append(inv)
        for i in range(j + 1, 8):
            factor[i][j] = a[i][j] * inv
        for i in range(j + 1, 8):
            for k in range(j + 1, i + 1):
                a[i][k] = a[i][k] - factor[i][j] * a[k][j]
    z = list(b)
    for j in range(8):
        for i in range(j + 1, 8):
            z[i] = z[i] - factor[i][j] * z[j]
    z = [z[j] * inverse[j] for j in range(8)]
    for j in range(7, -1, -1):
        for i in range(j):
            z[i] = z[i] - factor[j][i] * z[j]
    return z


def total_of(values):
    total = values[0]
    for value in values[1:]:
        total = total + value
    return total


def solve(rt, cb):
    for k in range(38):
        if k < 11 or k >= 16:
            cb[k] = jnp.broadcast_to(rt[:, k : k + 1], (8, 128))

    def at(k, i):
        return cb[k, i : i + 1, :]

    mean = [at(9, i) * (1.0 / N1) for i in range(8)]
    mean_p = jnp.sum(cb[10], axis=0, keepdims=True) * (1.0 / N1)
    a = [[at(j, i) * (1.0 / N1) - mean[i] * mean[j] for j in range(i + 1)] for i in range(8)]
    b = [at(8, i) * (1.0 / N1) - mean[i] * mean_p for i in range(8)]
    w = solve_spd(a, b)
    scale = 1.0 / total_of([b[i] * w[i] for i in range(8)])
    gain = [b[i] * scale for i in range(8)]
    sum_d = at(36, 0)
    sum_dd = at(37, 0)
    q = [at(32, i) for i in range(8)]
    mean2 = [(at(34, i) + gain[i] * sum_d) * (1.0 / N2) for i in range(8)]
    a2 = [
        [
            (at(16 + j, i) + gain[i] * q[j] + gain[j] * q[i] + gain[i] * gain[j] * sum_dd) * (1.0 / N2)
            - mean2[i] * mean2[j]
            for j in range(i + 1)
        ]
        for i in range(8)
    ]
    swir_mean = cb[35] * (1.0 / N2)
    cross = [
        (cb[24 + i] + gain[i] * cb[33]) * (1.0 / N2) - mean2[i] * swir_mean for i in range(8)
    ]
    y = [jnp.sum(cross[i], axis=0, keepdims=True) * 0.125 for i in range(8)]
    v = solve_spd(a2, y)
    share = total_of([v[i] * cross[i] for i in range(8)]) / total_of([v[i] * y[i] for i in range(8)])
    return gain, v, share


def wide(x, copies):
    return jnp.concatenate([x] * copies, axis=1)


def back_kernel(rt, up, d, vl, swu, dl, joined, joined_swir, cb, gs, out, sem):
    gain, v, share = solve(rt, cb)
    for b in range(8):
        gs[b] = jnp.broadcast_to(gain[b], (8, 128))

    @pl.loop(0, BANDS)
    def _(b):
        g = wide(gs[b], 2)
        rows = pl.multiple_of(b * 48, 48)
        for i in range(6):
            for t in range(6):
                at = slice(256 * t, 256 * t + 256)
                out[b, 8 * i : 8 * i + 8, at] = (
                    up[pl.ds(rows + 8 * i, 8), at] + g * d[8 * i : 8 * i + 8, at]
                )
        pltpu.make_async_copy(out.at[b], joined.at[b], sem.at[b]).start()

    row8 = lax.broadcasted_iota(jnp.int32, (8, 128), 0)
    v8 = jnp.zeros((8, 128), F32)
    for b in range(8):
        v8 = jnp.where(row8 == b, jnp.broadcast_to(v[b], (8, 128)), v8)
    v8 = wide(v8, 3)
    vg = wide(total_of([v[b] * gain[b] for b in range(8)]), 3)
    share3 = wide(share, 3)
    for i in range(12):
        detail = jnp.sum(v8 * vl[i], axis=0, keepdims=True) + vg * dl[i : i + 1, :]
        joined_swir[i] = swu[8 * i : 8 * i + 8, :] + share3 * detail

    @pl.loop(0, BANDS)
    def _(b):
        pltpu.make_async_copy(out.at[b], joined.at[b], sem.at[b]).wait()


def back(rt, up, d, vl, swu, dl):
    return pl.pallas_call(
        back_kernel,
        name="back",
        out_shape=[
            jax.ShapeDtypeStruct((8, 48, 1536), F32),
            jax.ShapeDtypeStruct((12, 8, 384), F32),
        ],
        in_specs=[pl.BlockSpec(memory_space=VM)] * 6,
        out_specs=[pl.BlockSpec(memory_space=pl.ANY), pl.BlockSpec(memory_space=VM)],
        scratch_shapes=[
            VM((38, 8, 128), F32),
            VM((8, 8, 128), F32),
            VM((8, 48, 1536), F32),
            pltpu.SemaphoreType.DMA((8,)),
        ],
        compiler_params=pltpu.CompilerParams(vmem_limit_bytes=32 << 20),
    )(rt, up, d, vl, swu, dl)


def local(pan, vnir, swir):
    joined, rows = back(*front(pan, vnir.reshape(288, 128), swir))
    return joined, jnp.swapaxes(rows, 0, 1)


def solution(mesh):
    return jax.shard_map(
        local,
        mesh=mesh,
        in_specs=(P("rows", "band"), P("band", "rows", None), P("band", "rows", None)),
        out_specs=(P(None, "rows", "band"), P(None, "rows", "band")),
        check_vma=False,
    )
```

```python
import functools
import math

import jax
import jax.numpy as jnp
import ml_dtypes
import numpy as np
from jax import lax
from jax.experimental import pallas as pl
from jax.experimental.pallas import tpu as pltpu
from jax.sharding import PartitionSpec as P

F32 = jnp.float32
BF16 = jnp.bfloat16
MESH = pl.DeviceIdType.MESH
VM = pltpu.VMEM

BANDS = 8
STRIPS = 16
BLOCKS = 8
HEIGHT = 768
WIDTH = 12288
N1 = float(HEIGHT * WIDTH)
N2 = float(HEIGHT * WIDTH // 16)
NYQUIST_GAIN = 0.29


def gauss_taps(upscale, kernel_len):
    spread = upscale * math.sqrt(-2.0 * math.log(NYQUIST_GAIN)) / math.pi
    radius = kernel_len // 2
    offsets = np.arange(-radius, radius + 1) * 1.0
    values = np.exp(-(offsets**2) / (2.0 * spread**2))
    return values / values.sum()


def cubic_weight(distance):
    distance = abs(distance)
    if distance <= 1.0:
        return 1.5 * distance**3 - 2.5 * distance**2 + 1.0
    if distance < 2.0:
        return -0.5 * distance**3 + 2.5 * distance**2 - 4.0 * distance + 2.0
    return 0.0


def cubic_table(upscale):
    weights = np.zeros((5, upscale))
    for phase_index in range(upscale):
        centre = (phase_index + 0.5) / upscale - 0.5
        first_tap = math.floor(centre)
        fraction = centre - first_tap
        for tap_index in range(-1, 3):
            weights[first_tap + tap_index + 2, phase_index] += cubic_weight(tap_index - fraction)
    return weights


C4 = cubic_table(4)
C3 = cubic_table(3)
G4 = gauss_taps(4, 17)
G3 = gauss_taps(3, 13)
MEAN_TAPS = C4.mean(axis=1)


def split(matrix):
    high = matrix.astype(np.float32).astype(ml_dtypes.bfloat16)
    low = (matrix - high.astype(np.float64)).astype(ml_dtypes.bfloat16)
    return high, low


def tables():
    up_rows = np.zeros((48, 16))
    for m in range(12):
        for p in range(4):
            for t in range(5):
                up_rows[4 * m + p, m + t] += C4[t, p]
    up_cols = np.zeros((1536, 512))
    for m in range(384):
        for p in range(4):
            for t in range(5):
                up_cols[4 * m + p, (m + t - 2) % 512] += C4[t, p]
    gram_rows = up_rows.T @ up_rows
    gram_cols = up_cols.T @ up_cols
    lanes = np.zeros((16, 512), np.float32)
    at = np.arange(512)
    for t in range(-4, 5):
        lanes[t + 4] = gram_cols[at, (at + t) % 512]
    lanes[9] = up_cols.sum(axis=0)
    row_sum = up_rows.sum(axis=0)

    low = np.zeros((96, 112))
    for f in range(96):
        for t in range(17):
            low[f, f + t] = G4[t]
    mean = np.zeros((24, 112))
    mean_low = np.zeros((24, 112))
    for i in range(24):
        mean[i, 8 + 4 * i : 12 + 4 * i] = 0.25
        mean_low[i] = low[4 * i : 4 * i + 4].mean(axis=0)
    g3_rows = np.zeros((12, 24))
    for i in range(12):
        g3_rows[i, i : i + 13] = G3
    row_stack = []
    for variant in range(3):
        keep = np.ones((24, 1))
        if variant == 0:
            keep[:6] = 0.0
        if variant == 2:
            keep[18:] = 0.0
        row_stack.append(
            np.concatenate(
                [
                    low[24:72],
                    up_rows.T @ low[24:72],
                    mean_low[6:18],
                    g3_rows @ (keep * mean_low),
                    mean[6:18],
                    g3_rows @ (keep * mean),
                ]
            )
        )
    rows_hi, rows_lo = split(np.stack(row_stack))

    low_cols = np.zeros((256, 128))
    for o in range(128):
        for t in range(-8, 9):
            q = o + t
            row = q if 0 <= q < 128 else (q if q >= 128 else 256 + q)
            low_cols[row, o] = G4[t + 8]
    mean_cols = np.zeros((640, 128))
    for f in range(512):
        mean_cols[f, f // 4] = 0.25
    for f in range(32):
        mean_cols[512 + f, f // 4] = 0.25
        mean_cols[512 + 96 + f, 120 + f // 4] = 0.25
    back_cols = np.zeros((640, 128))
    for n in range(128):
        for t in range(5):
            for p in range(4):
                f = 4 * (n - (t - 2)) + p
                row = f if f >= 0 else 640 + f
                back_cols[row, n] += C4[t, p]
    fine = np.zeros((256, 512))
    for m in range(128):
        for p in range(4):
            for t in range(5):
                fine[(m + t - 2) % 256, 4 * m + p] += C4[t, p]
    third = np.zeros((256, 384))
    for m in range(128):
        for p in range(3):
            for t in range(5):
                third[(m + t - 2) % 256, 3 * m + p] += C3[t, p]
    constants = (
        rows_hi,
        rows_lo,
        *split(low_cols),
        mean_cols.astype(ml_dtypes.bfloat16),
        *split(back_cols),
        *split(fine),
        *split(third),
        lanes,
    )
    return constants, gram_rows, row_sum, up_rows


CONSTANTS, GRAM_ROWS, ROW_SUM, UP_ROWS = tables()
NUM_CONST = len(CONSTANTS)


def halves(x):
    high = x.astype(BF16)
    return high, (x - high.astype(F32)).astype(BF16)


def mm(a, b):
    return jnp.dot(a, b, preferred_element_type=F32)


def dot3(x, high, low):
    xh, xl = halves(x)
    return mm(xh, high) + mm(xl, high) + mm(xh, low)


def dot2(x, exact):
    xh, xl = halves(x)
    return mm(xh, exact) + mm(xl, exact)


def lane(shape):
    return lax.broadcasted_iota(jnp.int32, shape, len(shape) - 1)


def edge(next_tile, prev_tile):
    return jnp.where(lane(next_tile.shape) < 64, next_tile, prev_tile)


def shifted(x, t):
    n = x.shape[1]
    return x if t == 0 else pltpu.roll(x, (-t) % n, 1)


def col_filter(x, taps):
    radius = len(taps) // 2
    total = float(taps[radius]) * x
    for t in range(-radius, radius + 1):
        if t:
            total = total + float(taps[t + radius]) * shifted(x, t)
    return total


def pick(e, strip, row, tile):
    return e[strip, tile, pl.ds(row, 8, stride=8), :]


def vnir_row(e, strip, i):
    if i < 8:
        parts = [pick(e, strip, i, t) for t in range(3)] + [pick(e, strip, i, 5)]
    else:
        j = i - 8
        parts = [
            pick(e, strip, j, 3),
            pick(e, strip, 4 + j, 3),
            pick(e, strip, j, 4),
            pltpu.roll(pick(e, strip, j, 5), 64, 1),
        ]
    return jnp.concatenate(parts, axis=1)


def swir_row(e, strip, j):
    return jnp.concatenate(
        [pick(e, strip, 4 + j, 4), pltpu.roll(pick(e, strip, 4 + j, 5), 64, 1)], axis=1
    )


def fold(x):
    total = x[:, 0:128]
    for t in range(1, x.shape[1] // 128):
        total = total + x[:, 128 * t : 128 * t + 128]
    return total


def pack(vs, ss, sb):
    at = lane((8, 128))
    zero = jnp.zeros((8, 128), F32)

    def coarse(first, tile):
        return vs[pl.ds(24 * first + tile, 8, stride=24), :] if 0 <= tile < 24 else zero

    def short(tile):
        return ss[0:4, 128 * tile : 128 * tile + 128] if 0 <= tile < 8 else zero[0:4]

    for d in range(BLOCKS):
        for t in range(3):
            sb[d, t] = coarse(0, 3 * d + t)
        sb[d, 3, 0:4] = coarse(8, 3 * d)[0:4]
        sb[d, 3, 4:8] = coarse(8, 3 * d + 1)[0:4]
        sb[d, 4, 0:4] = coarse(8, 3 * d + 2)[0:4]
        sb[d, 4, 4:8] = short(d)
        sb[d, 5, 0:4] = edge(coarse(8, 3 * d + 3), coarse(8, 3 * d - 1))[0:4]
        sb[d, 5, 4:8] = edge(short(d + 1), short(d - 1))
        other = pltpu.roll(sb[d, 5], 64, 1)
        own = edge(coarse(0, 3 * d + 3), coarse(0, 3 * d - 1))
        sb[d, 5] = jnp.where((at >= 32) & (at < 96), other, own)


def pan_stage(pan_ext, consts, variant, d_out, ts, dd):
    rows_hi, rows_lo, low_hi, low_lo, mean_c, back_hi, back_lo = consts[:7]
    halo = edge(pan_ext[:, 1664:1792], pan_ext[:, 1536:1664])
    full = jnp.concatenate([pan_ext[:, 0:1536], halo], axis=1)
    fh, fl = halves(full)
    rh, rl = rows_hi[variant], rows_lo[variant]
    q = mm(rh, fh) + mm(rh, fl) + mm(rl, fh)
    top = q[0:88]
    tiles = [top[:, 128 * j : 128 * j + 128] for j in range(13)]
    lhs = jnp.concatenate(
        [
            jnp.concatenate([tiles[j], edge(tiles[(j + 1) % 13], tiles[(j + 12) % 13])], axis=1)
            for j in range(13)
        ],
        axis=0,
    )
    low = dot3(lhs, low_hi[...], low_lo[...])
    low_tile = [low[88 * j : 88 * j + 88] for j in range(13)]
    total = jnp.zeros((8, 128), F32)
    for j in range(12):
        d_out[:, 128 * j : 128 * j + 128] = (
            pan_ext[32:80, 128 * j : 128 * j + 128] - low_tile[j][0:48]
        )
        for k in range(6):
            total = total + low_tile[j][8 * k : 8 * k + 8]
    zero = jnp.zeros((16, 128), F32)
    back = [low_tile[j][48:64] for j in range(12)] + [zero]
    lhs = jnp.concatenate(
        [
            jnp.concatenate(
                back[4 * t : 4 * t + 4] + [edge(back[4 * t + 4], back[(4 * t + 12) % 13])], axis=1
            )
            for t in range(3)
        ],
        axis=0,
    )
    main = dot3(lhs, back_hi[...], back_lo[...])
    rim = dot3(edge(back[0], back[11]), back_hi[512:640], back_lo[512:640])
    for t in range(3):
        ts[:, 128 * t : 128 * t + 128] = main[16 * t : 16 * t + 16]
    ts[:, 384:512] = rim
    diff = [q[88:112, 128 * j : 128 * j + 128] - low_tile[j][64:88] for j in range(13)]
    lhs = jnp.concatenate(
        [jnp.concatenate(diff[4 * t : 4 * t + 4], axis=1) for t in range(3)], axis=0
    )
    main = dot2(lhs, mean_c[0:512])
    for t in range(3):
        dd[0:24, 128 * t : 128 * t + 128] = main[24 * t : 24 * t + 24]
    dd[0:24, 384:512] = dot2(diff[12], mean_c[512:640])
    return total


def column_mask(block):
    at = lane((1, 512))
    left = jnp.where(block == 0, 0.0, 1.0)
    right = jnp.where(block == BLOCKS - 1, 0.0, 1.0)
    return jnp.where(at >= 448, left, jnp.where(at >= 384, right, 1.0))


def mean_row(xs, i):
    total = None
    for t in range(5):
        term = float(MEAN_TAPS[t]) * xs[i + t]
        total = term if total is None else total + term
    return total


def gram_cols(lanes, x):
    y = lanes[4:5, :] * x
    for t in range(-4, 5):
        if t:
            y = y + lanes[t + 4 : t + 5, :] * shifted(x, t)
    return y


def early_compute(e, pan_ext, consts, r, d_out, ts, dd, xs, xc, vl):
    lanes = consts[11]
    variant = jnp.where(r == 0, 0, jnp.where(r == STRIPS - 1, 2, 1))
    for i in range(12):
        row = vnir_row(e, 1, i)
        xs[i + 8] = row
        xc[i + 2] = gram_cols(lanes, row)
    for i in range(2, 10):
        vl[i] = col_filter(mean_row(xs, i + 6), MEAN_TAPS)[:, 0:384]
    return pan_stage(pan_ext, consts, variant, d_out, ts, dd)


def front_compute(e, consts, pan_sum, r, c, ts, dd, xs, xc, ys, lvs, vl, swu, dl, rl):
    third_hi, third_lo, lanes = consts[9:12]
    sums = {10: pan_sum[...]}
    for k in range(28):
        if k < 8:
            xs[k] = vnir_row(e, 0, k + 4)
        elif k >= 20:
            xs[k] = vnir_row(e, 2, k - 20)
    for i in (0, 1, 14, 15):
        xc[i] = gram_cols(lanes, xs[i + 6])
    for i in range(16):
        total = None
        for j in range(16):
            if GRAM_ROWS[i, j] != 0.0:
                term = float(GRAM_ROWS[i, j]) * xc[j]
                total = term if total is None else total + term
        ys[i] = total
    acc = [jnp.zeros((8, 128), F32) for _ in range(10)]
    ones = lanes[9:10, :]
    for i in range(16):
        x = xs[i + 6]
        for j in range(8):
            acc[j] = acc[j] + fold(x * ys[i, j : j + 1, :])
        acc[8] = acc[8] + fold(x * ts[i : i + 1, :])
        acc[9] = acc[9] + float(ROW_SUM[i]) * fold(x * ones)
    for k in range(10):
        sums[k] = acc[k]
    up_keep = jnp.where(r == 0, 0.0, 1.0)
    down_keep = jnp.where(r == STRIPS - 1, 0.0, 1.0)
    mask = column_mask(c)
    mean_rows = []
    for i in range(24):
        total = mean_row(xs, i)
        if i < 6:
            total = total * up_keep
        if i >= 18:
            total = total * down_keep
        mean_rows.append(total)
    for i in range(12):
        total = float(G3[6]) * mean_rows[i + 6]
        for t in range(6):
            total = total + float(G3[t]) * (mean_rows[i + t] + mean_rows[i + 12 - t])
        lowered = col_filter(total, MEAN_TAPS) * mask
        lowered = col_filter(lowered, G3)[:, 0:384]
        lvs[i] = lowered
        if 2 <= i < 10:
            vl[i] = vl[i] - lowered
        else:
            vl[i] = col_filter(mean_rows[i + 6], MEAN_TAPS)[:, 0:384] - lowered
    dcol = dd[8:24, :] * mask
    dcol = col_filter(dcol, G3)[:, 0:384]
    low_d = dcol[4:16]
    dl[...] = dd[0:12, 0:384] - low_d
    ts[0:12, 0:384] = low_d
    srow = [
        swir_row(e, *at)
        for at in ((0, 2), (0, 3), (1, 0), (1, 1), (1, 2), (1, 3), (2, 0), (2, 1))
    ]
    up = []
    for m in range(4):
        for p in range(3):
            total = None
            for t in range(5):
                if C3[t, p] != 0.0:
                    term = float(C3[t, p]) * srow[m + t]
                    total = term if total is None else total + term
            up.append(total)
    swu[...] = dot3(jnp.concatenate(up, axis=0), third_hi[...], third_lo[...])
    acc = [jnp.zeros((8, 128), F32) for _ in range(22)]
    for i in range(12):
        lv = lvs[i]
        sw = swu[8 * i : 8 * i + 8, :]
        ld = ts[i : i + 1, 0:384]
        for j in range(8):
            other = lvs[i, j : j + 1, :]
            acc[j] = acc[j] + fold(lv * other)
            acc[8 + j] = acc[8 + j] + fold(sw * other)
        acc[16] = acc[16] + fold(lv * ld)
        acc[17] = acc[17] + fold(sw * ld)
        acc[18] = acc[18] + fold(lv)
        acc[19] = acc[19] + fold(sw)
        acc[20] = acc[20] + fold(ld)
        acc[21] = acc[21] + fold(ld * ld)
    for k in range(22):
        sums[16 + k] = acc[k]
    at = lane((8, 128))
    packed = jnp.zeros((8, 128), F32)
    for k, value in sums.items():
        packed = jnp.where(at == k, jnp.sum(value, axis=1, keepdims=True), packed)
    rl[...] = packed


def upsample(xs, consts, zs, up_out):
    fine_hi, fine_lo = consts[7:9]
    for m in range(12):
        for p in range(4):
            total = None
            for t in range(5):
                if C4[t, p] != 0.0:
                    term = float(C4[t, p]) * xs[m + t + 6]
                    total = term if total is None else total + term
            for tile in range(4):
                zs[tile, pl.ds(4 * m + p, 8, stride=48), :] = total[
                    :, 128 * tile : 128 * tile + 128
                ]

    @pl.loop(0, BANDS)
    def _(b):
        at = pl.ds(pl.multiple_of(b * 48, 48), 48)
        z = [zs[k, at, :] for k in range(4)]
        lhs = jnp.concatenate(
            [
                jnp.concatenate([z[k], edge(z[k + 1], z[(k + 3) % 4])], axis=1)
                for k in range(3)
            ],
            axis=0,
        )
        up = dot3(lhs, fine_hi[...], fine_lo[...])
        for k in range(3):
            up_out[at, 512 * k : 512 * k + 512] = up[48 * k : 48 * k + 48]


def front_kernel(pan, vnir, swir, *rest):
    hbm_consts = rest[:NUM_CONST]
    rt, up_out, d_out, vl, swu, dl = rest[NUM_CONST : NUM_CONST + 6]
    rest = rest[NUM_CONST + 6 :]
    consts = rest[:NUM_CONST]
    (vs, ss, sb, e, pe, xs, xc, ys, ts, dd, lvs, zs, pan_sum, rl, g1, mid, g2) = rest[
        NUM_CONST : NUM_CONST + 17
    ]
    (csem, lsem, ssem, rsem, fsem, hsem, psem, qsem, g1s, g1r, g2s, g2r) = rest[NUM_CONST + 17 :]
    r = lax.axis_index("rows")
    c = lax.axis_index("band")

    def remote(src, dst, send, recv, row, block):
        return pltpu.make_async_remote_copy(
            src_ref=src, dst_ref=dst, send_sem=send, recv_sem=recv,
            device_id=(row, block), device_id_type=MESH,
        )

    rl8 = lax.rem(r, 8)
    base = r - rl8
    barrier = pltpu.get_barrier_semaphore()

    def greet(row, block):
        pl.semaphore_signal(barrier, inc=1, device_id=(row, block), device_id_type=MESH)

    core = lax.rem(rl8, 2)
    x = lax.div(rl8, 2)
    y_hi, z = lax.div(c, 4), lax.rem(c, 4)
    y_lo = lax.div(r, 8)
    y = 2 * y_hi + y_lo

    def step_one(dx, dcore):
        return 2 * lax.rem(x + dx, 4) + lax.rem(core + dcore, 2)

    def step_two(dy, dz):
        return 4 * lax.rem(y + dy, 4) + lax.rem(z + dz, 4)

    def place_two(slot):
        y2 = lax.div(slot, 4)
        return 8 * lax.rem(y2, 2) + rl8, 4 * lax.div(y2, 2) + lax.rem(slot, 4)

    near = lambda d: min(d, 4 - d)
    ones = sorted(
        [(dx, dc) for dx in range(4) for dc in range(2) if dx or dc], key=lambda d: (-near(d[0]), -d[1])
    )
    twos = sorted(
        [(dy, dz) for dy in range(4) for dz in range(4) if dy or dz],
        key=lambda d: (-near(d[0]) - near(d[1]), d),
    )
    first = [(base + step_one(*d), c) for d in ones]
    second = [place_two(step_two(*d)) for d in twos]
    around = [(lax.rem(r + 1, STRIPS), c), (lax.rem(r + STRIPS - 1, STRIPS), c)]
    partners = second + first + around
    for row, block in partners:
        greet(row, block)

    loads = [
        pltpu.make_async_copy(vnir, vs.at[pl.ds(0, 288)], lsem.at[0]),
        pltpu.make_async_copy(swir.at[0], ss, lsem.at[1]),
        pltpu.make_async_copy(pan, pe.at[pl.ds(32, 48), pl.ds(0, 1536)], lsem.at[2]),
    ]
    for copy in loads:
        copy.start()
    const_loads = [
        pltpu.make_async_copy(hbm_consts[k], consts[k], csem.at[k]) for k in range(NUM_CONST)
    ]

    @pl.when(r == 0)
    def _():
        pe[0:32, :] = jnp.zeros((32, 1792), F32)
        e[0] = jnp.zeros((6, 64, 128), F32)

    @pl.when(r == STRIPS - 1)
    def _():
        pe[80:112, :] = jnp.zeros((32, 1792), F32)
        e[2] = jnp.zeros((6, 64, 128), F32)

    @pl.when(c == 0)
    def _():
        pe[32:80, 1536:1664] = jnp.zeros((48, 128), F32)

    @pl.when(c == BLOCKS - 1)
    def _():
        pe[32:80, 1664:1792] = jnp.zeros((48, 128), F32)

    loads[0].wait()
    loads[1].wait()
    pack(vs, ss, sb)
    loads[2].wait()
    pl.semaphore_wait(barrier, len(partners))

    def pan_cols(side):
        src = pe.at[pl.ds(32, 48), pl.ds(1408, 128)] if side == 0 else pan_first
        dst = pe.at[pl.ds(32, 48), pl.ds(1536 + 128 * side, 128)]
        block = c + 1 if side == 0 else c - 1
        return remote(src, dst, psem.at[side], qsem.at[side], r, block)

    pan_first = pe.at[pl.ds(32, 48), pl.ds(0, 128)]

    def pan_rows(side):
        src = pe.at[pl.ds(48, 32), pl.ds(0, 1536)] if side == 0 else pe.at[pl.ds(32, 32), pl.ds(0, 1536)]
        dst = pe.at[pl.ds(0, 32), pl.ds(0, 1536)] if side == 0 else pe.at[pl.ds(80, 32), pl.ds(0, 1536)]
        row = r + 1 if side == 0 else r - 1
        return remote(src, dst, psem.at[2 + side], qsem.at[2 + side], row, c)

    def pan_corner(side):
        src = pe.at[pl.ds(48, 32), pl.ds(1536, 256)] if side == 0 else pe.at[pl.ds(32, 32), pl.ds(1536, 256)]
        dst = pe.at[pl.ds(0, 32), pl.ds(1536, 256)] if side == 0 else pe.at[pl.ds(80, 32), pl.ds(1536, 256)]
        row = r + 1 if side == 0 else r - 1
        return remote(src, dst, psem.at[4 + side], qsem.at[4 + side], row, c)

    has_below, has_above = r < STRIPS - 1, r > 0
    has_right, has_left = c < BLOCKS - 1, c > 0

    def when(cond, action):
        @pl.when(cond)
        def _():
            action()

    when(has_right, lambda: pan_cols(0).start())
    when(has_left, lambda: pan_cols(1).start())

    def band_rows(b):
        return pl.ds(pl.multiple_of(b * 8, 8), 8)

    turns = [(0, 0), (1, 2), (1, 1), (1, 3), (1, 0), (0, 2), (0, 1), (0, 3)]

    def band_at(dyh, dz):
        return 4 * lax.rem(y_hi + dyh, 2) + lax.rem(z + dz, 4)

    def block_send(k):
        block = band_at(*turns[k])
        return remote(sb.at[block], e.at[1, pl.ds(0, 6), band_rows(c)], ssem.at[k], rsem.at[k], r, block)

    def block_recv(k):
        b = band_at(turns[k][0], 4 - turns[k][1])
        return remote(sb.at[0], e.at[1, pl.ds(0, 6), band_rows(b)], ssem.at[k], rsem.at[k], r, c)

    def forward(k, side):
        b = band_at(turns[k][0], 4 - turns[k][1])
        dst = e.at[2 * side, pl.ds(0, 6), band_rows(b)]
        src = sb.at[c] if k == 0 else e.at[1, pl.ds(0, 6), band_rows(b)]
        row = r + 1 if side == 0 else r - 1
        return remote(src, dst, fsem.at[side, k], hsem.at[side, k], row, c)

    for k in range(1, 8):
        block_send(k).start()
    own = pltpu.make_async_copy(sb.at[c], e.at[1, pl.ds(0, 6), band_rows(c)], lsem.at[3])
    own.start()
    when(has_below, lambda: forward(0, 0).start())
    when(has_above, lambda: forward(0, 1).start())
    when(has_below, lambda: pan_rows(0).start())
    when(has_above, lambda: pan_rows(1).start())

    for copy in const_loads:
        copy.start()

    when(has_left, lambda: pan_cols(0).wait_recv())
    when(has_right, lambda: pan_cols(1).wait_recv())
    when(has_below, lambda: pan_corner(0).start())
    when(has_above, lambda: pan_corner(1).start())
    for k in range(7, 0, -1):
        block_recv(k).wait_recv()
        when(has_below, functools.partial(lambda k: forward(k, 0).start(), k))
        when(has_above, functools.partial(lambda k: forward(k, 1).start(), k))
    own.wait()
    for copy in const_loads:
        copy.wait()
    when(has_above, lambda: (pan_rows(0).wait_recv(), pan_corner(0).wait_recv()))
    when(has_below, lambda: (pan_rows(1).wait_recv(), pan_corner(1).wait_recv()))
    pan_sum[...] = early_compute(e, pe, consts, r, d_out, ts, dd, xs, xc, vl)
    for k in range(8):
        when(has_above, functools.partial(lambda k: forward(k, 0).wait_recv(), k))
        when(has_below, functools.partial(lambda k: forward(k, 1).wait_recv(), k))

    front_compute(e, consts, pan_sum, r, c, ts, dd, xs, xc, ys, lvs, vl, swu, dl, rl)

    me_two = 4 * y + z

    def sum_one(n):
        row, block = first[n]
        return remote(rl, g1.at[rl8], g1s.at[n], g1r.at[n], row, block)

    def sum_one_recv(n):
        dx, dc = ones[n]
        return remote(rl, g1.at[step_one(4 - dx, 2 - dc)], g1s.at[n], g1r.at[n], r, c)

    def sum_two(n):
        row, block = second[n]
        return remote(mid, g2.at[me_two], g2s.at[n], g2r.at[n], row, block)

    def sum_two_recv(n):
        dy, dz = twos[n]
        return remote(mid, g2.at[step_two(4 - dy, 4 - dz)], g2s.at[n], g2r.at[n], r, c)

    for n in range(7):
        sum_one(n).start()
    g1[rl8] = rl[...]
    for n in range(7):
        sum_one_recv(n).wait_recv()
    total = g1[0]
    for k in range(1, 8):
        total = total + g1[k]
    mid[...] = total
    for n in range(15):
        sum_two(n).start()
    g2[me_two] = total
    upsample(xs, consts, zs, up_out)
    for n in range(15):
        sum_two_recv(n).wait_recv()
    total = g2[0]
    for k in range(1, 16):
        total = total + g2[k]
    rt[...] = total

    for k in range(1, 8):
        block_send(k).wait_send()
        sum_one(k - 1).wait_send()
    for n in range(15):
        sum_two(n).wait_send()
    when(has_right, lambda: pan_cols(0).wait_send())
    when(has_left, lambda: pan_cols(1).wait_send())
    for side, cond in ((0, has_below), (1, has_above)):
        when(cond, functools.partial(lambda side: (pan_rows(side).wait_send(), pan_corner(side).wait_send()), side))
        for k in range(8):
            when(cond, functools.partial(lambda k, side: forward(k, side).wait_send(), k, side))


def front(pan, vnir, swir):
    return pl.pallas_call(
        front_kernel,
        name="front",
        out_shape=[
            VM((8, 128), F32),
            VM((384, 1536), F32),
            VM((48, 1536), F32),
            VM((12, 8, 384), F32),
            VM((96, 384), F32),
            VM((12, 384), F32),
        ],
        in_specs=[pl.BlockSpec(memory_space=pl.ANY)] * (3 + NUM_CONST),
        out_specs=[pl.BlockSpec(memory_space=VM)] * 6,
        scratch_shapes=[VM(k.shape, BF16 if k.dtype == ml_dtypes.bfloat16 else F32) for k in CONSTANTS]
        + [
            VM((384, 128), F32),
            VM((4, 1024), F32),
            VM((8, 6, 8, 128), F32),
            VM((3, 6, 64, 128), F32),
            VM((112, 1792), F32),
            VM((28, 8, 512), F32),
            VM((16, 8, 512), F32),
            VM((16, 8, 512), F32),
            VM((16, 512), F32),
            VM((24, 512), F32),
            VM((12, 8, 384), F32),
            VM((4, 384, 128), F32),
            VM((8, 128), F32),
            VM((8, 128), F32),
            VM((8, 8, 128), F32),
            VM((8, 128), F32),
            VM((16, 8, 128), F32),
            pltpu.SemaphoreType.DMA((NUM_CONST,)),
            pltpu.SemaphoreType.DMA((4,)),
            pltpu.SemaphoreType.DMA((8,)),
            pltpu.SemaphoreType.DMA((8,)),
            pltpu.SemaphoreType.DMA((2, 8)),
            pltpu.SemaphoreType.DMA((2, 8)),
            pltpu.SemaphoreType.DMA((6,)),
            pltpu.SemaphoreType.DMA((6,)),
            pltpu.SemaphoreType.DMA((8,)),
            pltpu.SemaphoreType.DMA((8,)),
            pltpu.SemaphoreType.DMA((16,)),
            pltpu.SemaphoreType.DMA((16,)),
        ],
        compiler_params=pltpu.CompilerParams(
            collective_id=0, has_side_effects=True, vmem_limit_bytes=56 << 20
        ),
    )(pan, vnir, swir, *[jnp.asarray(k) for k in CONSTANTS])


def solve_spd(a, b):
    a = [list(row) for row in a]
    inverse = []
    factor = [[None] * 8 for _ in range(8)]
    for j in range(8):
        inv = 1.0 / a[j][j]
        inverse.append(inv)
        for i in range(j + 1, 8):
            factor[i][j] = a[i][j] * inv
        for i in range(j + 1, 8):
            for k in range(j + 1, i + 1):
                a[i][k] = a[i][k] - factor[i][j] * a[k][j]
    z = list(b)
    for j in range(8):
        for i in range(j + 1, 8):
            z[i] = z[i] - factor[i][j] * z[j]
    z = [z[j] * inverse[j] for j in range(8)]
    for j in range(7, -1, -1):
        for i in range(j):
            z[i] = z[i] - factor[j][i] * z[j]
    return z


def total_of(values):
    total = values[0]
    for value in values[1:]:
        total = total + value
    return total


def solve_first(rt, cb):
    for k in range(11):
        cb[k] = jnp.broadcast_to(rt[:, k : k + 1], (8, 128))
    mean = [cb[9, i : i + 1, :] * (1.0 / N1) for i in range(8)]
    mean_p = jnp.sum(cb[10], axis=0, keepdims=True) * (1.0 / N1)
    a = [
        [cb[j, i : i + 1, :] * (1.0 / N1) - mean[i] * mean[j] for j in range(i + 1)]
        for i in range(8)
    ]
    b = [cb[8, i : i + 1, :] * (1.0 / N1) - mean[i] * mean_p for i in range(8)]
    w = solve_spd(a, b)
    scale = 1.0 / total_of([b[i] * w[i] for i in range(8)])
    return [b[i] * scale for i in range(8)]


def solve_second(rt, cb, gain):
    for k in range(16, 38):
        cb[k] = jnp.broadcast_to(rt[:, k : k + 1], (8, 128))

    def at(k, i):
        return cb[k, i : i + 1, :]

    sum_d = at(36, 0)
    sum_dd = at(37, 0)
    q = [at(32, i) for i in range(8)]
    mean2 = [(at(34, i) + gain[i] * sum_d) * (1.0 / N2) for i in range(8)]
    a2 = [
        [
            (at(16 + j, i) + gain[i] * q[j] + gain[j] * q[i] + gain[i] * gain[j] * sum_dd) * (1.0 / N2)
            - mean2[i] * mean2[j]
            for j in range(i + 1)
        ]
        for i in range(8)
    ]
    swir_mean = cb[35] * (1.0 / N2)
    cross = [
        (cb[24 + i] + gain[i] * cb[33]) * (1.0 / N2) - mean2[i] * swir_mean for i in range(8)
    ]
    y = [jnp.sum(cross[i], axis=0, keepdims=True) * 0.125 for i in range(8)]
    v = solve_spd(a2, y)
    share = total_of([v[i] * cross[i] for i in range(8)]) / total_of([v[i] * y[i] for i in range(8)])
    return v, share


def wide(x, copies):
    return jnp.concatenate([x] * copies, axis=1)


def back_kernel(rt, up, d, vl, swu, dl, joined, joined_swir, cb, gs, out, sem):
    gain = solve_first(rt, cb)
    for b in range(8):
        gs[b] = jnp.broadcast_to(gain[b], (8, 128))

    @pl.loop(0, BANDS)
    def _(b):
        g = wide(gs[b], 2)
        rows = pl.multiple_of(b * 48, 48)
        for i in range(6):
            for t in range(6):
                at = slice(256 * t, 256 * t + 256)
                out[b, 8 * i : 8 * i + 8, at] = (
                    up[pl.ds(rows + 8 * i, 8), at] + g * d[8 * i : 8 * i + 8, at]
                )
        pltpu.make_async_copy(out.at[b], joined.at[b], sem.at[b]).start()

    gain = [gs[b, 0:1, :] for b in range(8)]
    v, share = solve_second(rt, cb, gain)
    row8 = lax.broadcasted_iota(jnp.int32, (8, 128), 0)
    v8 = jnp.zeros((8, 128), F32)
    for b in range(8):
        v8 = jnp.where(row8 == b, jnp.broadcast_to(v[b], (8, 128)), v8)
    v8 = wide(v8, 3)
    vg = wide(total_of([v[b] * gain[b] for b in range(8)]), 3)
    share3 = wide(share, 3)
    for i in range(12):
        detail = jnp.sum(v8 * vl[i], axis=0, keepdims=True) + vg * dl[i : i + 1, :]
        joined_swir[i] = swu[8 * i : 8 * i + 8, :] + share3 * detail

    @pl.loop(0, BANDS)
    def _(b):
        pltpu.make_async_copy(out.at[b], joined.at[b], sem.at[b]).wait()


def back(rt, up, d, vl, swu, dl):
    return pl.pallas_call(
        back_kernel,
        name="back",
        out_shape=[
            jax.ShapeDtypeStruct((8, 48, 1536), F32),
            jax.ShapeDtypeStruct((12, 8, 384), F32),
        ],
        in_specs=[pl.BlockSpec(memory_space=VM)] * 6,
        out_specs=[pl.BlockSpec(memory_space=pl.ANY), pl.BlockSpec(memory_space=VM)],
        scratch_shapes=[
            VM((38, 8, 128), F32),
            VM((8, 8, 128), F32),
            VM((8, 48, 1536), F32),
            pltpu.SemaphoreType.DMA((8,)),
        ],
        compiler_params=pltpu.CompilerParams(vmem_limit_bytes=32 << 20),
    )(rt, up, d, vl, swu, dl)


def local(pan, vnir, swir):
    joined, rows = back(*front(pan, vnir.reshape(288, 128), swir))
    return joined, jnp.swapaxes(rows, 0, 1)


def solution(mesh):
    return jax.shard_map(
        local,
        mesh=mesh,
        in_specs=(P("rows", "band"), P("band", "rows", None), P("band", "rows", None)),
        out_specs=(P(None, "rows", "band"), P(None, "rows", "band")),
        check_vma=False,
    )
```

```python
import functools
import math

import jax
import jax.numpy as jnp
import ml_dtypes
import numpy as np
from jax import lax
from jax.experimental import pallas as pl
from jax.experimental.pallas import tpu as pltpu
from jax.sharding import PartitionSpec as P

F32 = jnp.float32
BF16 = jnp.bfloat16
MESH = pl.DeviceIdType.MESH
VM = pltpu.VMEM

BANDS = 8
STRIPS = 16
BLOCKS = 8
HEIGHT = 768
WIDTH = 12288
N1 = float(HEIGHT * WIDTH)
N2 = float(HEIGHT * WIDTH // 16)
NYQUIST_GAIN = 0.29


def gauss_taps(upscale, kernel_len):
    spread = upscale * math.sqrt(-2.0 * math.log(NYQUIST_GAIN)) / math.pi
    radius = kernel_len // 2
    offsets = np.arange(-radius, radius + 1) * 1.0
    values = np.exp(-(offsets**2) / (2.0 * spread**2))
    return values / values.sum()


def cubic_weight(distance):
    distance = abs(distance)
    if distance <= 1.0:
        return 1.5 * distance**3 - 2.5 * distance**2 + 1.0
    if distance < 2.0:
        return -0.5 * distance**3 + 2.5 * distance**2 - 4.0 * distance + 2.0
    return 0.0


def cubic_table(upscale):
    weights = np.zeros((5, upscale))
    for phase_index in range(upscale):
        centre = (phase_index + 0.5) / upscale - 0.5
        first_tap = math.floor(centre)
        fraction = centre - first_tap
        for tap_index in range(-1, 3):
            weights[first_tap + tap_index + 2, phase_index] += cubic_weight(tap_index - fraction)
    return weights


C4 = cubic_table(4)
C3 = cubic_table(3)
G4 = gauss_taps(4, 17)
G3 = gauss_taps(3, 13)
MEAN_TAPS = C4.mean(axis=1)


def split(matrix):
    high = matrix.astype(np.float32).astype(ml_dtypes.bfloat16)
    low = (matrix - high.astype(np.float64)).astype(ml_dtypes.bfloat16)
    return high, low


def tables():
    up_rows = np.zeros((48, 16))
    for m in range(12):
        for p in range(4):
            for t in range(5):
                up_rows[4 * m + p, m + t] += C4[t, p]
    up_cols = np.zeros((1536, 512))
    for m in range(384):
        for p in range(4):
            for t in range(5):
                up_cols[4 * m + p, (m + t - 2) % 512] += C4[t, p]
    gram_rows = up_rows.T @ up_rows
    gram_cols = up_cols.T @ up_cols
    lanes = np.zeros((16, 512), np.float32)
    at = np.arange(512)
    for t in range(-4, 5):
        lanes[t + 4] = gram_cols[at, (at + t) % 512]
    lanes[9] = up_cols.sum(axis=0)
    row_sum = up_rows.sum(axis=0)

    low = np.zeros((48, 64))
    mean = np.zeros((16, 64))
    for f in range(48):
        low[f, f : f + 17] = G4
    for i in range(12):
        mean[i, 8 + 4 * i : 12 + 4 * i] = 0.25
    mean_low = np.zeros((16, 64))
    mean_low[:12] = low.reshape(12, 4, 64).mean(axis=1)
    rows_hi, rows_lo = split(np.concatenate([low, up_rows.T @ low, mean_low, mean]))

    low_cols = np.zeros((256, 128))
    for o in range(128):
        for t in range(-8, 9):
            q = o + t
            row = q if 0 <= q < 128 else (q if q >= 128 else 256 + q)
            low_cols[row, o] = G4[t + 8]
    mean_cols = np.zeros((640, 128))
    for f in range(512):
        mean_cols[f, f // 4] = 0.25
    for f in range(32):
        mean_cols[512 + f, f // 4] = 0.25
        mean_cols[512 + 96 + f, 120 + f // 4] = 0.25
    back_cols = np.zeros((640, 128))
    for n in range(128):
        for t in range(5):
            for p in range(4):
                f = 4 * (n - (t - 2)) + p
                row = f if f >= 0 else 640 + f
                back_cols[row, n] += C4[t, p]
    fine = np.zeros((256, 512))
    for m in range(128):
        for p in range(4):
            for t in range(5):
                fine[(m + t - 2) % 256, 4 * m + p] += C4[t, p]
    third = np.zeros((256, 384))
    for m in range(128):
        for p in range(3):
            for t in range(5):
                third[(m + t - 2) % 256, 3 * m + p] += C3[t, p]
    constants = (
        rows_hi,
        rows_lo,
        *split(low_cols),
        mean_cols.astype(ml_dtypes.bfloat16),
        *split(back_cols),
        *split(fine),
        *split(third),
        lanes,
    )
    return constants, gram_rows, row_sum, up_rows


CONSTANTS, GRAM_ROWS, ROW_SUM, UP_ROWS = tables()
NUM_CONST = len(CONSTANTS)


def halves(x):
    high = x.astype(BF16)
    return high, (x - high.astype(F32)).astype(BF16)


def mm(a, b):
    return jnp.dot(a, b, preferred_element_type=F32)


def dot3(x, high, low):
    xh, xl = halves(x)
    return mm(xh, high) + mm(xl, high) + mm(xh, low)


def dot2(x, exact):
    xh, xl = halves(x)
    return mm(xh, exact) + mm(xl, exact)


def lane(shape):
    return lax.broadcasted_iota(jnp.int32, shape, len(shape) - 1)


def edge(next_tile, prev_tile):
    return jnp.where(lane(next_tile.shape) < 64, next_tile, prev_tile)


def shifted(x, t):
    n = x.shape[1]
    return x if t == 0 else pltpu.roll(x, (-t) % n, 1)


def col_filter(x, taps):
    radius = len(taps) // 2
    total = float(taps[radius]) * x
    for t in range(1, radius + 1):
        total = total + float(taps[radius + t]) * (shifted(x, t) + shifted(x, -t))
    return total


TILES = 7


def pick(e, strip, row, tile):
    return e[strip, tile, pl.ds(row, 8, stride=8), :]


def vnir_row(e, strip, i):
    first, at = (0, i) if strip == 2 or (strip == 1 and i < 8) else (4, i - 4)
    halo = pick(e, strip, i, 3) if i < 8 else pltpu.roll(pick(e, strip, i - 8, 3), 64, 1)
    return jnp.concatenate([pick(e, strip, at, first + t) for t in range(3)] + [halo], axis=1)


def swir_row(e, strip, j):
    at = lane((8, 128))
    base = 16 if j < 2 else 80
    row = None
    for k in range(4):
        part = pltpu.roll(pick(e, strip, 4 * (j % 2) + k, 3), (32 * k - base) % 128, 1)
        row = part if row is None else jnp.where(at >= 32 * k, part, row)
    return jnp.concatenate([row, pltpu.roll(pick(e, strip, 4 + j, 3), 64, 1)], axis=1)


def total_of(values):
    total = values[0]
    for value in values[1:]:
        total = total + value
    return total


def fold(x):
    total = x[:, 0:128]
    for t in range(1, x.shape[1] // 128):
        total = total + x[:, 128 * t : 128 * t + 128]
    return total


def pack(vs, ss, sb):
    at = lane((8, 128))
    zero = jnp.zeros((8, 128), F32)

    def coarse(first, tile):
        return vs[pl.ds(24 * first + tile, 8, stride=24), :] if 0 <= tile < 24 else zero

    def short(tile):
        return ss[0:4, 128 * tile : 128 * tile + 128] if 0 <= tile < 8 else zero[0:4]

    sub = lax.broadcasted_iota(jnp.int32, (8, 128), 0)
    for d in range(BLOCKS):
        for t in range(3):
            sb[d, t] = coarse(0, 3 * d + t)
            sb[d, 4 + t] = coarse(4, 3 * d + t)
        sb[d, 3, 0:4] = edge(coarse(8, 3 * d + 3), coarse(8, 3 * d - 1))[0:4]
        sb[d, 3, 4:8] = edge(short(d + 1), short(d - 1))
        other = pltpu.roll(sb[d, 3], 64, 1)
        own = edge(coarse(0, 3 * d + 3), coarse(0, 3 * d - 1))
        tile = jnp.where((at >= 56) & (at < 72), other, own)
        for j in (0, 2):
            base = 16 + 32 * j
            rows = jnp.where(
                sub < 4,
                ss[j : j + 1, 128 * d : 128 * d + 128],
                ss[j + 1 : j + 2, 128 * d : 128 * d + 128],
            )
            quarters = None
            for k in range(4):
                part = pltpu.roll(rows, (base - 32 * k) % 128, 1)
                quarters = part if quarters is None else jnp.where(lax.rem(sub, 4) == k, part, quarters)
            tile = jnp.where((at >= base) & (at < base + 32), quarters, tile)
        sb[d, 3] = tile


def pan_full(pan_ext):
    halo = edge(pan_ext[:, 1664:1792], pan_ext[:, 1536:1664])
    return halves(jnp.concatenate([pan_ext[:, 0:1536], halo], axis=1))


def pan_low_tiles(rows, consts, count):
    tiles = [rows[:count, 128 * j : 128 * j + 128] for j in range(13)]
    lhs = jnp.concatenate(
        [
            jnp.concatenate([tiles[j], edge(tiles[(j + 1) % 13], tiles[(j + 12) % 13])], axis=1)
            for j in range(13)
        ],
        axis=0,
    )
    low = dot3(lhs, consts[2][...], consts[3][...])
    return [low[count * j : count * j + count] for j in range(13)]


def mean_stage(pan_ext, consts, dd, down):
    fh, fl = pan_full(pan_ext)
    rh, rl = consts[0][64:96], consts[1][64:96]
    q = mm(rh, fh) + mm(rh, fl) + mm(rl, fh)
    low_tile = pan_low_tiles(q, consts, 16)
    diff = [q[16:32, 128 * j : 128 * j + 128] - low_tile[j] for j in range(13)]
    lhs = jnp.concatenate(
        [jnp.concatenate(diff[4 * t : 4 * t + 4], axis=1) for t in range(3)], axis=0
    )
    mean_c = consts[4]
    main = dot2(lhs, mean_c[0:512])
    for t in range(3):
        dd[8:24, 128 * t : 128 * t + 128] = main[16 * t : 16 * t + 16]
    dd[8:24, 384:512] = dot2(diff[12], mean_c[512:640])
    down[...] = dd[12:20, :]


def pan_stage(pan_ext, consts, d_out, ts):
    back_hi, back_lo = consts[5:7]
    fh, fl = pan_full(pan_ext)
    rh, rl = consts[0][0:64], consts[1][0:64]
    q = mm(rh, fh) + mm(rh, fl) + mm(rl, fh)
    low_tile = pan_low_tiles(q, consts, 64)
    total = jnp.zeros((8, 128), F32)
    for j in range(12):
        d_out[:, 128 * j : 128 * j + 128] = (
            pan_ext[8:56, 128 * j : 128 * j + 128] - low_tile[j][0:48]
        )
        for k in range(6):
            total = total + low_tile[j][8 * k : 8 * k + 8]
    zero = jnp.zeros((16, 128), F32)
    back = [low_tile[j][48:64] for j in range(12)] + [zero]
    lhs = jnp.concatenate(
        [
            jnp.concatenate(
                back[4 * t : 4 * t + 4] + [edge(back[4 * t + 4], back[(4 * t + 12) % 13])], axis=1
            )
            for t in range(3)
        ],
        axis=0,
    )
    main = dot3(lhs, back_hi[...], back_lo[...])
    rim = dot3(edge(back[0], back[11]), back_hi[512:640], back_lo[512:640])
    for t in range(3):
        ts[:, 128 * t : 128 * t + 128] = main[16 * t : 16 * t + 16]
    ts[:, 384:512] = rim
    return total


def column_mask(block):
    at = lane((1, 512))
    left = jnp.where(block == 0, 0.0, 1.0)
    right = jnp.where(block == BLOCKS - 1, 0.0, 1.0)
    return jnp.where(at >= 448, left, jnp.where(at >= 384, right, 1.0))


def mean_row(xs, i):
    total = None
    for t in range(5):
        term = float(MEAN_TAPS[t]) * xs[i + t]
        total = term if total is None else total + term
    return total


def gram_cols(lanes, x):
    y = lanes[4:5, :] * x
    for t in range(-4, 5):
        if t:
            y = y + lanes[t + 4 : t + 5, :] * shifted(x, t)
    return y


OWN = range(2, 14)
RIM = (0, 1, 14, 15)
EARLY = range(2, 10)


def gram_row(xc, i, among, scale):
    total = None
    for j in among:
        if GRAM_ROWS[i, j] != 0.0:
            term = float(scale * GRAM_ROWS[i, j]) * xc[j]
            total = term if total is None else total + term
    return total


def add_products(acc, xs, ys, ts, ones, i):
    x = xs[i + 6]
    for j in range(8):
        acc[j] = acc[j] + fold(x * ys[i, j : j + 1, :])
    acc[8] = acc[8] + fold(x * ts[i : i + 1, :])
    acc[9] = acc[9] + float(ROW_SUM[i]) * fold(x * ones)


def early_compute(e, consts, ts, xs, xc, ys, vl, lvp, sums):
    lanes = consts[11]
    for i in range(12):
        row = vnir_row(e, 1, i)
        xs[i + 8] = row
        xc[i + 2] = gram_cols(lanes, row)
    acc = [jnp.zeros((8, 128), F32) for _ in range(10)]
    for i in OWN:
        ys[i] = gram_row(xc, i, OWN, 1.0)
    for i in OWN:
        add_products(acc, xs, ys, ts, lanes[9:10, :], i)
    for k in range(10):
        sums[k] = acc[k]
    means = {i: mean_row(xs, i + 6) for i in EARLY}
    for i in EARLY:
        vl[i] = col_filter(means[i], MEAN_TAPS)[:, 0:384]
    for i in range(12):
        lvp[i] = total_of([float(G3[k - i + 6]) * means[k] for k in EARLY if abs(k - i) <= 6])


def front_compute(e, consts, sums_ref, r, c, ts, dd, xs, xc, ys, lvs, vl, lvp, swu, dl, rl):
    third_hi, third_lo, lanes = consts[9:12]
    for k in range(28):
        if k < 8:
            xs[k] = vnir_row(e, 0, k + 4)
        elif k >= 20:
            xs[k] = vnir_row(e, 2, k - 20)
    up_keep = jnp.where(r == 0, 0.0, 1.0)
    down_keep = jnp.where(r == STRIPS - 1, 0.0, 1.0)
    mask = column_mask(c)
    means = {}
    for i in range(-6, 18):
        if i not in EARLY:
            row = mean_row(xs, i + 6)
            means[i] = row * up_keep if i < 0 else (row * down_keep if i >= 12 else row)
    for i in range(12):
        total = lvp[i] + total_of(
            [float(G3[k - i + 6]) * means[k] for k in means if abs(k - i) <= 6]
        )
        lowered = col_filter(total, MEAN_TAPS) * mask
        lowered = col_filter(lowered, G3)[:, 0:384]
        lvs[i] = lowered
        if i in EARLY:
            vl[i] = vl[i] - lowered
        else:
            vl[i] = col_filter(means[i], MEAN_TAPS)[:, 0:384] - lowered
    for i in RIM:
        xc[i] = gram_cols(lanes, xs[i + 6])
    acc = [sums_ref[k] for k in range(10)]
    for i in RIM:
        ys[i] = gram_row(xc, i, OWN, 2.0) + gram_row(xc, i, RIM, 1.0)
        add_products(acc, xs, ys, ts, lanes[9:10, :], i)
    sums = {k: acc[k] for k in range(10)}
    sums[10] = sums_ref[10]
    dcol = total_of([float(G3[t]) * dd[t + 2 : t + 14, :] for t in range(13)]) * mask
    low_d = col_filter(dcol, G3)[:, 0:384]
    dl[...] = dd[8:20, 0:384] - low_d
    ts[0:12, 0:384] = low_d
    srow = [
        swir_row(e, *at)
        for at in ((0, 2), (0, 3), (1, 0), (1, 1), (1, 2), (1, 3), (2, 0), (2, 1))
    ]
    up = []
    for m in range(4):
        for p in range(3):
            total = None
            for t in range(5):
                if C3[t, p] != 0.0:
                    term = float(C3[t, p]) * srow[m + t]
                    total = term if total is None else total + term
            up.append(total)
    swu[...] = dot3(jnp.concatenate(up, axis=0), third_hi[...], third_lo[...])
    acc = [jnp.zeros((8, 128), F32) for _ in range(22)]
    for i in range(12):
        lv = lvs[i]
        sw = swu[8 * i : 8 * i + 8, :]
        ld = ts[i : i + 1, 0:384]
        for j in range(8):
            other = lvs[i, j : j + 1, :]
            acc[j] = acc[j] + fold(lv * other)
            acc[8 + j] = acc[8 + j] + fold(sw * other)
        acc[16] = acc[16] + fold(lv * ld)
        acc[17] = acc[17] + fold(sw * ld)
        acc[18] = acc[18] + fold(lv)
        acc[19] = acc[19] + fold(sw)
        acc[20] = acc[20] + fold(ld)
        acc[21] = acc[21] + fold(ld * ld)
    for k in range(22):
        sums[16 + k] = acc[k]
    at = lane((8, 128))
    packed = jnp.zeros((8, 128), F32)
    for k, value in sums.items():
        packed = jnp.where(at == k, jnp.sum(value, axis=1, keepdims=True), packed)
    rl[...] = packed


def upsample(xs, consts, zs, up_out):
    fine_hi, fine_lo = consts[7:9]
    for m in range(12):
        for p in range(4):
            total = None
            for t in range(5):
                if C4[t, p] != 0.0:
                    term = float(C4[t, p]) * xs[m + t + 6]
                    total = term if total is None else total + term
            for tile in range(4):
                zs[tile, pl.ds(4 * m + p, 8, stride=48), :] = total[
                    :, 128 * tile : 128 * tile + 128
                ]

    @pl.loop(0, BANDS)
    def _(b):
        at = pl.ds(pl.multiple_of(b * 48, 48), 48)
        z = [zs[k, at, :] for k in range(4)]
        lhs = jnp.concatenate(
            [
                jnp.concatenate([z[k], edge(z[k + 1], z[(k + 3) % 4])], axis=1)
                for k in range(3)
            ],
            axis=0,
        )
        up = dot3(lhs, fine_hi[...], fine_lo[...])
        for k in range(3):
            up_out[at, 512 * k : 512 * k + 512] = up[48 * k : 48 * k + 48]


def front_kernel(pan, vnir, swir, *rest):
    hbm_consts = rest[:NUM_CONST]
    rt, up_out, d_out, vl, swu, dl = rest[NUM_CONST : NUM_CONST + 6]
    rest = rest[NUM_CONST + 6 :]
    consts = rest[:NUM_CONST]
    (vs, ss, sb, e, pe, xs, xc, ys, ts, dd, lvs, zs, sums, rl, g1, mid, g2, lvp, down, dup, ddn) = rest[
        NUM_CONST : NUM_CONST + 21
    ]
    (csem, lsem, ssem, rsem, fsem, hsem, psem, qsem, g1s, g1r, g2s, g2r) = rest[NUM_CONST + 21 :]
    r = lax.axis_index("rows")
    c = lax.axis_index("band")

    def remote(src, dst, send, recv, row, block):
        return pltpu.make_async_remote_copy(
            src_ref=src, dst_ref=dst, send_sem=send, recv_sem=recv,
            device_id=(row, block), device_id_type=MESH,
        )

    rl8 = lax.rem(r, 8)
    base = r - rl8
    barrier = pltpu.get_barrier_semaphore()

    def greet(row, block):
        pl.semaphore_signal(barrier, inc=1, device_id=(row, block), device_id_type=MESH)

    core = lax.rem(rl8, 2)
    x = lax.div(rl8, 2)
    y_hi, z = lax.div(c, 4), lax.rem(c, 4)
    y_lo = lax.div(r, 8)
    y = 2 * y_hi + y_lo

    def step_one(dx, dcore):
        return 2 * lax.rem(x + dx, 4) + lax.rem(core + dcore, 2)

    def step_two(dy, dz):
        return 4 * lax.rem(y + dy, 4) + lax.rem(z + dz, 4)

    def place_two(slot):
        y2 = lax.div(slot, 4)
        return 8 * lax.rem(y2, 2) + rl8, 4 * lax.div(y2, 2) + lax.rem(slot, 4)

    near = lambda d: min(d, 4 - d)
    ones = sorted(
        [(dx, dc) for dx in range(4) for dc in range(2) if dx or dc], key=lambda d: (-near(d[0]), -d[1])
    )
    twos = sorted(
        [(dy, dz) for dy in range(4) for dz in range(4) if dy or dz],
        key=lambda d: (-near(d[0]) - near(d[1]), d),
    )
    first = [(base + step_one(*d), c) for d in ones]
    second = [place_two(step_two(*d)) for d in twos]
    strips = ((1, r < STRIPS - 1), (-1, r > 0))
    beside = [(r + dr, c, ok) for dr, ok in strips]
    greetings = len(second) + len(first)
    for row, block in second:
        greet(row, block)
    for row, block, ok in beside:
        pl.when(ok)(functools.partial(greet, row, block))
        greetings = greetings + jnp.where(ok, 1, 0)
    for row, block in first:
        greet(row, block)

    loads = [
        pltpu.make_async_copy(vnir, vs.at[pl.ds(0, 288)], lsem.at[0]),
        pltpu.make_async_copy(swir.at[0], ss, lsem.at[1]),
        pltpu.make_async_copy(pan, pe.at[pl.ds(8, 48), pl.ds(0, 1536)], lsem.at[2]),
    ]
    for copy in loads:
        copy.start()
    const_loads = [
        pltpu.make_async_copy(hbm_consts[k], consts[k], csem.at[k]) for k in range(NUM_CONST)
    ]

    @pl.when(r == 0)
    def _():
        pe[0:8, :] = jnp.zeros((8, 1792), F32)
        e[0, 3:7] = jnp.zeros((4, 64, 128), F32)
        dup[...] = jnp.zeros((8, 512), F32)

    @pl.when(r == STRIPS - 1)
    def _():
        pe[56:64, :] = jnp.zeros((8, 1792), F32)
        e[2, 0:4] = jnp.zeros((4, 64, 128), F32)
        ddn[...] = jnp.zeros((8, 512), F32)

    @pl.when(c == 0)
    def _():
        pe[8:56, 1536:1664] = jnp.zeros((48, 128), F32)

    @pl.when(c == BLOCKS - 1)
    def _():
        pe[8:56, 1664:1792] = jnp.zeros((48, 128), F32)

    loads[0].wait()
    loads[1].wait()
    pack(vs, ss, sb)
    loads[2].wait()
    pl.semaphore_wait(barrier, greetings)

    def pan_cols(side):
        src = pe.at[pl.ds(8, 48), pl.ds(1408, 128)] if side == 0 else pan_first
        dst = pe.at[pl.ds(8, 48), pl.ds(1536 + 128 * side, 128)]
        block = c + 1 if side == 0 else c - 1
        return remote(src, dst, psem.at[side], qsem.at[side], r, block)

    pan_first = pe.at[pl.ds(8, 48), pl.ds(0, 128)]

    def pan_part(side, cols, n):
        src = pe.at[pl.ds(48, 8), cols] if side == 0 else pe.at[pl.ds(8, 8), cols]
        dst = pe.at[pl.ds(0, 8), cols] if side == 0 else pe.at[pl.ds(56, 8), cols]
        row = r + 1 if side == 0 else r - 1
        return remote(src, dst, psem.at[n + side], qsem.at[n + side], row, c)

    def pan_rows(side):
        return pan_part(side, pl.ds(0, 1536), 2)

    def pan_corner(side):
        return pan_part(side, pl.ds(1536, 256), 4)

    def mean_rows(side):
        src, dst = (down, dup) if side == 0 else (dd.at[pl.ds(8, 8)], ddn)
        row = r + 1 if side == 0 else r - 1
        return remote(src, dst, psem.at[6 + side], qsem.at[6 + side], row, c)

    has_below, has_above = r < STRIPS - 1, r > 0
    has_right, has_left = c < BLOCKS - 1, c > 0

    def when(cond, action):
        @pl.when(cond)
        def _():
            action()

    when(has_right, lambda: pan_cols(0).start())
    when(has_left, lambda: pan_cols(1).start())

    def band_rows(b):
        return pl.ds(pl.multiple_of(b * 8, 8), 8)

    turns = [(0, 0), (1, 2), (1, 1), (1, 3), (1, 0), (0, 2), (0, 1), (0, 3)]

    def band_at(dyh, dz):
        return 4 * lax.rem(y_hi + dyh, 2) + lax.rem(z + dz, 4)

    def block_send(k):
        block = band_at(*turns[k])
        return remote(sb.at[block], e.at[1, pl.ds(0, TILES), band_rows(c)], ssem.at[k], rsem.at[k], r, block)

    def block_recv(k):
        b = band_at(turns[k][0], 4 - turns[k][1])
        return remote(sb.at[0], e.at[1, pl.ds(0, TILES), band_rows(b)], ssem.at[k], rsem.at[k], r, c)

    def forward(k, side):
        b = band_at(turns[k][0], 4 - turns[k][1])
        part = pl.ds(3 - 3 * side, 4)
        dst = e.at[2 * side, part, band_rows(b)]
        src = sb.at[c, part] if k == 0 else e.at[1, part, band_rows(b)]
        row = r + 1 if side == 0 else r - 1
        return remote(src, dst, fsem.at[side, k], hsem.at[side, k], row, c)

    for k in range(1, 8):
        block_send(k).start()
    own = pltpu.make_async_copy(sb.at[c], e.at[1, pl.ds(0, TILES), band_rows(c)], lsem.at[3])
    own.start()
    when(has_below, lambda: forward(0, 0).start())
    when(has_above, lambda: forward(0, 1).start())
    when(has_below, lambda: pan_rows(0).start())
    when(has_above, lambda: pan_rows(1).start())

    for copy in const_loads:
        copy.start()

    when(has_left, lambda: pan_cols(0).wait_recv())
    when(has_right, lambda: pan_cols(1).wait_recv())
    when(has_below, lambda: pan_corner(0).start())
    when(has_above, lambda: pan_corner(1).start())
    for k in range(7, 0, -1):
        block_recv(k).wait_recv()
        when(has_below, functools.partial(lambda k: forward(k, 0).start(), k))
        when(has_above, functools.partial(lambda k: forward(k, 1).start(), k))
    own.wait()
    for copy in const_loads:
        copy.wait()
    when(has_above, lambda: (pan_rows(0).wait_recv(), pan_corner(0).wait_recv()))
    when(has_below, lambda: (pan_rows(1).wait_recv(), pan_corner(1).wait_recv()))
    mean_stage(pe, consts, dd, down)
    when(has_below, lambda: mean_rows(0).start())
    when(has_above, lambda: mean_rows(1).start())
    sums[10] = pan_stage(pe, consts, d_out, ts)
    early_compute(e, consts, ts, xs, xc, ys, vl, lvp, sums)
    for k in range(8):
        when(has_above, functools.partial(lambda k: forward(k, 0).wait_recv(), k))
        when(has_below, functools.partial(lambda k: forward(k, 1).wait_recv(), k))

    when(has_above, lambda: mean_rows(0).wait_recv())
    when(has_below, lambda: mean_rows(1).wait_recv())
    dd[0:8] = dup[...]
    dd[20:28] = ddn[...]
    front_compute(e, consts, sums, r, c, ts, dd, xs, xc, ys, lvs, vl, lvp, swu, dl, rl)

    me_two = 4 * y + z

    def sum_one(n):
        row, block = first[n]
        return remote(rl, g1.at[rl8], g1s.at[n], g1r.at[n], row, block)

    def sum_one_recv(n):
        dx, dc = ones[n]
        return remote(rl, g1.at[step_one(4 - dx, 2 - dc)], g1s.at[n], g1r.at[n], r, c)

    def sum_two(n):
        row, block = second[n]
        return remote(mid, g2.at[me_two], g2s.at[n], g2r.at[n], row, block)

    def sum_two_recv(n):
        dy, dz = twos[n]
        return remote(mid, g2.at[step_two(4 - dy, 4 - dz)], g2s.at[n], g2r.at[n], r, c)

    for n in range(7):
        sum_one(n).start()
    g1[rl8] = rl[...]
    for n in range(7):
        sum_one_recv(n).wait_recv()
    total = g1[0]
    for k in range(1, 8):
        total = total + g1[k]
    mid[...] = total
    for n in range(15):
        sum_two(n).start()
    g2[me_two] = total
    upsample(xs, consts, zs, up_out)
    for n in range(15):
        sum_two_recv(n).wait_recv()
    total = g2[0]
    for k in range(1, 16):
        total = total + g2[k]
    rt[...] = total

    when(has_below, lambda: mean_rows(0).wait_send())
    when(has_above, lambda: mean_rows(1).wait_send())
    for k in range(1, 8):
        block_send(k).wait_send()
        sum_one(k - 1).wait_send()
    for n in range(15):
        sum_two(n).wait_send()
    when(has_right, lambda: pan_cols(0).wait_send())
    when(has_left, lambda: pan_cols(1).wait_send())
    for side, cond in ((0, has_below), (1, has_above)):
        when(cond, functools.partial(lambda side: (pan_rows(side).wait_send(), pan_corner(side).wait_send()), side))
        for k in range(8):
            when(cond, functools.partial(lambda k, side: forward(k, side).wait_send(), k, side))


def front(pan, vnir, swir):
    return pl.pallas_call(
        front_kernel,
        name="front",
        out_shape=[
            VM((8, 128), F32),
            VM((384, 1536), F32),
            VM((48, 1536), F32),
            VM((12, 8, 384), F32),
            VM((96, 384), F32),
            VM((12, 384), F32),
        ],
        in_specs=[pl.BlockSpec(memory_space=pl.ANY)] * (3 + NUM_CONST),
        out_specs=[pl.BlockSpec(memory_space=VM)] * 6,
        scratch_shapes=[VM(k.shape, BF16 if k.dtype == ml_dtypes.bfloat16 else F32) for k in CONSTANTS]
        + [
            VM((384, 128), F32),
            VM((4, 1024), F32),
            VM((8, TILES, 8, 128), F32),
            VM((3, TILES, 64, 128), F32),
            VM((64, 1792), F32),
            VM((28, 8, 512), F32),
            VM((16, 8, 512), F32),
            VM((16, 8, 512), F32),
            VM((16, 512), F32),
            VM((32, 512), F32),
            VM((12, 8, 384), F32),
            VM((4, 384, 128), F32),
            VM((11, 8, 128), F32),
            VM((8, 128), F32),
            VM((8, 8, 128), F32),
            VM((8, 128), F32),
            VM((16, 8, 128), F32),
            VM((12, 8, 512), F32),
            VM((8, 512), F32),
            VM((8, 512), F32),
            VM((8, 512), F32),
            pltpu.SemaphoreType.DMA((NUM_CONST,)),
            pltpu.SemaphoreType.DMA((4,)),
            pltpu.SemaphoreType.DMA((8,)),
            pltpu.SemaphoreType.DMA((8,)),
            pltpu.SemaphoreType.DMA((2, 8)),
            pltpu.SemaphoreType.DMA((2, 8)),
            pltpu.SemaphoreType.DMA((8,)),
            pltpu.SemaphoreType.DMA((8,)),
            pltpu.SemaphoreType.DMA((8,)),
            pltpu.SemaphoreType.DMA((8,)),
            pltpu.SemaphoreType.DMA((16,)),
            pltpu.SemaphoreType.DMA((16,)),
        ],
        compiler_params=pltpu.CompilerParams(
            collective_id=0, has_side_effects=True, vmem_limit_bytes=56 << 20
        ),
    )(pan, vnir, swir, *[jnp.asarray(k) for k in CONSTANTS])


def solve_spd(a, b):
    a = [list(row) for row in a]
    inverse = []
    factor = [[None] * 8 for _ in range(8)]
    for j in range(8):
        inv = 1.0 / a[j][j]
        inverse.append(inv)
        for i in range(j + 1, 8):
            factor[i][j] = a[i][j] * inv
        for i in range(j + 1, 8):
            for k in range(j + 1, i + 1):
                a[i][k] = a[i][k] - factor[i][j] * a[k][j]
    z = list(b)
    for j in range(8):
        for i in range(j + 1, 8):
            z[i] = z[i] - factor[i][j] * z[j]
    z = [z[j] * inverse[j] for j in range(8)]
    for j in range(7, -1, -1):
        for i in range(j):
            z[i] = z[i] - factor[j][i] * z[j]
    return z


def solve_first(rt, cb):
    for k in range(11):
        cb[k] = jnp.broadcast_to(rt[:, k : k + 1], (8, 128))
    mean = [cb[9, i : i + 1, :] * (1.0 / N1) for i in range(8)]
    mean_p = jnp.sum(cb[10], axis=0, keepdims=True) * (1.0 / N1)
    a = [
        [
            (cb[j, i : i + 1, :] + cb[i, j : j + 1, :]) * (0.5 / N1) - mean[i] * mean[j]
            for j in range(i + 1)
        ]
        for i in range(8)
    ]
    b = [cb[8, i : i + 1, :] * (1.0 / N1) - mean[i] * mean_p for i in range(8)]
    w = solve_spd(a, b)
    scale = 1.0 / total_of([b[i] * w[i] for i in range(8)])
    return [b[i] * scale for i in range(8)]


def solve_second(rt, cb, gain):
    for k in range(16, 38):
        cb[k] = jnp.broadcast_to(rt[:, k : k + 1], (8, 128))

    def at(k, i):
        return cb[k, i : i + 1, :]

    sum_d = at(36, 0)
    sum_dd = at(37, 0)
    q = [at(32, i) for i in range(8)]
    mean2 = [(at(34, i) + gain[i] * sum_d) * (1.0 / N2) for i in range(8)]
    a2 = [
        [
            (at(16 + j, i) + gain[i] * q[j] + gain[j] * q[i] + gain[i] * gain[j] * sum_dd) * (1.0 / N2)
            - mean2[i] * mean2[j]
            for j in range(i + 1)
        ]
        for i in range(8)
    ]
    swir_mean = cb[35] * (1.0 / N2)
    cross = [
        (cb[24 + i] + gain[i] * cb[33]) * (1.0 / N2) - mean2[i] * swir_mean for i in range(8)
    ]
    y = [jnp.sum(cross[i], axis=0, keepdims=True) * 0.125 for i in range(8)]
    v = solve_spd(a2, y)
    share = total_of([v[i] * cross[i] for i in range(8)]) / total_of([v[i] * y[i] for i in range(8)])
    return v, share


def wide(x, copies):
    return jnp.concatenate([x] * copies, axis=1)


def back_kernel(rt, up, d, vl, swu, dl, joined, joined_swir, cb, gs, out, sem):
    gain = solve_first(rt, cb)
    for b in range(8):
        gs[b] = jnp.broadcast_to(gain[b], (8, 128))

    @pl.loop(0, BANDS)
    def _(b):
        g = wide(gs[b], 2)
        rows = pl.multiple_of(b * 48, 48)
        for i in range(6):
            for t in range(6):
                at = slice(256 * t, 256 * t + 256)
                out[b, 8 * i : 8 * i + 8, at] = (
                    up[pl.ds(rows + 8 * i, 8), at] + g * d[8 * i : 8 * i + 8, at]
                )
        pltpu.make_async_copy(out.at[b], joined.at[b], sem.at[b]).start()

    gain = [gs[b, 0:1, :] for b in range(8)]
    v, share = solve_second(rt, cb, gain)
    row8 = lax.broadcasted_iota(jnp.int32, (8, 128), 0)
    v8 = jnp.zeros((8, 128), F32)
    for b in range(8):
        v8 = jnp.where(row8 == b, jnp.broadcast_to(v[b], (8, 128)), v8)
    v8 = wide(v8, 3)
    vg = wide(total_of([v[b] * gain[b] for b in range(8)]), 3)
    share3 = wide(share, 3)
    for i in range(12):
        detail = jnp.sum(v8 * vl[i], axis=0, keepdims=True) + vg * dl[i : i + 1, :]
        joined_swir[i] = swu[8 * i : 8 * i + 8, :] + share3 * detail

    @pl.loop(0, BANDS)
    def _(b):
        pltpu.make_async_copy(out.at[b], joined.at[b], sem.at[b]).wait()


def back(rt, up, d, vl, swu, dl):
    return pl.pallas_call(
        back_kernel,
        name="back",
        out_shape=[
            jax.ShapeDtypeStruct((8, 48, 1536), F32),
            jax.ShapeDtypeStruct((12, 8, 384), F32),
        ],
        in_specs=[pl.BlockSpec(memory_space=VM)] * 6,
        out_specs=[pl.BlockSpec(memory_space=pl.ANY), pl.BlockSpec(memory_space=VM)],
        scratch_shapes=[
            VM((38, 8, 128), F32),
            VM((8, 8, 128), F32),
            VM((8, 48, 1536), F32),
            pltpu.SemaphoreType.DMA((8,)),
        ],
        compiler_params=pltpu.CompilerParams(vmem_limit_bytes=32 << 20),
    )(rt, up, d, vl, swu, dl)


def local(pan, vnir, swir):
    joined, rows = back(*front(pan, vnir.reshape(288, 128), swir))
    return joined, jnp.swapaxes(rows, 0, 1)


def solution(mesh):
    return jax.shard_map(
        local,
        mesh=mesh,
        in_specs=(P("rows", "band"), P("band", "rows", None), P("band", "rows", None)),
        out_specs=(P(None, "rows", "band"), P(None, "rows", "band")),
        check_vma=False,
    )
```

```python
import functools
import math

import jax
import jax.numpy as jnp
import ml_dtypes
import numpy as np
from jax import lax
from jax.experimental import pallas as pl
from jax.experimental.pallas import tpu as pltpu
from jax.sharding import PartitionSpec as P

F32 = jnp.float32
BF16 = jnp.bfloat16
MESH = pl.DeviceIdType.MESH
VM = pltpu.VMEM

BANDS = 8
STRIPS = 16
BLOCKS = 8
HEIGHT = 768
WIDTH = 12288
N1 = float(HEIGHT * WIDTH)
N2 = float(HEIGHT * WIDTH // 16)
NYQUIST_GAIN = 0.29


def gauss_taps(upscale, kernel_len):
    spread = upscale * math.sqrt(-2.0 * math.log(NYQUIST_GAIN)) / math.pi
    radius = kernel_len // 2
    offsets = np.arange(-radius, radius + 1) * 1.0
    values = np.exp(-(offsets**2) / (2.0 * spread**2))
    return values / values.sum()


def cubic_weight(distance):
    distance = abs(distance)
    if distance <= 1.0:
        return 1.5 * distance**3 - 2.5 * distance**2 + 1.0
    if distance < 2.0:
        return -0.5 * distance**3 + 2.5 * distance**2 - 4.0 * distance + 2.0
    return 0.0


def cubic_table(upscale):
    weights = np.zeros((5, upscale))
    for phase_index in range(upscale):
        centre = (phase_index + 0.5) / upscale - 0.5
        first_tap = math.floor(centre)
        fraction = centre - first_tap
        for tap_index in range(-1, 3):
            weights[first_tap + tap_index + 2, phase_index] += cubic_weight(tap_index - fraction)
    return weights


C4 = cubic_table(4)
C3 = cubic_table(3)
G4 = gauss_taps(4, 17)
G3 = gauss_taps(3, 13)
MEAN_TAPS = C4.mean(axis=1)


def split(matrix):
    high = matrix.astype(np.float32).astype(ml_dtypes.bfloat16)
    low = (matrix - high.astype(np.float64)).astype(ml_dtypes.bfloat16)
    return high, low


def tables():
    up_rows = np.zeros((48, 16))
    for m in range(12):
        for p in range(4):
            for t in range(5):
                up_rows[4 * m + p, m + t] += C4[t, p]
    up_cols = np.zeros((1536, 512))
    for m in range(384):
        for p in range(4):
            for t in range(5):
                up_cols[4 * m + p, (m + t - 2) % 512] += C4[t, p]
    gram_rows = up_rows.T @ up_rows
    gram_cols = up_cols.T @ up_cols
    lanes = np.zeros((16, 512), np.float32)
    at = np.arange(512)
    for t in range(-4, 5):
        lanes[t + 4] = gram_cols[at, (at + t) % 512]
    lanes[9] = up_cols.sum(axis=0)
    row_sum = up_rows.sum(axis=0)

    low = np.zeros((48, 64))
    mean = np.zeros((16, 64))
    for f in range(48):
        low[f, f : f + 17] = G4
    for i in range(12):
        mean[i, 8 + 4 * i : 12 + 4 * i] = 0.25
    mean_low = np.zeros((16, 64))
    mean_low[:12] = low.reshape(12, 4, 64).mean(axis=1)
    rows_hi, rows_lo = split(np.concatenate([low, up_rows.T @ low, mean_low, mean]))

    low_cols = np.zeros((256, 128))
    for o in range(128):
        for t in range(-8, 9):
            q = o + t
            row = q if 0 <= q < 128 else (q if q >= 128 else 256 + q)
            low_cols[row, o] = G4[t + 8]
    mean_cols = np.zeros((640, 128))
    for f in range(512):
        mean_cols[f, f // 4] = 0.25
    for f in range(32):
        mean_cols[512 + f, f // 4] = 0.25
        mean_cols[512 + 96 + f, 120 + f // 4] = 0.25
    back_cols = np.zeros((640, 128))
    for n in range(128):
        for t in range(5):
            for p in range(4):
                f = 4 * (n - (t - 2)) + p
                row = f if f >= 0 else 640 + f
                back_cols[row, n] += C4[t, p]
    fine = np.zeros((256, 512))
    for m in range(128):
        for p in range(4):
            for t in range(5):
                fine[(m + t - 2) % 256, 4 * m + p] += C4[t, p]
    third = np.zeros((256, 384))
    for m in range(128):
        for p in range(3):
            for t in range(5):
                third[(m + t - 2) % 256, 3 * m + p] += C3[t, p]
    both = np.convolve(MEAN_TAPS, G3)
    joint = np.zeros((256, 128))
    for o in range(128):
        for t in range(-8, 9):
            joint[(o + t) % 256, o] = both[t + 8]
    for o in range(6):
        for k in (-1, -2):
            if o - k <= 6:
                for source in range(k + 3):
                    joint[128 + 16 + source, o] -= G3[6 + o - k] * MEAN_TAPS[2 + source - k]
        joint[128 + 111, 127 - o] = joint[128 + 16, o]
        joint[128 + 110, 127 - o] = joint[128 + 17, o]
    constants = (
        rows_hi,
        rows_lo,
        *split(low_cols),
        mean_cols.astype(ml_dtypes.bfloat16),
        *split(back_cols),
        *split(fine),
        *split(third),
        *split(joint),
        lanes,
    )
    return constants, gram_rows, row_sum, up_rows


CONSTANTS, GRAM_ROWS, ROW_SUM, UP_ROWS = tables()
NUM_CONST = len(CONSTANTS)


def halves(x):
    high = x.astype(BF16)
    return high, (x - high.astype(F32)).astype(BF16)


def mm(a, b):
    return jnp.dot(a, b, preferred_element_type=F32)


def dot3(x, high, low):
    xh, xl = halves(x)
    return mm(xh, high) + mm(xl, high) + mm(xh, low)


def dot2(x, exact):
    xh, xl = halves(x)
    return mm(xh, exact) + mm(xl, exact)


def lane(shape):
    return lax.broadcasted_iota(jnp.int32, shape, len(shape) - 1)


def edge(next_tile, prev_tile):
    return jnp.where(lane(next_tile.shape) < 64, next_tile, prev_tile)


def shifted(x, t):
    n = x.shape[1]
    return x if t == 0 else pltpu.roll(x, (-t) % n, 1)


def col_filter(x, taps):
    radius = len(taps) // 2
    total = float(taps[radius]) * x
    for t in range(1, radius + 1):
        total = total + float(taps[radius + t]) * (shifted(x, t) + shifted(x, -t))
    return total


TILES = 7


def pick(e, strip, row, tile):
    return e[strip, tile, pl.ds(row, 8, stride=8), :]


def vnir_row(e, strip, i):
    first, at = (0, i) if strip == 2 or (strip == 1 and i < 8) else (4, i - 4)
    halo = pick(e, strip, i, 3) if i < 8 else pltpu.roll(pick(e, strip, i - 8, 3), 64, 1)
    return jnp.concatenate([pick(e, strip, at, first + t) for t in range(3)] + [halo], axis=1)


def swir_row(e, strip, j):
    at = lane((8, 128))
    base = 16 if j < 2 else 80
    row = None
    for k in range(4):
        part = pltpu.roll(pick(e, strip, 4 * (j % 2) + k, 3), (32 * k - base) % 128, 1)
        row = part if row is None else jnp.where(at >= 32 * k, part, row)
    return jnp.concatenate([row, pltpu.roll(pick(e, strip, 4 + j, 3), 64, 1)], axis=1)


def total_of(values):
    total = values[0]
    for value in values[1:]:
        total = total + value
    return total


def fold(x):
    total = x[:, 0:128]
    for t in range(1, x.shape[1] // 128):
        total = total + x[:, 128 * t : 128 * t + 128]
    return total


def pack(vs, ss, sb):
    at = lane((8, 128))
    zero = jnp.zeros((8, 128), F32)

    def coarse(first, tile):
        return vs[pl.ds(24 * first + tile, 8, stride=24), :] if 0 <= tile < 24 else zero

    def short(tile):
        return ss[0:4, 128 * tile : 128 * tile + 128] if 0 <= tile < 8 else zero[0:4]

    sub = lax.broadcasted_iota(jnp.int32, (8, 128), 0)
    for d in range(BLOCKS):
        for t in range(3):
            sb[d, t] = coarse(0, 3 * d + t)
            sb[d, 4 + t] = coarse(4, 3 * d + t)
        sb[d, 3, 0:4] = edge(coarse(8, 3 * d + 3), coarse(8, 3 * d - 1))[0:4]
        sb[d, 3, 4:8] = edge(short(d + 1), short(d - 1))
        other = pltpu.roll(sb[d, 3], 64, 1)
        own = edge(coarse(0, 3 * d + 3), coarse(0, 3 * d - 1))
        tile = jnp.where((at >= 56) & (at < 72), other, own)
        for j in (0, 2):
            base = 16 + 32 * j
            rows = jnp.where(
                sub < 4,
                ss[j : j + 1, 128 * d : 128 * d + 128],
                ss[j + 1 : j + 2, 128 * d : 128 * d + 128],
            )
            quarters = None
            for k in range(4):
                part = pltpu.roll(rows, (base - 32 * k) % 128, 1)
                quarters = part if quarters is None else jnp.where(lax.rem(sub, 4) == k, part, quarters)
            tile = jnp.where((at >= base) & (at < base + 32), quarters, tile)
        sb[d, 3] = tile


def pan_full(pan_ext):
    halo = edge(pan_ext[:, 1664:1792], pan_ext[:, 1536:1664])
    return halves(jnp.concatenate([pan_ext[:, 0:1536], halo], axis=1))


def pan_low_tiles(rows, consts, count):
    tiles = [rows[:count, 128 * j : 128 * j + 128] for j in range(13)]
    lhs = jnp.concatenate(
        [
            jnp.concatenate([tiles[j], edge(tiles[(j + 1) % 13], tiles[(j + 12) % 13])], axis=1)
            for j in range(13)
        ],
        axis=0,
    )
    low = dot3(lhs, consts[2][...], consts[3][...])
    return [low[count * j : count * j + count] for j in range(13)]


def mean_stage(pan_ext, consts, dd, down):
    fh, fl = pan_full(pan_ext)
    rh, rl = consts[0][64:96], consts[1][64:96]
    q = mm(rh, fh) + mm(rh, fl) + mm(rl, fh)
    low_tile = pan_low_tiles(q, consts, 16)
    diff = [q[16:32, 128 * j : 128 * j + 128] - low_tile[j] for j in range(13)]
    lhs = jnp.concatenate(
        [jnp.concatenate(diff[4 * t : 4 * t + 4], axis=1) for t in range(3)], axis=0
    )
    mean_c = consts[4]
    main = dot2(lhs, mean_c[0:512])
    for t in range(3):
        dd[8:24, 128 * t : 128 * t + 128] = main[16 * t : 16 * t + 16]
    dd[8:24, 384:512] = dot2(diff[12], mean_c[512:640])
    down[...] = dd[12:20, :]


def pan_stage(pan_ext, consts, d_out, ts):
    back_hi, back_lo = consts[5:7]
    fh, fl = pan_full(pan_ext)
    rh, rl = consts[0][0:64], consts[1][0:64]
    q = mm(rh, fh) + mm(rh, fl) + mm(rl, fh)
    low_tile = pan_low_tiles(q, consts, 64)
    total = jnp.zeros((8, 128), F32)
    for j in range(12):
        d_out[:, 128 * j : 128 * j + 128] = (
            pan_ext[8:56, 128 * j : 128 * j + 128] - low_tile[j][0:48]
        )
        for k in range(6):
            total = total + low_tile[j][8 * k : 8 * k + 8]
    zero = jnp.zeros((16, 128), F32)
    back = [low_tile[j][48:64] for j in range(12)] + [zero]
    lhs = jnp.concatenate(
        [
            jnp.concatenate(
                back[4 * t : 4 * t + 4] + [edge(back[4 * t + 4], back[(4 * t + 12) % 13])], axis=1
            )
            for t in range(3)
        ],
        axis=0,
    )
    main = dot3(lhs, back_hi[...], back_lo[...])
    rim = dot3(edge(back[0], back[11]), back_hi[512:640], back_lo[512:640])
    for t in range(3):
        ts[:, 128 * t : 128 * t + 128] = main[16 * t : 16 * t + 16]
    ts[:, 384:512] = rim
    return total


def column_mask(block):
    at = lane((1, 512))
    left = jnp.where(block == 0, 0.0, 1.0)
    right = jnp.where(block == BLOCKS - 1, 0.0, 1.0)
    return jnp.where(at >= 448, left, jnp.where(at >= 384, right, 1.0))


def mean_row(xs, i):
    total = None
    for t in range(5):
        term = float(MEAN_TAPS[t]) * xs[i + t]
        total = term if total is None else total + term
    return total


def gram_cols(lanes, x):
    y = lanes[4:5, :] * x
    for t in range(-4, 5):
        if t:
            y = y + lanes[t + 4 : t + 5, :] * shifted(x, t)
    return y


OWN = range(2, 14)
RIM = (0, 1, 14, 15)
EARLY = range(2, 10)


def gram_row(xc, i, among, scale):
    total = None
    for j in among:
        if GRAM_ROWS[i, j] != 0.0:
            term = float(scale * GRAM_ROWS[i, j]) * xc[j]
            total = term if total is None else total + term
    return total


def add_products(acc, xs, ys, ts, ones, i):
    x = xs[i + 6]
    for j in range(8):
        acc[j] = acc[j] + fold(x * ys[i, j : j + 1, :])
    acc[8] = acc[8] + fold(x * ts[i : i + 1, :])
    acc[9] = acc[9] + float(ROW_SUM[i]) * fold(x * ones)


def early_compute(e, consts, ts, xs, xc, ys, vl, lvp, sums):
    lanes = consts[13]
    for i in range(12):
        row = vnir_row(e, 1, i)
        xs[i + 8] = row
        xc[i + 2] = gram_cols(lanes, row)
    acc = [jnp.zeros((8, 128), F32) for _ in range(10)]
    for i in OWN:
        ys[i] = gram_row(xc, i, OWN, 1.0)
    for i in OWN:
        add_products(acc, xs, ys, ts, lanes[9:10, :], i)
    for k in range(10):
        sums[k] = acc[k]
    means = {i: mean_row(xs, i + 6) for i in EARLY}
    for i in EARLY:
        vl[i] = col_filter(means[i], MEAN_TAPS)[:, 0:384]
    for i in range(12):
        lvp[i] = total_of([float(G3[k - i + 6]) * means[k] for k in EARLY if abs(k - i) <= 6])


def front_compute(e, consts, sums_ref, r, c, ts, dd, xs, xc, ys, lvs, vl, lvp, swu, dl, rl):
    third_hi, third_lo, joint_hi, joint_lo, lanes = consts[9:14]
    for k in range(28):
        if k < 8:
            xs[k] = vnir_row(e, 0, k + 4)
        elif k >= 20:
            xs[k] = vnir_row(e, 2, k - 20)
    up_keep = jnp.where(r == 0, 0.0, 1.0)
    down_keep = jnp.where(r == STRIPS - 1, 0.0, 1.0)
    mask = column_mask(c)
    means = {}
    for i in range(-6, 18):
        if i not in EARLY:
            row = mean_row(xs, i + 6)
            means[i] = row * up_keep if i < 0 else (row * down_keep if i >= 12 else row)
    at = lane((8, 128))
    left = (at >= 16) & (at < 18) & (c == 0)
    right = (at >= 110) & (at < 112) & (c == BLOCKS - 1)
    rows = []
    for i in range(12):
        total = lvp[i] + total_of(
            [float(G3[k - i + 6]) * means[k] for k in means if abs(k - i) <= 6]
        )
        rows.append(total)
    lhs = []
    for t in range(3):
        for i in range(12):
            tile = [rows[i][:, 128 * k : 128 * k + 128] for k in range(4)]
            rim = jnp.where(at < 8, tile[t + 1], jnp.where(at >= 120, tile[(t + 3) % 4], 0.0))
            if t == 0:
                rim = jnp.where(left, pltpu.roll(tile[0], 16, 1), rim)
            if t == 2:
                rim = jnp.where(right, pltpu.roll(tile[2], 112, 1), rim)
            lhs.append(jnp.concatenate([tile[t], rim], axis=1))
    lowered = dot3(jnp.concatenate(lhs, axis=0), joint_hi[...], joint_lo[...])
    for i in range(12):
        low = jnp.concatenate([lowered[96 * t + 8 * i : 96 * t + 8 * i + 8] for t in range(3)], axis=1)
        lvs[i] = low
        if i in EARLY:
            vl[i] = vl[i] - low
        else:
            vl[i] = col_filter(means[i], MEAN_TAPS)[:, 0:384] - low
    for i in RIM:
        xc[i] = gram_cols(lanes, xs[i + 6])
    acc = [sums_ref[k] for k in range(10)]
    for i in RIM:
        ys[i] = gram_row(xc, i, OWN, 2.0) + gram_row(xc, i, RIM, 1.0)
        add_products(acc, xs, ys, ts, lanes[9:10, :], i)
    sums = {k: acc[k] for k in range(10)}
    sums[10] = sums_ref[10]
    dcol = total_of([float(G3[t]) * dd[t + 2 : t + 14, :] for t in range(13)]) * mask
    low_d = col_filter(dcol, G3)[:, 0:384]
    dl[...] = dd[8:20, 0:384] - low_d
    ts[0:12, 0:384] = low_d
    srow = [
        swir_row(e, *at)
        for at in ((0, 2), (0, 3), (1, 0), (1, 1), (1, 2), (1, 3), (2, 0), (2, 1))
    ]
    up = []
    for m in range(4):
        for p in range(3):
            total = None
            for t in range(5):
                if C3[t, p] != 0.0:
                    term = float(C3[t, p]) * srow[m + t]
                    total = term if total is None else total + term
            up.append(total)
    swu[...] = dot3(jnp.concatenate(up, axis=0), third_hi[...], third_lo[...])
    acc = [jnp.zeros((8, 128), F32) for _ in range(22)]
    for i in range(12):
        lv = lvs[i]
        sw = swu[8 * i : 8 * i + 8, :]
        ld = ts[i : i + 1, 0:384]
        for j in range(8):
            other = lvs[i, j : j + 1, :]
            acc[j] = acc[j] + fold(lv * other)
            acc[8 + j] = acc[8 + j] + fold(sw * other)
        acc[16] = acc[16] + fold(lv * ld)
        acc[17] = acc[17] + fold(sw * ld)
        acc[18] = acc[18] + fold(lv)
        acc[19] = acc[19] + fold(sw)
        acc[20] = acc[20] + fold(ld)
        acc[21] = acc[21] + fold(ld * ld)
    for k in range(22):
        sums[16 + k] = acc[k]
    at = lane((8, 128))
    packed = jnp.zeros((8, 128), F32)
    for k, value in sums.items():
        packed = jnp.where(at == k, jnp.sum(value, axis=1, keepdims=True), packed)
    rl[...] = packed


def upsample(xs, consts, zs, up_out):
    fine_hi, fine_lo = consts[7:9]
    for m in range(12):
        for p in range(4):
            total = None
            for t in range(5):
                if C4[t, p] != 0.0:
                    term = float(C4[t, p]) * xs[m + t + 6]
                    total = term if total is None else total + term
            for tile in range(4):
                zs[tile, pl.ds(4 * m + p, 8, stride=48), :] = total[
                    :, 128 * tile : 128 * tile + 128
                ]

    @pl.loop(0, BANDS)
    def _(b):
        at = pl.ds(pl.multiple_of(b * 48, 48), 48)
        z = [zs[k, at, :] for k in range(4)]
        lhs = jnp.concatenate(
            [
                jnp.concatenate([z[k], edge(z[k + 1], z[(k + 3) % 4])], axis=1)
                for k in range(3)
            ],
            axis=0,
        )
        up = dot3(lhs, fine_hi[...], fine_lo[...])
        for k in range(3):
            up_out[at, 512 * k : 512 * k + 512] = up[48 * k : 48 * k + 48]


def front_kernel(pan, vnir, swir, *rest):
    hbm_consts = rest[:NUM_CONST]
    rt, up_out, d_out, vl, swu, dl = rest[NUM_CONST : NUM_CONST + 6]
    rest = rest[NUM_CONST + 6 :]
    consts = rest[:NUM_CONST]
    (vs, ss, sb, e, pe, xs, xc, ys, ts, dd, lvs, zs, sums, rl, g1, mid, g2, lvp, down, dup, ddn) = rest[
        NUM_CONST : NUM_CONST + 21
    ]
    (csem, lsem, ssem, rsem, fsem, hsem, psem, qsem, g1s, g1r, g2s, g2r, dsem, tsem) = rest[NUM_CONST + 21 :]
    r = lax.axis_index("rows")
    c = lax.axis_index("band")

    def remote(src, dst, send, recv, row, block):
        return pltpu.make_async_remote_copy(
            src_ref=src, dst_ref=dst, send_sem=send, recv_sem=recv,
            device_id=(row, block), device_id_type=MESH,
        )

    rl8 = lax.rem(r, 8)
    base = r - rl8
    barrier = pltpu.get_barrier_semaphore()

    def greet(row, block):
        pl.semaphore_signal(barrier, inc=1, device_id=(row, block), device_id_type=MESH)

    core = lax.rem(rl8, 2)
    x = lax.div(rl8, 2)
    y_hi, z = lax.div(c, 4), lax.rem(c, 4)
    y_lo = lax.div(r, 8)
    y = 2 * y_hi + y_lo

    def step_one(dx, dcore):
        return 2 * lax.rem(x + dx, 4) + lax.rem(core + dcore, 2)

    def step_two(dy, dz):
        return 4 * lax.rem(y + dy, 4) + lax.rem(z + dz, 4)

    def place_two(slot):
        y2 = lax.div(slot, 4)
        return 8 * lax.rem(y2, 2) + rl8, 4 * lax.div(y2, 2) + lax.rem(slot, 4)

    near = lambda d: min(d, 4 - d)
    ones = sorted(
        [(dx, dc) for dx in range(4) for dc in range(2) if dx or dc], key=lambda d: (-near(d[0]), -d[1])
    )
    twos = sorted(
        [(dy, dz) for dy in range(4) for dz in range(4) if dy or dz],
        key=lambda d: (-near(d[0]) - near(d[1]), d),
    )
    first = [(base + step_one(*d), c) for d in ones]
    second = [place_two(step_two(*d)) for d in twos]
    strips = ((1, r < STRIPS - 1), (-1, r > 0))
    blocks = ((1, c < BLOCKS - 1), (-1, c > 0))
    beside = [(r + dr, c + dc, ok & also) for dr, ok in strips for dc, also in blocks]
    beside += [(r + dr, c, ok) for dr, ok in strips]
    greetings = len(second) + len(first)
    for row, block in second:
        greet(row, block)
    for row, block, ok in beside:
        pl.when(ok)(functools.partial(greet, row, block))
        greetings = greetings + jnp.where(ok, 1, 0)
    for row, block in first:
        greet(row, block)

    loads = [
        pltpu.make_async_copy(vnir, vs.at[pl.ds(0, 288)], lsem.at[0]),
        pltpu.make_async_copy(swir.at[0], ss, lsem.at[1]),
        pltpu.make_async_copy(pan, pe.at[pl.ds(8, 48), pl.ds(0, 1536)], lsem.at[2]),
    ]
    for copy in loads:
        copy.start()
    const_loads = [
        pltpu.make_async_copy(hbm_consts[k], consts[k], csem.at[k]) for k in range(NUM_CONST)
    ]

    @pl.when(r == 0)
    def _():
        pe[0:8, :] = jnp.zeros((8, 1792), F32)
        e[0, 3:7] = jnp.zeros((4, 64, 128), F32)
        dup[...] = jnp.zeros((8, 512), F32)

    @pl.when(r == STRIPS - 1)
    def _():
        pe[56:64, :] = jnp.zeros((8, 1792), F32)
        e[2, 0:4] = jnp.zeros((4, 64, 128), F32)
        ddn[...] = jnp.zeros((8, 512), F32)

    @pl.when(c == 0)
    def _():
        pe[:, 1536:1664] = jnp.zeros((64, 128), F32)

    @pl.when(c == BLOCKS - 1)
    def _():
        pe[:, 1664:1792] = jnp.zeros((64, 128), F32)

    loads[0].wait()
    loads[1].wait()
    pack(vs, ss, sb)
    loads[2].wait()
    pl.semaphore_wait(barrier, greetings)

    def pan_cols(side):
        src = pe.at[pl.ds(8, 48), pl.ds(1408, 128)] if side == 0 else pan_first
        dst = pe.at[pl.ds(8, 48), pl.ds(1536 + 128 * side, 128)]
        block = c + 1 if side == 0 else c - 1
        return remote(src, dst, psem.at[side], qsem.at[side], r, block)

    pan_first = pe.at[pl.ds(8, 48), pl.ds(0, 128)]

    def pan_part(side, cols, n):
        src = pe.at[pl.ds(48, 8), cols] if side == 0 else pe.at[pl.ds(8, 8), cols]
        dst = pe.at[pl.ds(0, 8), cols] if side == 0 else pe.at[pl.ds(56, 8), cols]
        row = r + 1 if side == 0 else r - 1
        return remote(src, dst, psem.at[n + side], qsem.at[n + side], row, c)

    def pan_rows(side):
        return pan_part(side, pl.ds(0, 1536), 2)

    def pan_corner(side, across):
        src = pe.at[
            pl.ds(48 if side == 0 else 8, 8), pl.ds(1408 if across == 0 else 0, 128)
        ]
        dst = pe.at[pl.ds(0 if side == 0 else 56, 8), pl.ds(1536 + 128 * across, 128)]
        row = r + 1 if side == 0 else r - 1
        block = c + 1 if across == 0 else c - 1
        n = 2 * side + across
        return remote(src, dst, dsem.at[n], tsem.at[n], row, block)

    def mean_rows(side):
        src, dst = (down, dup) if side == 0 else (dd.at[pl.ds(8, 8)], ddn)
        row = r + 1 if side == 0 else r - 1
        return remote(src, dst, psem.at[6 + side], qsem.at[6 + side], row, c)

    has_below, has_above = r < STRIPS - 1, r > 0
    has_right, has_left = c < BLOCKS - 1, c > 0
    to = {(s, a): (has_below if s == 0 else has_above) & (has_right if a == 0 else has_left)
          for s in range(2) for a in range(2)}
    into = {(s, a): (has_above if s == 0 else has_below) & (has_left if a == 0 else has_right)
            for s in range(2) for a in range(2)}

    def when(cond, action):
        @pl.when(cond)
        def _():
            action()

    when(has_right, lambda: pan_cols(0).start())
    when(has_left, lambda: pan_cols(1).start())
    for key in to:
        when(to[key], functools.partial(lambda key: pan_corner(*key).start(), key))

    def band_rows(b):
        return pl.ds(pl.multiple_of(b * 8, 8), 8)

    turns = [(0, 0), (1, 2), (1, 1), (1, 3), (1, 0), (0, 2), (0, 1), (0, 3)]

    def band_at(dyh, dz):
        return 4 * lax.rem(y_hi + dyh, 2) + lax.rem(z + dz, 4)

    def block_send(k):
        block = band_at(*turns[k])
        return remote(sb.at[block], e.at[1, pl.ds(0, TILES), band_rows(c)], ssem.at[k], rsem.at[k], r, block)

    def block_recv(k):
        b = band_at(turns[k][0], 4 - turns[k][1])
        return remote(sb.at[0], e.at[1, pl.ds(0, TILES), band_rows(b)], ssem.at[k], rsem.at[k], r, c)

    def forward(k, side):
        b = band_at(turns[k][0], 4 - turns[k][1])
        part = pl.ds(3 - 3 * side, 4)
        dst = e.at[2 * side, part, band_rows(b)]
        src = sb.at[c, part] if k == 0 else e.at[1, part, band_rows(b)]
        row = r + 1 if side == 0 else r - 1
        return remote(src, dst, fsem.at[side, k], hsem.at[side, k], row, c)

    for k in range(1, 8):
        block_send(k).start()
    own = pltpu.make_async_copy(sb.at[c], e.at[1, pl.ds(0, TILES), band_rows(c)], lsem.at[3])
    own.start()
    when(has_below, lambda: forward(0, 0).start())
    when(has_above, lambda: forward(0, 1).start())
    when(has_below, lambda: pan_rows(0).start())
    when(has_above, lambda: pan_rows(1).start())

    for copy in const_loads:
        copy.start()

    for copy in const_loads:
        copy.wait()
    when(has_left, lambda: pan_cols(0).wait_recv())
    when(has_right, lambda: pan_cols(1).wait_recv())
    when(has_above, lambda: pan_rows(0).wait_recv())
    when(has_below, lambda: pan_rows(1).wait_recv())
    for key in into:
        when(into[key], functools.partial(lambda key: pan_corner(*key).wait_recv(), key))
    mean_stage(pe, consts, dd, down)
    when(has_below, lambda: mean_rows(0).start())
    when(has_above, lambda: mean_rows(1).start())
    for k in range(7, 0, -1):
        block_recv(k).wait_recv()
        when(has_below, functools.partial(lambda k: forward(k, 0).start(), k))
        when(has_above, functools.partial(lambda k: forward(k, 1).start(), k))
    own.wait()
    sums[10] = pan_stage(pe, consts, d_out, ts)
    early_compute(e, consts, ts, xs, xc, ys, vl, lvp, sums)
    for k in range(8):
        when(has_above, functools.partial(lambda k: forward(k, 0).wait_recv(), k))
        when(has_below, functools.partial(lambda k: forward(k, 1).wait_recv(), k))

    when(has_above, lambda: mean_rows(0).wait_recv())
    when(has_below, lambda: mean_rows(1).wait_recv())
    dd[0:8] = dup[...]
    dd[20:28] = ddn[...]
    front_compute(e, consts, sums, r, c, ts, dd, xs, xc, ys, lvs, vl, lvp, swu, dl, rl)

    me_two = 4 * y + z

    def sum_one(n):
        row, block = first[n]
        return remote(rl, g1.at[rl8], g1s.at[n], g1r.at[n], row, block)

    def sum_one_recv(n):
        dx, dc = ones[n]
        return remote(rl, g1.at[step_one(4 - dx, 2 - dc)], g1s.at[n], g1r.at[n], r, c)

    def sum_two(n):
        row, block = second[n]
        return remote(mid, g2.at[me_two], g2s.at[n], g2r.at[n], row, block)

    def sum_two_recv(n):
        dy, dz = twos[n]
        return remote(mid, g2.at[step_two(4 - dy, 4 - dz)], g2s.at[n], g2r.at[n], r, c)

    for n in range(7):
        sum_one(n).start()
    g1[rl8] = rl[...]
    for n in range(7):
        sum_one_recv(n).wait_recv()
    total = g1[0]
    for k in range(1, 8):
        total = total + g1[k]
    mid[...] = total
    for n in range(15):
        sum_two(n).start()
    g2[me_two] = total
    upsample(xs, consts, zs, up_out)
    for n in range(15):
        sum_two_recv(n).wait_recv()
    total = g2[0]
    for k in range(1, 16):
        total = total + g2[k]
    rt[...] = total

    for key in to:
        when(to[key], functools.partial(lambda key: pan_corner(*key).wait_send(), key))
    when(has_below, lambda: mean_rows(0).wait_send())
    when(has_above, lambda: mean_rows(1).wait_send())
    for k in range(1, 8):
        block_send(k).wait_send()
        sum_one(k - 1).wait_send()
    for n in range(15):
        sum_two(n).wait_send()
    when(has_right, lambda: pan_cols(0).wait_send())
    when(has_left, lambda: pan_cols(1).wait_send())
    for side, cond in ((0, has_below), (1, has_above)):
        when(cond, functools.partial(lambda side: pan_rows(side).wait_send(), side))
        for k in range(8):
            when(cond, functools.partial(lambda k, side: forward(k, side).wait_send(), k, side))


def front(pan, vnir, swir):
    return pl.pallas_call(
        front_kernel,
        name="front",
        out_shape=[
            VM((8, 128), F32),
            VM((384, 1536), F32),
            VM((48, 1536), F32),
            VM((12, 8, 384), F32),
            VM((96, 384), F32),
            VM((12, 384), F32),
        ],
        in_specs=[pl.BlockSpec(memory_space=pl.ANY)] * (3 + NUM_CONST),
        out_specs=[pl.BlockSpec(memory_space=VM)] * 6,
        scratch_shapes=[VM(k.shape, BF16 if k.dtype == ml_dtypes.bfloat16 else F32) for k in CONSTANTS]
        + [
            VM((384, 128), F32),
            VM((4, 1024), F32),
            VM((8, TILES, 8, 128), F32),
            VM((3, TILES, 64, 128), F32),
            VM((64, 1792), F32),
            VM((28, 8, 512), F32),
            VM((16, 8, 512), F32),
            VM((16, 8, 512), F32),
            VM((16, 512), F32),
            VM((32, 512), F32),
            VM((12, 8, 384), F32),
            VM((4, 384, 128), F32),
            VM((11, 8, 128), F32),
            VM((8, 128), F32),
            VM((8, 8, 128), F32),
            VM((8, 128), F32),
            VM((16, 8, 128), F32),
            VM((12, 8, 512), F32),
            VM((8, 512), F32),
            VM((8, 512), F32),
            VM((8, 512), F32),
            pltpu.SemaphoreType.DMA((NUM_CONST,)),
            pltpu.SemaphoreType.DMA((4,)),
            pltpu.SemaphoreType.DMA((8,)),
            pltpu.SemaphoreType.DMA((8,)),
            pltpu.SemaphoreType.DMA((2, 8)),
            pltpu.SemaphoreType.DMA((2, 8)),
            pltpu.SemaphoreType.DMA((8,)),
            pltpu.SemaphoreType.DMA((8,)),
            pltpu.SemaphoreType.DMA((8,)),
            pltpu.SemaphoreType.DMA((8,)),
            pltpu.SemaphoreType.DMA((16,)),
            pltpu.SemaphoreType.DMA((16,)),
            pltpu.SemaphoreType.DMA((4,)),
            pltpu.SemaphoreType.DMA((4,)),
        ],
        compiler_params=pltpu.CompilerParams(
            collective_id=0, has_side_effects=True, vmem_limit_bytes=56 << 20
        ),
    )(pan, vnir, swir, *[jnp.asarray(k) for k in CONSTANTS])


def solve_spd(a, b):
    a = [list(row) for row in a]
    inverse = []
    factor = [[None] * 8 for _ in range(8)]
    for j in range(8):
        inv = 1.0 / a[j][j]
        inverse.append(inv)
        for i in range(j + 1, 8):
            factor[i][j] = a[i][j] * inv
        for i in range(j + 1, 8):
            for k in range(j + 1, i + 1):
                a[i][k] = a[i][k] - factor[i][j] * a[k][j]
    z = list(b)
    for j in range(8):
        for i in range(j + 1, 8):
            z[i] = z[i] - factor[i][j] * z[j]
    z = [z[j] * inverse[j] for j in range(8)]
    for j in range(7, -1, -1):
        for i in range(j):
            z[i] = z[i] - factor[j][i] * z[j]
    return z


def solve_first(rt, cb):
    for k in range(11):
        cb[k] = jnp.broadcast_to(rt[:, k : k + 1], (8, 128))
    mean = [cb[9, i : i + 1, :] * (1.0 / N1) for i in range(8)]
    mean_p = jnp.sum(cb[10], axis=0, keepdims=True) * (1.0 / N1)
    a = [
        [
            (cb[j, i : i + 1, :] + cb[i, j : j + 1, :]) * (0.5 / N1) - mean[i] * mean[j]
            for j in range(i + 1)
        ]
        for i in range(8)
    ]
    b = [cb[8, i : i + 1, :] * (1.0 / N1) - mean[i] * mean_p for i in range(8)]
    w = solve_spd(a, b)
    scale = 1.0 / total_of([b[i] * w[i] for i in range(8)])
    return [b[i] * scale for i in range(8)]


def solve_second(rt, cb, gain):
    for k in range(16, 38):
        cb[k] = jnp.broadcast_to(rt[:, k : k + 1], (8, 128))

    def at(k, i):
        return cb[k, i : i + 1, :]

    sum_d = at(36, 0)
    sum_dd = at(37, 0)
    q = [at(32, i) for i in range(8)]
    mean2 = [(at(34, i) + gain[i] * sum_d) * (1.0 / N2) for i in range(8)]
    a2 = [
        [
            (at(16 + j, i) + gain[i] * q[j] + gain[j] * q[i] + gain[i] * gain[j] * sum_dd) * (1.0 / N2)
            - mean2[i] * mean2[j]
            for j in range(i + 1)
        ]
        for i in range(8)
    ]
    swir_mean = cb[35] * (1.0 / N2)
    cross = [
        (cb[24 + i] + gain[i] * cb[33]) * (1.0 / N2) - mean2[i] * swir_mean for i in range(8)
    ]
    y = [jnp.sum(cross[i], axis=0, keepdims=True) * 0.125 for i in range(8)]
    v = solve_spd(a2, y)
    share = total_of([v[i] * cross[i] for i in range(8)]) / total_of([v[i] * y[i] for i in range(8)])
    return v, share


def wide(x, copies):
    return jnp.concatenate([x] * copies, axis=1)


def back_kernel(rt, up, d, vl, swu, dl, joined, joined_swir, cb, gs, out, sem):
    gain = solve_first(rt, cb)
    for b in range(8):
        gs[b] = jnp.broadcast_to(gain[b], (8, 128))

    @pl.loop(0, BANDS)
    def _(b):
        g = wide(gs[b], 2)
        rows = pl.multiple_of(b * 48, 48)
        for i in range(6):
            for t in range(6):
                at = slice(256 * t, 256 * t + 256)
                out[b, 8 * i : 8 * i + 8, at] = (
                    up[pl.ds(rows + 8 * i, 8), at] + g * d[8 * i : 8 * i + 8, at]
                )
        pltpu.make_async_copy(out.at[b], joined.at[b], sem.at[b]).start()

    gain = [gs[b, 0:1, :] for b in range(8)]
    v, share = solve_second(rt, cb, gain)
    row8 = lax.broadcasted_iota(jnp.int32, (8, 128), 0)
    v8 = jnp.zeros((8, 128), F32)
    for b in range(8):
        v8 = jnp.where(row8 == b, jnp.broadcast_to(v[b], (8, 128)), v8)
    v8 = wide(v8, 3)
    vg = wide(total_of([v[b] * gain[b] for b in range(8)]), 3)
    share3 = wide(share, 3)
    for i in range(12):
        detail = jnp.sum(v8 * vl[i], axis=0, keepdims=True) + vg * dl[i : i + 1, :]
        joined_swir[i] = swu[8 * i : 8 * i + 8, :] + share3 * detail

    @pl.loop(0, BANDS)
    def _(b):
        pltpu.make_async_copy(out.at[b], joined.at[b], sem.at[b]).wait()


def back(rt, up, d, vl, swu, dl):
    return pl.pallas_call(
        back_kernel,
        name="back",
        out_shape=[
            jax.ShapeDtypeStruct((8, 48, 1536), F32),
            jax.ShapeDtypeStruct((12, 8, 384), F32),
        ],
        in_specs=[pl.BlockSpec(memory_space=VM)] * 6,
        out_specs=[pl.BlockSpec(memory_space=pl.ANY), pl.BlockSpec(memory_space=VM)],
        scratch_shapes=[
            VM((38, 8, 128), F32),
            VM((8, 8, 128), F32),
            VM((8, 48, 1536), F32),
            pltpu.SemaphoreType.DMA((8,)),
        ],
        compiler_params=pltpu.CompilerParams(vmem_limit_bytes=32 << 20),
    )(rt, up, d, vl, swu, dl)


def local(pan, vnir, swir):
    joined, rows = back(*front(pan, vnir.reshape(288, 128), swir))
    return joined, jnp.swapaxes(rows, 0, 1)


def solution(mesh):
    return jax.shard_map(
        local,
        mesh=mesh,
        in_specs=(P("rows", "band"), P("band", "rows", None), P("band", "rows", None)),
        out_specs=(P(None, "rows", "band"), P(None, "rows", "band")),
        check_vma=False,
    )
```

```python
import functools
import math

import jax
import jax.numpy as jnp
import ml_dtypes
import numpy as np
from jax import lax
from jax.experimental import pallas as pl
from jax.experimental.pallas import tpu as pltpu
from jax.sharding import PartitionSpec as P

F32 = jnp.float32
BF16 = jnp.bfloat16
MESH = pl.DeviceIdType.MESH
VM = pltpu.VMEM

BANDS = 8
STRIPS = 16
BLOCKS = 8
HEIGHT = 768
WIDTH = 12288
N1 = float(HEIGHT * WIDTH)
N2 = float(HEIGHT * WIDTH // 16)
NYQUIST_GAIN = 0.29


def gauss_taps(upscale, kernel_len):
    spread = upscale * math.sqrt(-2.0 * math.log(NYQUIST_GAIN)) / math.pi
    radius = kernel_len // 2
    offsets = np.arange(-radius, radius + 1) * 1.0
    values = np.exp(-(offsets**2) / (2.0 * spread**2))
    return values / values.sum()


def cubic_weight(distance):
    distance = abs(distance)
    if distance <= 1.0:
        return 1.5 * distance**3 - 2.5 * distance**2 + 1.0
    if distance < 2.0:
        return -0.5 * distance**3 + 2.5 * distance**2 - 4.0 * distance + 2.0
    return 0.0


def cubic_table(upscale):
    weights = np.zeros((5, upscale))
    for phase_index in range(upscale):
        centre = (phase_index + 0.5) / upscale - 0.5
        first_tap = math.floor(centre)
        fraction = centre - first_tap
        for tap_index in range(-1, 3):
            weights[first_tap + tap_index + 2, phase_index] += cubic_weight(tap_index - fraction)
    return weights


C4 = cubic_table(4)
C3 = cubic_table(3)
G4 = gauss_taps(4, 17)
G3 = gauss_taps(3, 13)
MEAN_TAPS = C4.mean(axis=1)


def split(matrix):
    high = matrix.astype(np.float32).astype(ml_dtypes.bfloat16)
    low = (matrix - high.astype(np.float64)).astype(ml_dtypes.bfloat16)
    return high, low


def tables():
    up_rows = np.zeros((48, 16))
    for m in range(12):
        for p in range(4):
            for t in range(5):
                up_rows[4 * m + p, m + t] += C4[t, p]
    up_cols = np.zeros((1536, 512))
    for m in range(384):
        for p in range(4):
            for t in range(5):
                up_cols[4 * m + p, (m + t - 2) % 512] += C4[t, p]
    gram_rows = up_rows.T @ up_rows
    gram_cols = up_cols.T @ up_cols
    lanes = np.zeros((16, 512), np.float32)
    at = np.arange(512)
    for t in range(-4, 5):
        lanes[t + 4] = gram_cols[at, (at + t) % 512]
    lanes[9] = up_cols.sum(axis=0)
    row_sum = up_rows.sum(axis=0)

    low = np.zeros((48, 64))
    mean = np.zeros((16, 64))
    for f in range(48):
        low[f, f : f + 17] = G4
    for i in range(12):
        mean[i, 8 + 4 * i : 12 + 4 * i] = 0.25
    mean_low = np.zeros((16, 64))
    mean_low[:12] = low.reshape(12, 4, 64).mean(axis=1)
    rows_hi, rows_lo = split(np.concatenate([low, up_rows.T @ low, mean_low, mean]))

    low_cols = np.zeros((256, 128))
    for o in range(128):
        for t in range(-8, 9):
            q = o + t
            row = q if 0 <= q < 128 else (q if q >= 128 else 256 + q)
            low_cols[row, o] = G4[t + 8]
    mean_cols = np.zeros((640, 128))
    for f in range(512):
        mean_cols[f, f // 4] = 0.25
    for f in range(32):
        mean_cols[512 + f, f // 4] = 0.25
        mean_cols[512 + 96 + f, 120 + f // 4] = 0.25
    back_cols = np.zeros((640, 128))
    for n in range(128):
        for t in range(5):
            for p in range(4):
                f = 4 * (n - (t - 2)) + p
                row = f if f >= 0 else 640 + f
                back_cols[row, n] += C4[t, p]
    fine = np.zeros((256, 512))
    for m in range(128):
        for p in range(4):
            for t in range(5):
                fine[(m + t - 2) % 256, 4 * m + p] += C4[t, p]
    third = np.zeros((256, 384))
    for m in range(128):
        for p in range(3):
            for t in range(5):
                third[(m + t - 2) % 256, 3 * m + p] += C3[t, p]
    both = np.convolve(MEAN_TAPS, G3)
    joint = np.zeros((256, 128))
    for o in range(128):
        for t in range(-8, 9):
            joint[(o + t) % 256, o] = both[t + 8]
    for o in range(6):
        for k in (-1, -2):
            if o - k <= 6:
                for source in range(k + 3):
                    joint[128 + 16 + source, o] -= G3[6 + o - k] * MEAN_TAPS[2 + source - k]
        joint[128 + 111, 127 - o] = joint[128 + 16, o]
        joint[128 + 110, 127 - o] = joint[128 + 17, o]
    constants = (
        rows_hi,
        rows_lo,
        *split(low_cols),
        mean_cols.astype(ml_dtypes.bfloat16),
        *split(back_cols),
        *split(fine),
        *split(third),
        *split(joint),
        lanes,
    )
    return constants, gram_rows, row_sum, up_rows


CONSTANTS, GRAM_ROWS, ROW_SUM, UP_ROWS = tables()
NUM_CONST = len(CONSTANTS)


def halves(x):
    high = x.astype(BF16)
    return high, (x - high.astype(F32)).astype(BF16)


def mm(a, b):
    return jnp.dot(a, b, preferred_element_type=F32)


def dot3(x, high, low):
    xh, xl = halves(x)
    return mm(xh, high) + mm(xl, high) + mm(xh, low)


def dot2(x, exact):
    xh, xl = halves(x)
    return mm(xh, exact) + mm(xl, exact)


def lane(shape):
    return lax.broadcasted_iota(jnp.int32, shape, len(shape) - 1)


def edge(next_tile, prev_tile):
    return jnp.where(lane(next_tile.shape) < 64, next_tile, prev_tile)


def shifted(x, t):
    n = x.shape[1]
    return x if t == 0 else pltpu.roll(x, (-t) % n, 1)


def col_filter(x, taps):
    radius = len(taps) // 2
    total = float(taps[radius]) * x
    for t in range(1, radius + 1):
        total = total + float(taps[radius + t]) * (shifted(x, t) + shifted(x, -t))
    return total


TILES = 7


def pick(e, strip, row, tile):
    return e[strip, tile, pl.ds(row, 8, stride=8), :]


def vnir_row(e, strip, i):
    first, at = (0, i) if strip == 2 or (strip == 1 and i < 8) else (4, i - 4)
    halo = pick(e, strip, i, 3) if i < 8 else pltpu.roll(pick(e, strip, i - 8, 3), 64, 1)
    return jnp.concatenate([pick(e, strip, at, first + t) for t in range(3)] + [halo], axis=1)


def swir_row(e, strip, j):
    at = lane((8, 128))
    base = 16 if j < 2 else 80
    row = None
    for k in range(4):
        part = pltpu.roll(pick(e, strip, 4 * (j % 2) + k, 3), (32 * k - base) % 128, 1)
        row = part if row is None else jnp.where(at >= 32 * k, part, row)
    return jnp.concatenate([row, pltpu.roll(pick(e, strip, 4 + j, 3), 64, 1)], axis=1)


def total_of(values):
    total = values[0]
    for value in values[1:]:
        total = total + value
    return total


def fold(x):
    total = x[:, 0:128]
    for t in range(1, x.shape[1] // 128):
        total = total + x[:, 128 * t : 128 * t + 128]
    return total


def pack(vs, ss, sb):
    at = lane((8, 128))
    zero = jnp.zeros((8, 128), F32)

    def coarse(first, tile):
        return vs[pl.ds(24 * first + tile, 8, stride=24), :] if 0 <= tile < 24 else zero

    def short(tile):
        return ss[0:4, 128 * tile : 128 * tile + 128] if 0 <= tile < 8 else zero[0:4]

    sub = lax.broadcasted_iota(jnp.int32, (8, 128), 0)
    for d in range(BLOCKS):
        for t in range(3):
            sb[d, t] = coarse(0, 3 * d + t)
            sb[d, 4 + t] = coarse(4, 3 * d + t)
        sb[d, 3, 0:4] = edge(coarse(8, 3 * d + 3), coarse(8, 3 * d - 1))[0:4]
        sb[d, 3, 4:8] = edge(short(d + 1), short(d - 1))
        other = pltpu.roll(sb[d, 3], 64, 1)
        own = edge(coarse(0, 3 * d + 3), coarse(0, 3 * d - 1))
        tile = jnp.where((at >= 56) & (at < 72), other, own)
        for j in (0, 2):
            base = 16 + 32 * j
            rows = jnp.where(
                sub < 4,
                ss[j : j + 1, 128 * d : 128 * d + 128],
                ss[j + 1 : j + 2, 128 * d : 128 * d + 128],
            )
            quarters = None
            for k in range(4):
                part = pltpu.roll(rows, (base - 32 * k) % 128, 1)
                quarters = part if quarters is None else jnp.where(lax.rem(sub, 4) == k, part, quarters)
            tile = jnp.where((at >= base) & (at < base + 32), quarters, tile)
        sb[d, 3] = tile


def pan_full(pan_ext):
    halo = edge(pan_ext[:, 1664:1792], pan_ext[:, 1536:1664])
    return halves(jnp.concatenate([pan_ext[:, 0:1536], halo], axis=1))


def pan_low_tiles(rows, consts, count):
    tiles = [rows[:count, 128 * j : 128 * j + 128] for j in range(13)]
    lhs = jnp.concatenate(
        [
            jnp.concatenate([tiles[j], edge(tiles[(j + 1) % 13], tiles[(j + 12) % 13])], axis=1)
            for j in range(13)
        ],
        axis=0,
    )
    low = dot3(lhs, consts[2][...], consts[3][...])
    return [low[count * j : count * j + count] for j in range(13)]


def mean_stage(pan_ext, consts, dd, down):
    fh, fl = pan_full(pan_ext)
    rh, rl = consts[0][64:96], consts[1][64:96]
    q = mm(rh, fh) + mm(rh, fl) + mm(rl, fh)
    low_tile = pan_low_tiles(q, consts, 16)
    diff = [q[16:32, 128 * j : 128 * j + 128] - low_tile[j] for j in range(13)]
    lhs = jnp.concatenate(
        [jnp.concatenate(diff[4 * t : 4 * t + 4], axis=1) for t in range(3)], axis=0
    )
    mean_c = consts[4]
    main = dot2(lhs, mean_c[0:512])
    for t in range(3):
        dd[8:24, 128 * t : 128 * t + 128] = main[16 * t : 16 * t + 16]
    dd[8:24, 384:512] = dot2(diff[12], mean_c[512:640])
    down[...] = dd[12:20, :]


def pan_stage(pan_ext, consts, d_out, ts):
    back_hi, back_lo = consts[5:7]
    fh, fl = pan_full(pan_ext)
    rh, rl = consts[0][0:64], consts[1][0:64]
    q = mm(rh, fh) + mm(rh, fl) + mm(rl, fh)
    low_tile = pan_low_tiles(q, consts, 64)
    total = jnp.zeros((8, 128), F32)
    for j in range(12):
        d_out[:, 128 * j : 128 * j + 128] = (
            pan_ext[8:56, 128 * j : 128 * j + 128] - low_tile[j][0:48]
        )
        for k in range(6):
            total = total + low_tile[j][8 * k : 8 * k + 8]
    zero = jnp.zeros((16, 128), F32)
    back = [low_tile[j][48:64] for j in range(12)] + [zero]
    lhs = jnp.concatenate(
        [
            jnp.concatenate(
                back[4 * t : 4 * t + 4] + [edge(back[4 * t + 4], back[(4 * t + 12) % 13])], axis=1
            )
            for t in range(3)
        ],
        axis=0,
    )
    main = dot3(lhs, back_hi[...], back_lo[...])
    rim = dot3(edge(back[0], back[11]), back_hi[512:640], back_lo[512:640])
    for t in range(3):
        ts[:, 128 * t : 128 * t + 128] = main[16 * t : 16 * t + 16]
    ts[:, 384:512] = rim
    return total


def column_mask(block):
    at = lane((1, 512))
    left = jnp.where(block == 0, 0.0, 1.0)
    right = jnp.where(block == BLOCKS - 1, 0.0, 1.0)
    return jnp.where(at >= 448, left, jnp.where(at >= 384, right, 1.0))


def mean_row(xs, i):
    total = None
    for t in range(5):
        term = float(MEAN_TAPS[t]) * xs[i + t]
        total = term if total is None else total + term
    return total


def gram_cols(lanes, x):
    y = lanes[4:5, :] * x
    for t in range(-4, 5):
        if t:
            y = y + lanes[t + 4 : t + 5, :] * shifted(x, t)
    return y


OWN = range(2, 14)
RIM = (0, 1, 14, 15)
EARLY = range(2, 10)


def gram_row(xc, i, among, scale):
    total = None
    for j in among:
        if GRAM_ROWS[i, j] != 0.0:
            term = float(scale * GRAM_ROWS[i, j]) * xc[j]
            total = term if total is None else total + term
    return total


def add_products(acc, xs, ys, ts, ones, i):
    x = xs[i + 6]
    for j in range(8):
        acc[j] = acc[j] + fold(x * ys[i, j : j + 1, :])
    acc[8] = acc[8] + fold(x * ts[i : i + 1, :])
    acc[9] = acc[9] + float(ROW_SUM[i]) * fold(x * ones)


def early_compute(e, consts, ts, xs, xc, ys, vl, lvp, sums):
    lanes = consts[13]
    for i in range(12):
        row = vnir_row(e, 1, i)
        xs[i + 8] = row
        xc[i + 2] = gram_cols(lanes, row)
    acc = [jnp.zeros((8, 128), F32) for _ in range(10)]
    for i in OWN:
        ys[i] = gram_row(xc, i, OWN, 1.0)
    for i in OWN:
        add_products(acc, xs, ys, ts, lanes[9:10, :], i)
    for k in range(10):
        sums[k] = acc[k]
    means = {i: mean_row(xs, i + 6) for i in EARLY}
    for i in EARLY:
        vl[i] = col_filter(means[i], MEAN_TAPS)[:, 0:384]
    for i in range(12):
        lvp[i] = total_of([float(G3[k - i + 6]) * means[k] for k in EARLY if abs(k - i) <= 6])


def front_compute(e, consts, sums_ref, r, c, ts, dd, xs, xc, ys, lvs, vl, lvp, swu, dl, rl):
    third_hi, third_lo, joint_hi, joint_lo, lanes = consts[9:14]
    for k in range(28):
        if k < 8:
            xs[k] = vnir_row(e, 0, k + 4)
        elif k >= 20:
            xs[k] = vnir_row(e, 2, k - 20)
    up_keep = jnp.where(r == 0, 0.0, 1.0)
    down_keep = jnp.where(r == STRIPS - 1, 0.0, 1.0)
    mask = column_mask(c)
    means = {}
    for i in range(-6, 18):
        if i not in EARLY:
            row = mean_row(xs, i + 6)
            means[i] = row * up_keep if i < 0 else (row * down_keep if i >= 12 else row)
    at = lane((8, 128))
    left = (at >= 16) & (at < 18) & (c == 0)
    right = (at >= 110) & (at < 112) & (c == BLOCKS - 1)
    rows = []
    for i in range(12):
        total = lvp[i] + total_of(
            [float(G3[k - i + 6]) * means[k] for k in means if abs(k - i) <= 6]
        )
        rows.append(total)
    lhs = []
    for t in range(3):
        for i in range(12):
            tile = [rows[i][:, 128 * k : 128 * k + 128] for k in range(4)]
            rim = jnp.where(at < 8, tile[t + 1], jnp.where(at >= 120, tile[(t + 3) % 4], 0.0))
            if t == 0:
                rim = jnp.where(left, pltpu.roll(tile[0], 16, 1), rim)
            if t == 2:
                rim = jnp.where(right, pltpu.roll(tile[2], 112, 1), rim)
            lhs.append(jnp.concatenate([tile[t], rim], axis=1))
    lowered = dot3(jnp.concatenate(lhs, axis=0), joint_hi[...], joint_lo[...])
    for i in range(12):
        low = jnp.concatenate([lowered[96 * t + 8 * i : 96 * t + 8 * i + 8] for t in range(3)], axis=1)
        lvs[i] = low
        if i in EARLY:
            vl[i] = vl[i] - low
        else:
            vl[i] = col_filter(means[i], MEAN_TAPS)[:, 0:384] - low
    for i in RIM:
        xc[i] = gram_cols(lanes, xs[i + 6])
    acc = [sums_ref[k] for k in range(10)]
    for i in RIM:
        ys[i] = gram_row(xc, i, OWN, 2.0) + gram_row(xc, i, RIM, 1.0)
        add_products(acc, xs, ys, ts, lanes[9:10, :], i)
    sums = {k: acc[k] for k in range(10)}
    sums[10] = sums_ref[10]
    dcol = total_of([float(G3[t]) * dd[t + 2 : t + 14, :] for t in range(13)]) * mask
    low_d = col_filter(dcol, G3)[:, 0:384]
    dl[...] = dd[8:20, 0:384] - low_d
    ts[0:12, 0:384] = low_d
    srow = [
        swir_row(e, *at)
        for at in ((0, 2), (0, 3), (1, 0), (1, 1), (1, 2), (1, 3), (2, 0), (2, 1))
    ]
    up = []
    for m in range(4):
        for p in range(3):
            total = None
            for t in range(5):
                if C3[t, p] != 0.0:
                    term = float(C3[t, p]) * srow[m + t]
                    total = term if total is None else total + term
            up.append(total)
    swu[...] = dot3(jnp.concatenate(up, axis=0), third_hi[...], third_lo[...])
    acc = [jnp.zeros((8, 128), F32) for _ in range(22)]
    for i in range(12):
        lv = lvs[i]
        sw = swu[8 * i : 8 * i + 8, :]
        ld = ts[i : i + 1, 0:384]
        for j in range(8):
            other = lvs[i, j : j + 1, :]
            acc[j] = acc[j] + fold(lv * other)
            acc[8 + j] = acc[8 + j] + fold(sw * other)
        acc[16] = acc[16] + fold(lv * ld)
        acc[17] = acc[17] + fold(sw * ld)
        acc[18] = acc[18] + fold(lv)
        acc[19] = acc[19] + fold(sw)
        acc[20] = acc[20] + fold(ld)
        acc[21] = acc[21] + fold(ld * ld)
    for k in range(22):
        sums[16 + k] = acc[k]
    at = lane((8, 128))
    packed = jnp.zeros((8, 128), F32)
    for k, value in sums.items():
        packed = jnp.where(at == k, jnp.sum(value, axis=1, keepdims=True), packed)
    rl[...] = packed


def upsample(xs, consts, zs, up_out):
    fine_hi, fine_lo = consts[7:9]
    for m in range(12):
        for p in range(4):
            total = None
            for t in range(5):
                if C4[t, p] != 0.0:
                    term = float(C4[t, p]) * xs[m + t + 6]
                    total = term if total is None else total + term
            for tile in range(4):
                zs[tile, pl.ds(4 * m + p, 8, stride=48), :] = total[
                    :, 128 * tile : 128 * tile + 128
                ]

    @pl.loop(0, BANDS)
    def _(b):
        at = pl.ds(pl.multiple_of(b * 48, 48), 48)
        z = [zs[k, at, :] for k in range(4)]
        lhs = jnp.concatenate(
            [
                jnp.concatenate([z[k], edge(z[k + 1], z[(k + 3) % 4])], axis=1)
                for k in range(3)
            ],
            axis=0,
        )
        up = dot3(lhs, fine_hi[...], fine_lo[...])
        for k in range(3):
            up_out[at, 512 * k : 512 * k + 512] = up[48 * k : 48 * k + 48]


def front_kernel(pan, vnir, swir, *rest):
    hbm_consts = rest[:NUM_CONST]
    rt, up_out, d_out, vl, swu, dl = rest[NUM_CONST : NUM_CONST + 6]
    rest = rest[NUM_CONST + 6 :]
    consts = rest[:NUM_CONST]
    (vs, ss, sb, e, pe, xs, xc, ys, ts, dd, lvs, zs, sums, rl, g1, mid, g2, lvp, down, dup, ddn) = rest[
        NUM_CONST : NUM_CONST + 21
    ]
    (csem, lsem, ssem, rsem, fsem, hsem, psem, qsem, g1s, g1r, g2s, g2r, dsem, tsem) = rest[NUM_CONST + 21 :]
    r = lax.axis_index("rows")
    c = lax.axis_index("band")

    def remote(src, dst, send, recv, row, block):
        return pltpu.make_async_remote_copy(
            src_ref=src, dst_ref=dst, send_sem=send, recv_sem=recv,
            device_id=(row, block), device_id_type=MESH,
        )

    rl8 = lax.rem(r, 8)
    base = r - rl8
    barrier = pltpu.get_barrier_semaphore()

    def greet(row, block):
        pl.semaphore_signal(barrier, inc=1, device_id=(row, block), device_id_type=MESH)

    core = lax.rem(rl8, 2)
    x = lax.div(rl8, 2)
    y_hi, z = lax.div(c, 4), lax.rem(c, 4)
    y_lo = lax.div(r, 8)
    y = 2 * y_hi + y_lo

    def step_one(dx, dcore):
        return 2 * lax.rem(x + dx, 4) + lax.rem(core + dcore, 2)

    def step_two(dy, dz):
        return 4 * lax.rem(y + dy, 4) + lax.rem(z + dz, 4)

    def place_two(slot):
        y2 = lax.div(slot, 4)
        return 8 * lax.rem(y2, 2) + rl8, 4 * lax.div(y2, 2) + lax.rem(slot, 4)

    near = lambda d: min(d, 4 - d)
    ones = sorted(
        [(dx, dc) for dx in range(4) for dc in range(2) if dx or dc], key=lambda d: (-near(d[0]), -d[1])
    )
    twos = sorted(
        [(dy, dz) for dy in range(4) for dz in range(4) if dy or dz],
        key=lambda d: (-near(d[0]) - near(d[1]), d),
    )
    first = [(base + step_one(*d), c) for d in ones]
    second = [place_two(step_two(*d)) for d in twos]
    strips = ((1, r < STRIPS - 1), (-1, r > 0))
    blocks = ((1, c < BLOCKS - 1), (-1, c > 0))
    beside = [(r + dr, c + dc, ok & also) for dr, ok in strips for dc, also in blocks]
    beside += [(r + dr, c, ok) for dr, ok in strips]
    greetings = len(second) + len(first)
    for row, block in second:
        greet(row, block)
    for row, block, ok in beside:
        pl.when(ok)(functools.partial(greet, row, block))
        greetings = greetings + jnp.where(ok, 1, 0)
    for row, block in first:
        greet(row, block)

    loads = [
        pltpu.make_async_copy(vnir, vs.at[pl.ds(0, 288)], lsem.at[0]),
        pltpu.make_async_copy(swir.at[0], ss, lsem.at[1]),
        pltpu.make_async_copy(pan, pe.at[pl.ds(8, 48), pl.ds(0, 1536)], lsem.at[2]),
    ]
    for copy in loads:
        copy.start()
    const_loads = [
        pltpu.make_async_copy(hbm_consts[k], consts[k], csem.at[k]) for k in range(NUM_CONST)
    ]

    @pl.when(r == 0)
    def _():
        pe[0:8, :] = jnp.zeros((8, 1792), F32)
        e[0, 3:7] = jnp.zeros((4, 64, 128), F32)
        dup[...] = jnp.zeros((8, 512), F32)

    @pl.when(r == STRIPS - 1)
    def _():
        pe[56:64, :] = jnp.zeros((8, 1792), F32)
        e[2, 0:4] = jnp.zeros((4, 64, 128), F32)
        ddn[...] = jnp.zeros((8, 512), F32)

    @pl.when(c == 0)
    def _():
        pe[:, 1536:1664] = jnp.zeros((64, 128), F32)

    @pl.when(c == BLOCKS - 1)
    def _():
        pe[:, 1664:1792] = jnp.zeros((64, 128), F32)

    loads[0].wait()
    loads[1].wait()
    pack(vs, ss, sb)
    loads[2].wait()
    pl.semaphore_wait(barrier, greetings)

    def pan_cols(side):
        src = pe.at[pl.ds(8, 48), pl.ds(1408, 128)] if side == 0 else pan_first
        dst = pe.at[pl.ds(8, 48), pl.ds(1536 + 128 * side, 128)]
        block = c + 1 if side == 0 else c - 1
        return remote(src, dst, psem.at[side], qsem.at[side], r, block)

    pan_first = pe.at[pl.ds(8, 48), pl.ds(0, 128)]

    def pan_part(side, cols, n):
        src = pe.at[pl.ds(48, 8), cols] if side == 0 else pe.at[pl.ds(8, 8), cols]
        dst = pe.at[pl.ds(0, 8), cols] if side == 0 else pe.at[pl.ds(56, 8), cols]
        row = r + 1 if side == 0 else r - 1
        return remote(src, dst, psem.at[n + side], qsem.at[n + side], row, c)

    def pan_rows(side):
        return pan_part(side, pl.ds(0, 1536), 2)

    def pan_corner(side, across):
        src = pe.at[
            pl.ds(48 if side == 0 else 8, 8), pl.ds(1408 if across == 0 else 0, 128)
        ]
        dst = pe.at[pl.ds(0 if side == 0 else 56, 8), pl.ds(1536 + 128 * across, 128)]
        row = r + 1 if side == 0 else r - 1
        block = c + 1 if across == 0 else c - 1
        n = 2 * side + across
        return remote(src, dst, dsem.at[n], tsem.at[n], row, block)

    def mean_rows(side):
        src, dst = (down, dup) if side == 0 else (dd.at[pl.ds(8, 8)], ddn)
        row = r + 1 if side == 0 else r - 1
        return remote(src, dst, psem.at[6 + side], qsem.at[6 + side], row, c)

    has_below, has_above = r < STRIPS - 1, r > 0
    has_right, has_left = c < BLOCKS - 1, c > 0
    to = {(s, a): (has_below if s == 0 else has_above) & (has_right if a == 0 else has_left)
          for s in range(2) for a in range(2)}
    into = {(s, a): (has_above if s == 0 else has_below) & (has_left if a == 0 else has_right)
            for s in range(2) for a in range(2)}

    def when(cond, action):
        @pl.when(cond)
        def _():
            action()

    when(has_right, lambda: pan_cols(0).start())
    when(has_left, lambda: pan_cols(1).start())
    for key in to:
        when(to[key], functools.partial(lambda key: pan_corner(*key).start(), key))

    def band_rows(b):
        return pl.ds(pl.multiple_of(b * 8, 8), 8)

    turns = [(0, 0), (1, 2), (1, 1), (1, 3), (1, 0), (0, 2), (0, 1), (0, 3)]

    def band_at(dyh, dz):
        return 4 * lax.rem(y_hi + dyh, 2) + lax.rem(z + dz, 4)

    def block_send(k):
        block = band_at(*turns[k])
        return remote(sb.at[block], e.at[1, pl.ds(0, TILES), band_rows(c)], ssem.at[k], rsem.at[k], r, block)

    def block_recv(k):
        b = band_at(turns[k][0], 4 - turns[k][1])
        return remote(sb.at[0], e.at[1, pl.ds(0, TILES), band_rows(b)], ssem.at[k], rsem.at[k], r, c)

    def forward(k, side):
        b = band_at(turns[k][0], 4 - turns[k][1])
        part = pl.ds(3 - 3 * side, 4)
        dst = e.at[2 * side, part, band_rows(b)]
        src = sb.at[c, part] if k == 0 else e.at[1, part, band_rows(b)]
        row = r + 1 if side == 0 else r - 1
        return remote(src, dst, fsem.at[side, k], hsem.at[side, k], row, c)

    for k in range(1, 8):
        block_send(k).start()
    own = pltpu.make_async_copy(sb.at[c], e.at[1, pl.ds(0, TILES), band_rows(c)], lsem.at[3])
    own.start()
    when(has_below, lambda: forward(0, 0).start())
    when(has_above, lambda: forward(0, 1).start())
    when(has_below, lambda: pan_rows(0).start())
    when(has_above, lambda: pan_rows(1).start())

    for copy in const_loads:
        copy.start()

    for copy in const_loads:
        copy.wait()
    when(has_left, lambda: pan_cols(0).wait_recv())
    when(has_right, lambda: pan_cols(1).wait_recv())
    when(has_above, lambda: pan_rows(0).wait_recv())
    when(has_below, lambda: pan_rows(1).wait_recv())
    for key in into:
        when(into[key], functools.partial(lambda key: pan_corner(*key).wait_recv(), key))
    mean_stage(pe, consts, dd, down)
    when(has_below, lambda: mean_rows(0).start())
    when(has_above, lambda: mean_rows(1).start())
    for k in range(7, 0, -1):
        block_recv(k).wait_recv()
        when(has_below, functools.partial(lambda k: forward(k, 0).start(), k))
        when(has_above, functools.partial(lambda k: forward(k, 1).start(), k))
    own.wait()
    sums[10] = pan_stage(pe, consts, d_out, ts)
    early_compute(e, consts, ts, xs, xc, ys, vl, lvp, sums)
    for k in range(8):
        when(has_above, functools.partial(lambda k: forward(k, 0).wait_recv(), k))
        when(has_below, functools.partial(lambda k: forward(k, 1).wait_recv(), k))

    when(has_above, lambda: mean_rows(0).wait_recv())
    when(has_below, lambda: mean_rows(1).wait_recv())
    dd[0:8] = dup[...]
    dd[20:28] = ddn[...]
    front_compute(e, consts, sums, r, c, ts, dd, xs, xc, ys, lvs, vl, lvp, swu, dl, rl)

    me_two = 4 * y + z

    def sum_one(n):
        row, block = first[n]
        return remote(rl, g1.at[rl8], g1s.at[n], g1r.at[n], row, block)

    def sum_one_recv(n):
        dx, dc = ones[n]
        return remote(rl, g1.at[step_one(4 - dx, 2 - dc)], g1s.at[n], g1r.at[n], r, c)

    def sum_two(n):
        row, block = second[n]
        return remote(mid, g2.at[me_two], g2s.at[n], g2r.at[n], row, block)

    def sum_two_recv(n):
        dy, dz = twos[n]
        return remote(mid, g2.at[step_two(4 - dy, 4 - dz)], g2s.at[n], g2r.at[n], r, c)

    for n in range(7):
        sum_one(n).start()
    g1[rl8] = rl[...]
    for n in range(7):
        sum_one_recv(n).wait_recv()
    total = g1[0]
    for k in range(1, 8):
        total = total + g1[k]
    mid[...] = total
    for n in range(15):
        sum_two(n).start()
    g2[me_two] = total
    upsample(xs, consts, zs, up_out)
    for n in range(15):
        sum_two_recv(n).wait_recv()
    total = g2[0]
    for k in range(1, 16):
        total = total + g2[k]
    rt[...] = total

    for key in to:
        when(to[key], functools.partial(lambda key: pan_corner(*key).wait_send(), key))
    when(has_below, lambda: mean_rows(0).wait_send())
    when(has_above, lambda: mean_rows(1).wait_send())
    for k in range(1, 8):
        block_send(k).wait_send()
        sum_one(k - 1).wait_send()
    for n in range(15):
        sum_two(n).wait_send()
    when(has_right, lambda: pan_cols(0).wait_send())
    when(has_left, lambda: pan_cols(1).wait_send())
    for side, cond in ((0, has_below), (1, has_above)):
        when(cond, functools.partial(lambda side: pan_rows(side).wait_send(), side))
        for k in range(8):
            when(cond, functools.partial(lambda k, side: forward(k, side).wait_send(), k, side))


def front(pan, vnir, swir):
    return pl.pallas_call(
        front_kernel,
        name="front",
        out_shape=[
            VM((8, 128), F32),
            VM((384, 1536), F32),
            VM((48, 1536), F32),
            VM((12, 8, 384), F32),
            VM((96, 384), F32),
            VM((12, 384), F32),
        ],
        in_specs=[pl.BlockSpec(memory_space=pl.ANY)] * (3 + NUM_CONST),
        out_specs=[pl.BlockSpec(memory_space=VM)] * 6,
        scratch_shapes=[VM(k.shape, BF16 if k.dtype == ml_dtypes.bfloat16 else F32) for k in CONSTANTS]
        + [
            VM((384, 128), F32),
            VM((4, 1024), F32),
            VM((8, TILES, 8, 128), F32),
            VM((3, TILES, 64, 128), F32),
            VM((64, 1792), F32),
            VM((28, 8, 512), F32),
            VM((16, 8, 512), F32),
            VM((16, 8, 512), F32),
            VM((16, 512), F32),
            VM((32, 512), F32),
            VM((12, 8, 384), F32),
            VM((4, 384, 128), F32),
            VM((11, 8, 128), F32),
            VM((8, 128), F32),
            VM((8, 8, 128), F32),
            VM((8, 128), F32),
            VM((16, 8, 128), F32),
            VM((12, 8, 512), F32),
            VM((8, 512), F32),
            VM((8, 512), F32),
            VM((8, 512), F32),
            pltpu.SemaphoreType.DMA((NUM_CONST,)),
            pltpu.SemaphoreType.DMA((4,)),
            pltpu.SemaphoreType.DMA((8,)),
            pltpu.SemaphoreType.DMA((8,)),
            pltpu.SemaphoreType.DMA((2, 8)),
            pltpu.SemaphoreType.DMA((2, 8)),
            pltpu.SemaphoreType.DMA((8,)),
            pltpu.SemaphoreType.DMA((8,)),
            pltpu.SemaphoreType.DMA((8,)),
            pltpu.SemaphoreType.DMA((8,)),
            pltpu.SemaphoreType.DMA((16,)),
            pltpu.SemaphoreType.DMA((16,)),
            pltpu.SemaphoreType.DMA((4,)),
            pltpu.SemaphoreType.DMA((4,)),
        ],
        compiler_params=pltpu.CompilerParams(
            collective_id=0, has_side_effects=True, vmem_limit_bytes=56 << 20
        ),
    )(pan, vnir, swir, *[jnp.asarray(k) for k in CONSTANTS])


def solve_spd(a, b):
    a = [list(row) for row in a]
    inverse = []
    factor = [[None] * 8 for _ in range(8)]
    for j in range(8):
        inv = 1.0 / a[j][j]
        inverse.append(inv)
        for i in range(j + 1, 8):
            factor[i][j] = a[i][j] * inv
        for i in range(j + 1, 8):
            for k in range(j + 1, i + 1):
                a[i][k] = a[i][k] - factor[i][j] * a[k][j]
    z = list(b)
    for j in range(8):
        for i in range(j + 1, 8):
            z[i] = z[i] - factor[i][j] * z[j]
    z = [z[j] * inverse[j] for j in range(8)]
    for j in range(7, -1, -1):
        for i in range(j):
            z[i] = z[i] - factor[j][i] * z[j]
    return z


def solve_first(rt, cb):
    for k in range(11):
        cb[k] = jnp.broadcast_to(rt[:, k : k + 1], (8, 128))
    mean = [cb[9, i : i + 1, :] * (1.0 / N1) for i in range(8)]
    mean_p = jnp.sum(cb[10], axis=0, keepdims=True) * (1.0 / N1)
    a = [
        [
            (cb[j, i : i + 1, :] + cb[i, j : j + 1, :]) * (0.5 / N1) - mean[i] * mean[j]
            for j in range(i + 1)
        ]
        for i in range(8)
    ]
    b = [cb[8, i : i + 1, :] * (1.0 / N1) - mean[i] * mean_p for i in range(8)]
    w = solve_spd(a, b)
    scale = 1.0 / total_of([b[i] * w[i] for i in range(8)])
    return [b[i] * scale for i in range(8)]


def solve_second(rt, cb, gain):
    for k in range(16, 38):
        cb[k] = jnp.broadcast_to(rt[:, k : k + 1], (8, 128))

    def at(k, i):
        return cb[k, i : i + 1, :]

    sum_d = at(36, 0)
    sum_dd = at(37, 0)
    q = [at(32, i) for i in range(8)]
    mean2 = [(at(34, i) + gain[i] * sum_d) * (1.0 / N2) for i in range(8)]
    a2 = [
        [
            (at(16 + j, i) + gain[i] * q[j] + gain[j] * q[i] + gain[i] * gain[j] * sum_dd) * (1.0 / N2)
            - mean2[i] * mean2[j]
            for j in range(i + 1)
        ]
        for i in range(8)
    ]
    swir_mean = cb[35] * (1.0 / N2)
    cross = [
        (cb[24 + i] + gain[i] * cb[33]) * (1.0 / N2) - mean2[i] * swir_mean for i in range(8)
    ]
    y = [jnp.sum(cross[i], axis=0, keepdims=True) * 0.125 for i in range(8)]
    v = solve_spd(a2, y)
    share = total_of([v[i] * cross[i] for i in range(8)]) / total_of([v[i] * y[i] for i in range(8)])
    return v, share


def wide(x, copies):
    return jnp.concatenate([x] * copies, axis=1)


def back_kernel(rt, up, d, vl, swu, dl, joined, joined_swir, cb, gs, out, rows_out, sem):
    gain = solve_first(rt, cb)
    for b in range(8):
        gs[b] = jnp.broadcast_to(gain[b], (8, 128))

    @pl.loop(0, BANDS)
    def _(b):
        g = wide(gs[b], 2)
        rows = pl.multiple_of(b * 48, 48)
        for i in range(6):
            for t in range(6):
                at = slice(256 * t, 256 * t + 256)
                out[b, 8 * i : 8 * i + 8, at] = (
                    up[pl.ds(rows + 8 * i, 8), at] + g * d[8 * i : 8 * i + 8, at]
                )
        pltpu.make_async_copy(out.at[b], joined.at[b], sem.at[b]).start()

    gain = [gs[b, 0:1, :] for b in range(8)]
    v, share = solve_second(rt, cb, gain)
    row8 = lax.broadcasted_iota(jnp.int32, (8, 128), 0)
    v8 = jnp.zeros((8, 128), F32)
    for b in range(8):
        v8 = jnp.where(row8 == b, jnp.broadcast_to(v[b], (8, 128)), v8)
    v8 = wide(v8, 3)
    vg = wide(total_of([v[b] * gain[b] for b in range(8)]), 3)
    share3 = wide(share, 3)
    for i in range(12):
        detail = jnp.sum(v8 * vl[i], axis=0, keepdims=True) + vg * dl[i : i + 1, :]
        rows_out[i] = swu[8 * i : 8 * i + 8, :] + share3 * detail
    last = pltpu.make_async_copy(rows_out, joined_swir, sem.at[8])
    last.start()

    @pl.loop(0, BANDS)
    def _(b):
        pltpu.make_async_copy(out.at[b], joined.at[b], sem.at[b]).wait()

    last.wait()


def back(rt, up, d, vl, swu, dl):
    return pl.pallas_call(
        back_kernel,
        name="back",
        out_shape=[
            jax.ShapeDtypeStruct((8, 48, 1536), F32),
            jax.ShapeDtypeStruct((12, 8, 384), F32),
        ],
        in_specs=[pl.BlockSpec(memory_space=VM)] * 6,
        out_specs=[pl.BlockSpec(memory_space=pl.ANY)] * 2,
        scratch_shapes=[
            VM((38, 8, 128), F32),
            VM((8, 8, 128), F32),
            VM((8, 48, 1536), F32),
            VM((12, 8, 384), F32),
            pltpu.SemaphoreType.DMA((9,)),
        ],
        compiler_params=pltpu.CompilerParams(vmem_limit_bytes=32 << 20),
    )(rt, up, d, vl, swu, dl)


def local(pan, vnir, swir):
    joined, rows = back(*front(pan, vnir.reshape(288, 128), swir))
    return joined, jnp.swapaxes(rows, 0, 1)


def solution(mesh):
    return jax.shard_map(
        local,
        mesh=mesh,
        in_specs=(P("rows", "band"), P("band", "rows", None), P("band", "rows", None)),
        out_specs=(P(None, "rows", "band"), P(None, "rows", "band")),
        check_vma=False,
    )
```

```python
import functools
import math

import jax
import jax.numpy as jnp
import ml_dtypes
import numpy as np
from jax import lax
from jax.experimental import pallas as pl
from jax.experimental.pallas import tpu as pltpu
from jax.sharding import PartitionSpec as P

F32 = jnp.float32
BF16 = jnp.bfloat16
MESH = pl.DeviceIdType.MESH
VM = pltpu.VMEM

BANDS = 8
STRIPS = 16
BLOCKS = 8
HEIGHT = 768
WIDTH = 12288
N1 = float(HEIGHT * WIDTH)
N2 = float(HEIGHT * WIDTH // 16)
NYQUIST_GAIN = 0.29


def gauss_taps(upscale, kernel_len):
    spread = upscale * math.sqrt(-2.0 * math.log(NYQUIST_GAIN)) / math.pi
    radius = kernel_len // 2
    offsets = np.arange(-radius, radius + 1) * 1.0
    values = np.exp(-(offsets**2) / (2.0 * spread**2))
    return values / values.sum()


def cubic_weight(distance):
    distance = abs(distance)
    if distance <= 1.0:
        return 1.5 * distance**3 - 2.5 * distance**2 + 1.0
    if distance < 2.0:
        return -0.5 * distance**3 + 2.5 * distance**2 - 4.0 * distance + 2.0
    return 0.0


def cubic_table(upscale):
    weights = np.zeros((5, upscale))
    for phase_index in range(upscale):
        centre = (phase_index + 0.5) / upscale - 0.5
        first_tap = math.floor(centre)
        fraction = centre - first_tap
        for tap_index in range(-1, 3):
            weights[first_tap + tap_index + 2, phase_index] += cubic_weight(tap_index - fraction)
    return weights


C4 = cubic_table(4)
C3 = cubic_table(3)
G4 = gauss_taps(4, 17)
G3 = gauss_taps(3, 13)
MEAN_TAPS = C4.mean(axis=1)


def split(matrix):
    high = matrix.astype(np.float32).astype(ml_dtypes.bfloat16)
    low = (matrix - high.astype(np.float64)).astype(ml_dtypes.bfloat16)
    return high, low


def tables():
    up_rows = np.zeros((48, 16))
    for m in range(12):
        for p in range(4):
            for t in range(5):
                up_rows[4 * m + p, m + t] += C4[t, p]
    up_cols = np.zeros((1536, 512))
    for m in range(384):
        for p in range(4):
            for t in range(5):
                up_cols[4 * m + p, (m + t - 2) % 512] += C4[t, p]
    gram_rows = up_rows.T @ up_rows
    gram_cols = up_cols.T @ up_cols
    lanes = np.zeros((16, 512), np.float32)
    at = np.arange(512)
    for t in range(-4, 5):
        lanes[t + 4] = gram_cols[at, (at + t) % 512]
    lanes[9] = up_cols.sum(axis=0)
    row_sum = up_rows.sum(axis=0)

    low = np.zeros((48, 64))
    mean = np.zeros((16, 64))
    for f in range(48):
        low[f, f : f + 17] = G4
    for i in range(12):
        mean[i, 8 + 4 * i : 12 + 4 * i] = 0.25
    mean_low = np.zeros((16, 64))
    mean_low[:12] = low.reshape(12, 4, 64).mean(axis=1)
    rows_hi, rows_lo = split(np.concatenate([low, up_rows.T @ low, mean_low, mean]))

    low_cols = np.zeros((256, 128))
    for o in range(128):
        for t in range(-8, 9):
            q = o + t
            row = q if 0 <= q < 128 else (q if q >= 128 else 256 + q)
            low_cols[row, o] = G4[t + 8]
    mean_cols = np.zeros((640, 128))
    for f in range(512):
        mean_cols[f, f // 4] = 0.25
    for f in range(32):
        mean_cols[512 + f, f // 4] = 0.25
        mean_cols[512 + 96 + f, 120 + f // 4] = 0.25
    back_cols = np.zeros((640, 128))
    for n in range(128):
        for t in range(5):
            for p in range(4):
                f = 4 * (n - (t - 2)) + p
                row = f if f >= 0 else 640 + f
                back_cols[row, n] += C4[t, p]
    fine = np.zeros((256, 512))
    for m in range(128):
        for p in range(4):
            for t in range(5):
                fine[(m + t - 2) % 256, 4 * m + p] += C4[t, p]
    third = np.zeros((256, 384))
    for m in range(128):
        for p in range(3):
            for t in range(5):
                third[(m + t - 2) % 256, 3 * m + p] += C3[t, p]
    both = np.convolve(MEAN_TAPS, G3)
    joint = np.zeros((256, 128))
    for o in range(128):
        for t in range(-8, 9):
            joint[(o + t) % 256, o] = both[t + 8]
    for o in range(6):
        for k in (-1, -2):
            if o - k <= 6:
                for source in range(k + 3):
                    joint[128 + 16 + source, o] -= G3[6 + o - k] * MEAN_TAPS[2 + source - k]
        joint[128 + 111, 127 - o] = joint[128 + 16, o]
        joint[128 + 110, 127 - o] = joint[128 + 17, o]
    constants = (
        rows_hi,
        rows_lo,
        *split(low_cols),
        mean_cols.astype(ml_dtypes.bfloat16),
        *split(back_cols),
        *split(fine),
        *split(third),
        *split(joint),
        lanes,
    )
    return constants, gram_rows, row_sum, up_rows


CONSTANTS, GRAM_ROWS, ROW_SUM, UP_ROWS = tables()
NUM_CONST = len(CONSTANTS)


def halves(x):
    high = x.astype(BF16)
    return high, (x - high.astype(F32)).astype(BF16)


def mm(a, b):
    return jnp.dot(a, b, preferred_element_type=F32)


def dot3(x, high, low):
    xh, xl = halves(x)
    return mm(xh, high) + mm(xl, high) + mm(xh, low)


def dot2(x, exact):
    xh, xl = halves(x)
    return mm(xh, exact) + mm(xl, exact)


def lane(shape):
    return lax.broadcasted_iota(jnp.int32, shape, len(shape) - 1)


def edge(next_tile, prev_tile):
    return jnp.where(lane(next_tile.shape) < 64, next_tile, prev_tile)


def shifted(x, t):
    n = x.shape[1]
    return x if t == 0 else pltpu.roll(x, (-t) % n, 1)


def col_filter(x, taps):
    radius = len(taps) // 2
    total = float(taps[radius]) * x
    for t in range(1, radius + 1):
        total = total + float(taps[radius + t]) * (shifted(x, t) + shifted(x, -t))
    return total


TILES = 7


def pick(e, strip, row, tile):
    return e[strip, tile, pl.ds(row, 8, stride=8), :]


def vnir_row(e, strip, i):
    first, at = (0, i) if strip == 2 or (strip == 1 and i < 8) else (4, i - 4)
    halo = pick(e, strip, i, 3) if i < 8 else pltpu.roll(pick(e, strip, i - 8, 3), 64, 1)
    return jnp.concatenate([pick(e, strip, at, first + t) for t in range(3)] + [halo], axis=1)


def swir_row(e, strip, j):
    at = lane((8, 128))
    base = 16 if j < 2 else 80
    row = None
    for k in range(4):
        part = pltpu.roll(pick(e, strip, 4 * (j % 2) + k, 3), (32 * k - base) % 128, 1)
        row = part if row is None else jnp.where(at >= 32 * k, part, row)
    return jnp.concatenate([row, pltpu.roll(pick(e, strip, 4 + j, 3), 64, 1)], axis=1)


def total_of(values):
    total = values[0]
    for value in values[1:]:
        total = total + value
    return total


def fold(x):
    total = x[:, 0:128]
    for t in range(1, x.shape[1] // 128):
        total = total + x[:, 128 * t : 128 * t + 128]
    return total


def pack(vs, ss, sb):
    at = lane((8, 128))
    zero = jnp.zeros((8, 128), F32)

    def coarse(first, tile):
        return vs[pl.ds(24 * first + tile, 8, stride=24), :] if 0 <= tile < 24 else zero

    def short(tile):
        return ss[0:4, 128 * tile : 128 * tile + 128] if 0 <= tile < 8 else zero[0:4]

    sub = lax.broadcasted_iota(jnp.int32, (8, 128), 0)
    for d in range(BLOCKS):
        for t in range(3):
            sb[d, t] = coarse(0, 3 * d + t)
            sb[d, 4 + t] = coarse(4, 3 * d + t)
        sb[d, 3, 0:4] = edge(coarse(8, 3 * d + 3), coarse(8, 3 * d - 1))[0:4]
        sb[d, 3, 4:8] = edge(short(d + 1), short(d - 1))
        other = pltpu.roll(sb[d, 3], 64, 1)
        own = edge(coarse(0, 3 * d + 3), coarse(0, 3 * d - 1))
        tile = jnp.where((at >= 56) & (at < 72), other, own)
        for j in (0, 2):
            base = 16 + 32 * j
            rows = jnp.where(
                sub < 4,
                ss[j : j + 1, 128 * d : 128 * d + 128],
                ss[j + 1 : j + 2, 128 * d : 128 * d + 128],
            )
            quarters = None
            for k in range(4):
                part = pltpu.roll(rows, (base - 32 * k) % 128, 1)
                quarters = part if quarters is None else jnp.where(lax.rem(sub, 4) == k, part, quarters)
            tile = jnp.where((at >= base) & (at < base + 32), quarters, tile)
        sb[d, 3] = tile


def pan_full(pan_ext):
    halo = edge(pan_ext[:, 1664:1792], pan_ext[:, 1536:1664])
    return halves(jnp.concatenate([pan_ext[:, 0:1536], halo], axis=1))


def pan_low_tiles(rows, consts, count):
    tiles = [rows[:count, 128 * j : 128 * j + 128] for j in range(13)]
    lhs = jnp.concatenate(
        [
            jnp.concatenate([tiles[j], edge(tiles[(j + 1) % 13], tiles[(j + 12) % 13])], axis=1)
            for j in range(13)
        ],
        axis=0,
    )
    low = dot3(lhs, consts[2][...], consts[3][...])
    return [low[count * j : count * j + count] for j in range(13)]


def mean_stage(pan_ext, consts, dd, down):
    fh, fl = pan_full(pan_ext)
    rh, rl = consts[0][64:96], consts[1][64:96]
    q = mm(rh, fh) + mm(rh, fl) + mm(rl, fh)
    low_tile = pan_low_tiles(q, consts, 16)
    diff = [q[16:32, 128 * j : 128 * j + 128] - low_tile[j] for j in range(13)]
    lhs = jnp.concatenate(
        [jnp.concatenate(diff[4 * t : 4 * t + 4], axis=1) for t in range(3)], axis=0
    )
    mean_c = consts[4]
    main = dot2(lhs, mean_c[0:512])
    for t in range(3):
        dd[8:24, 128 * t : 128 * t + 128] = main[16 * t : 16 * t + 16]
    dd[8:24, 384:512] = dot2(diff[12], mean_c[512:640])
    down[...] = dd[12:20, :]


def pan_stage(pan_ext, consts, d_out, ts):
    back_hi, back_lo = consts[5:7]
    fh, fl = pan_full(pan_ext)
    rh, rl = consts[0][0:64], consts[1][0:64]
    q = mm(rh, fh) + mm(rh, fl) + mm(rl, fh)
    low_tile = pan_low_tiles(q, consts, 64)
    total = jnp.zeros((8, 128), F32)
    for j in range(12):
        d_out[:, 128 * j : 128 * j + 128] = (
            pan_ext[8:56, 128 * j : 128 * j + 128] - low_tile[j][0:48]
        )
        for k in range(6):
            total = total + low_tile[j][8 * k : 8 * k + 8]
    zero = jnp.zeros((16, 128), F32)
    back = [low_tile[j][48:64] for j in range(12)] + [zero]
    lhs = jnp.concatenate(
        [
            jnp.concatenate(
                back[4 * t : 4 * t + 4] + [edge(back[4 * t + 4], back[(4 * t + 12) % 13])], axis=1
            )
            for t in range(3)
        ],
        axis=0,
    )
    main = dot3(lhs, back_hi[...], back_lo[...])
    rim = dot3(edge(back[0], back[11]), back_hi[512:640], back_lo[512:640])
    for t in range(3):
        ts[:, 128 * t : 128 * t + 128] = main[16 * t : 16 * t + 16]
    ts[:, 384:512] = rim
    return total


def column_mask(block):
    at = lane((1, 512))
    left = jnp.where(block == 0, 0.0, 1.0)
    right = jnp.where(block == BLOCKS - 1, 0.0, 1.0)
    return jnp.where(at >= 448, left, jnp.where(at >= 384, right, 1.0))


def mean_row(xs, i):
    total = None
    for t in range(5):
        term = float(MEAN_TAPS[t]) * xs[i + t]
        total = term if total is None else total + term
    return total


def gram_cols(lanes, x):
    y = lanes[4:5, :] * x
    for t in range(-4, 5):
        if t:
            y = y + lanes[t + 4 : t + 5, :] * shifted(x, t)
    return y


OWN = range(2, 14)
RIM = (0, 1, 14, 15)
EARLY = range(2, 10)


def gram_row(xc, i, among, scale):
    total = None
    for j in among:
        if GRAM_ROWS[i, j] != 0.0:
            term = float(scale * GRAM_ROWS[i, j]) * xc[j]
            total = term if total is None else total + term
    return total


def add_products(acc, xs, ys, ts, ones, i):
    x = xs[i + 6]
    for j in range(8):
        acc[j] = acc[j] + fold(x * ys[i, j : j + 1, :])
    acc[8] = acc[8] + fold(x * ts[i : i + 1, :])
    acc[9] = acc[9] + float(ROW_SUM[i]) * fold(x * ones)


def early_compute(e, consts, ts, xs, xc, ys, vl, lvp, sums):
    lanes = consts[13]
    for i in range(12):
        row = vnir_row(e, 1, i)
        xs[i + 8] = row
        xc[i + 2] = gram_cols(lanes, row)
    acc = [jnp.zeros((8, 128), F32) for _ in range(10)]
    for i in OWN:
        ys[i] = gram_row(xc, i, OWN, 1.0)
    for i in OWN:
        add_products(acc, xs, ys, ts, lanes[9:10, :], i)
    for k in range(10):
        sums[k] = acc[k]
    means = {i: mean_row(xs, i + 6) for i in EARLY}
    for i in EARLY:
        vl[i] = col_filter(means[i], MEAN_TAPS)[:, 0:384]
    for i in range(12):
        lvp[i] = total_of([float(G3[k - i + 6]) * means[k] for k in EARLY if abs(k - i) <= 6])


def front_compute(e, consts, sums_ref, r, c, ts, dd, xs, xc, ys, lvs, vl, lvp, swu, dl, rl):
    third_hi, third_lo, joint_hi, joint_lo, lanes = consts[9:14]
    for k in range(28):
        if k < 8:
            xs[k] = vnir_row(e, 0, k + 4)
        elif k >= 20:
            xs[k] = vnir_row(e, 2, k - 20)
    up_keep = jnp.where(r == 0, 0.0, 1.0)
    down_keep = jnp.where(r == STRIPS - 1, 0.0, 1.0)
    mask = column_mask(c)
    means = {}
    for i in range(-6, 18):
        if i not in EARLY:
            row = mean_row(xs, i + 6)
            means[i] = row * up_keep if i < 0 else (row * down_keep if i >= 12 else row)
    at = lane((8, 128))
    left = (at >= 16) & (at < 18) & (c == 0)
    right = (at >= 110) & (at < 112) & (c == BLOCKS - 1)
    rows = []
    for i in range(12):
        total = lvp[i] + total_of(
            [float(G3[k - i + 6]) * means[k] for k in means if abs(k - i) <= 6]
        )
        rows.append(total)
    lhs = []
    for t in range(3):
        for i in range(12):
            tile = [rows[i][:, 128 * k : 128 * k + 128] for k in range(4)]
            rim = jnp.where(at < 8, tile[t + 1], jnp.where(at >= 120, tile[(t + 3) % 4], 0.0))
            if t == 0:
                rim = jnp.where(left, pltpu.roll(tile[0], 16, 1), rim)
            if t == 2:
                rim = jnp.where(right, pltpu.roll(tile[2], 112, 1), rim)
            lhs.append(jnp.concatenate([tile[t], rim], axis=1))
    lowered = dot3(jnp.concatenate(lhs, axis=0), joint_hi[...], joint_lo[...])
    for i in range(12):
        low = jnp.concatenate([lowered[96 * t + 8 * i : 96 * t + 8 * i + 8] for t in range(3)], axis=1)
        lvs[i] = low
        if i in EARLY:
            vl[i] = vl[i] - low
        else:
            vl[i] = col_filter(means[i], MEAN_TAPS)[:, 0:384] - low
    for i in RIM:
        xc[i] = gram_cols(lanes, xs[i + 6])
    acc = [sums_ref[k] for k in range(10)]
    for i in RIM:
        ys[i] = gram_row(xc, i, OWN, 2.0) + gram_row(xc, i, RIM, 1.0)
        add_products(acc, xs, ys, ts, lanes[9:10, :], i)
    sums = {k: acc[k] for k in range(10)}
    sums[10] = sums_ref[10]
    dcol = total_of([float(G3[t]) * dd[t + 2 : t + 14, :] for t in range(13)]) * mask
    low_d = col_filter(dcol, G3)[:, 0:384]
    dl[...] = dd[8:20, 0:384] - low_d
    ts[0:12, 0:384] = low_d
    srow = [
        swir_row(e, *at)
        for at in ((0, 2), (0, 3), (1, 0), (1, 1), (1, 2), (1, 3), (2, 0), (2, 1))
    ]
    up = []
    for m in range(4):
        for p in range(3):
            total = None
            for t in range(5):
                if C3[t, p] != 0.0:
                    term = float(C3[t, p]) * srow[m + t]
                    total = term if total is None else total + term
            up.append(total)
    swu[...] = dot3(jnp.concatenate(up, axis=0), third_hi[...], third_lo[...])
    acc = [jnp.zeros((8, 128), F32) for _ in range(22)]
    for i in range(12):
        lv = lvs[i]
        sw = swu[8 * i : 8 * i + 8, :]
        ld = ts[i : i + 1, 0:384]
        for j in range(8):
            other = lvs[i, j : j + 1, :]
            acc[j] = acc[j] + fold(lv * other)
            acc[8 + j] = acc[8 + j] + fold(sw * other)
        acc[16] = acc[16] + fold(lv * ld)
        acc[17] = acc[17] + fold(sw * ld)
        acc[18] = acc[18] + fold(lv)
        acc[19] = acc[19] + fold(sw)
        acc[20] = acc[20] + fold(ld)
        acc[21] = acc[21] + fold(ld * ld)
    for k in range(22):
        sums[16 + k] = acc[k]
    at = lane((8, 128))
    packed = jnp.zeros((8, 128), F32)
    for k, value in sums.items():
        packed = jnp.where(at == k, jnp.sum(value, axis=1, keepdims=True), packed)
    rl[...] = packed


def upsample(xs, consts, zs, up_out):
    fine_hi, fine_lo = consts[7:9]
    for m in range(12):
        for p in range(4):
            total = None
            for t in range(5):
                if C4[t, p] != 0.0:
                    term = float(C4[t, p]) * xs[m + t + 6]
                    total = term if total is None else total + term
            for tile in range(4):
                zs[tile, pl.ds(4 * m + p, 8, stride=48), :] = total[
                    :, 128 * tile : 128 * tile + 128
                ]

    @pl.loop(0, BANDS)
    def _(b):
        at = pl.ds(pl.multiple_of(b * 48, 48), 48)
        z = [zs[k, at, :] for k in range(4)]
        lhs = jnp.concatenate(
            [
                jnp.concatenate([z[k], edge(z[k + 1], z[(k + 3) % 4])], axis=1)
                for k in range(3)
            ],
            axis=0,
        )
        up = dot3(lhs, fine_hi[...], fine_lo[...])
        for k in range(3):
            up_out[at, 512 * k : 512 * k + 512] = up[48 * k : 48 * k + 48]


def front_kernel(pan, vnir, swir, *rest):
    hbm_consts = rest[:NUM_CONST]
    rt, up_out, d_out, vl, swu, dl = rest[NUM_CONST : NUM_CONST + 6]
    rest = rest[NUM_CONST + 6 :]
    consts = rest[:NUM_CONST]
    (vs, ss, sb, e, pe, xs, xc, ys, ts, dd, lvs, zs, sums, rl, g1, mid, g2, lvp, down, dup, ddn) = rest[
        NUM_CONST : NUM_CONST + 21
    ]
    (csem, lsem, ssem, rsem, fsem, hsem, psem, qsem, g1s, g1r, g2s, g2r, dsem, tsem) = rest[NUM_CONST + 21 :]
    r = lax.axis_index("rows")
    c = lax.axis_index("band")

    def remote(src, dst, send, recv, row, block):
        return pltpu.make_async_remote_copy(
            src_ref=src, dst_ref=dst, send_sem=send, recv_sem=recv,
            device_id=(row, block), device_id_type=MESH,
        )

    rl8 = lax.rem(r, 8)
    base = r - rl8
    barrier = pltpu.get_barrier_semaphore()

    def greet(row, block):
        pl.semaphore_signal(barrier, inc=1, device_id=(row, block), device_id_type=MESH)

    core = lax.rem(rl8, 2)
    x = lax.div(rl8, 2)
    y_hi, z = lax.div(c, 4), lax.rem(c, 4)
    y_lo = lax.div(r, 8)
    y = 2 * y_hi + y_lo

    def step_one(dx, dcore):
        return 2 * lax.rem(x + dx, 4) + lax.rem(core + dcore, 2)

    def step_two(dy, dz):
        return 4 * lax.rem(y + dy, 4) + lax.rem(z + dz, 4)

    def place_two(slot):
        y2 = lax.div(slot, 4)
        return 8 * lax.rem(y2, 2) + rl8, 4 * lax.div(y2, 2) + lax.rem(slot, 4)

    near = lambda d: min(d, 4 - d)
    ones = sorted(
        [(dx, dc) for dx in range(4) for dc in range(2) if dx or dc], key=lambda d: (-near(d[0]), -d[1])
    )
    twos = sorted(
        [(dy, dz) for dy in range(4) for dz in range(4) if dy or dz],
        key=lambda d: (-near(d[0]) - near(d[1]), d),
    )
    first = [(base + step_one(*d), c) for d in ones]
    second = [place_two(step_two(*d)) for d in twos]
    strips = ((1, r < STRIPS - 1), (-1, r > 0))
    blocks = ((1, c < BLOCKS - 1), (-1, c > 0))
    beside = [(r + dr, c + dc, ok & also) for dr, ok in strips for dc, also in blocks]
    beside += [(r + dr, c, ok) for dr, ok in strips]
    greetings = len(second) + len(first)
    for row, block in second:
        greet(row, block)
    for row, block, ok in beside:
        pl.when(ok)(functools.partial(greet, row, block))
        greetings = greetings + jnp.where(ok, 1, 0)
    for row, block in first:
        greet(row, block)

    loads = [
        pltpu.make_async_copy(vnir, vs.at[pl.ds(0, 288)], lsem.at[0]),
        pltpu.make_async_copy(swir.at[0], ss, lsem.at[1]),
        pltpu.make_async_copy(pan, pe.at[pl.ds(8, 48), pl.ds(0, 1536)], lsem.at[2]),
    ]
    for copy in loads:
        copy.start()
    const_loads = [
        pltpu.make_async_copy(hbm_consts[k], consts[k], csem.at[k]) for k in range(NUM_CONST)
    ]

    @pl.when(r == 0)
    def _():
        pe[0:8, :] = jnp.zeros((8, 1792), F32)
        e[0, 3:7] = jnp.zeros((4, 64, 128), F32)
        dup[...] = jnp.zeros((8, 512), F32)

    @pl.when(r == STRIPS - 1)
    def _():
        pe[56:64, :] = jnp.zeros((8, 1792), F32)
        e[2, 0:4] = jnp.zeros((4, 64, 128), F32)
        ddn[...] = jnp.zeros((8, 512), F32)

    @pl.when(c == 0)
    def _():
        pe[:, 1536:1664] = jnp.zeros((64, 128), F32)

    @pl.when(c == BLOCKS - 1)
    def _():
        pe[:, 1664:1792] = jnp.zeros((64, 128), F32)

    loads[0].wait()
    loads[1].wait()
    pack(vs, ss, sb)
    loads[2].wait()
    pl.semaphore_wait(barrier, greetings)

    def pan_cols(side):
        src = pe.at[pl.ds(8, 48), pl.ds(1408, 128)] if side == 0 else pan_first
        dst = pe.at[pl.ds(8, 48), pl.ds(1536 + 128 * side, 128)]
        block = c + 1 if side == 0 else c - 1
        return remote(src, dst, psem.at[side], qsem.at[side], r, block)

    pan_first = pe.at[pl.ds(8, 48), pl.ds(0, 128)]

    def pan_part(side, cols, n):
        src = pe.at[pl.ds(48, 8), cols] if side == 0 else pe.at[pl.ds(8, 8), cols]
        dst = pe.at[pl.ds(0, 8), cols] if side == 0 else pe.at[pl.ds(56, 8), cols]
        row = r + 1 if side == 0 else r - 1
        return remote(src, dst, psem.at[n + side], qsem.at[n + side], row, c)

    def pan_rows(side):
        return pan_part(side, pl.ds(0, 1536), 2)

    def pan_corner(side, across):
        src = pe.at[
            pl.ds(48 if side == 0 else 8, 8), pl.ds(1408 if across == 0 else 0, 128)
        ]
        dst = pe.at[pl.ds(0 if side == 0 else 56, 8), pl.ds(1536 + 128 * across, 128)]
        row = r + 1 if side == 0 else r - 1
        block = c + 1 if across == 0 else c - 1
        n = 2 * side + across
        return remote(src, dst, dsem.at[n], tsem.at[n], row, block)

    def mean_rows(side):
        src, dst = (down, dup) if side == 0 else (dd.at[pl.ds(8, 8)], ddn)
        row = r + 1 if side == 0 else r - 1
        return remote(src, dst, psem.at[6 + side], qsem.at[6 + side], row, c)

    has_below, has_above = r < STRIPS - 1, r > 0
    has_right, has_left = c < BLOCKS - 1, c > 0
    to = {(s, a): (has_below if s == 0 else has_above) & (has_right if a == 0 else has_left)
          for s in range(2) for a in range(2)}
    into = {(s, a): (has_above if s == 0 else has_below) & (has_left if a == 0 else has_right)
            for s in range(2) for a in range(2)}

    def when(cond, action):
        @pl.when(cond)
        def _():
            action()

    when(has_right, lambda: pan_cols(0).start())
    when(has_left, lambda: pan_cols(1).start())
    for key in to:
        when(to[key], functools.partial(lambda key: pan_corner(*key).start(), key))

    def band_rows(b):
        return pl.ds(pl.multiple_of(b * 8, 8), 8)

    turns = [(0, 0), (1, 2), (1, 1), (1, 3), (1, 0), (0, 2), (0, 1), (0, 3)]

    def band_at(dyh, dz):
        return 4 * lax.rem(y_hi + dyh, 2) + lax.rem(z + dz, 4)

    def block_send(k):
        block = band_at(*turns[k])
        return remote(sb.at[block], e.at[1, pl.ds(0, TILES), band_rows(c)], ssem.at[k], rsem.at[k], r, block)

    def block_recv(k):
        b = band_at(turns[k][0], 4 - turns[k][1])
        return remote(sb.at[0], e.at[1, pl.ds(0, TILES), band_rows(b)], ssem.at[k], rsem.at[k], r, c)

    def forward(k, side):
        b = band_at(turns[k][0], 4 - turns[k][1])
        part = pl.ds(3 - 3 * side, 4)
        dst = e.at[2 * side, part, band_rows(b)]
        src = sb.at[c, part] if k == 0 else e.at[1, part, band_rows(b)]
        row = r + 1 if side == 0 else r - 1
        return remote(src, dst, fsem.at[side, k], hsem.at[side, k], row, c)

    for k in range(1, 8):
        block_send(k).start()
    own = pltpu.make_async_copy(sb.at[c], e.at[1, pl.ds(0, TILES), band_rows(c)], lsem.at[3])
    own.start()
    when(has_below, lambda: forward(0, 0).start())
    when(has_above, lambda: forward(0, 1).start())
    when(has_below, lambda: pan_rows(0).start())
    when(has_above, lambda: pan_rows(1).start())

    for copy in const_loads:
        copy.start()

    for copy in const_loads:
        copy.wait()
    when(has_left, lambda: pan_cols(0).wait_recv())
    when(has_right, lambda: pan_cols(1).wait_recv())
    when(has_above, lambda: pan_rows(0).wait_recv())
    when(has_below, lambda: pan_rows(1).wait_recv())
    for key in into:
        when(into[key], functools.partial(lambda key: pan_corner(*key).wait_recv(), key))
    mean_stage(pe, consts, dd, down)
    when(has_below, lambda: mean_rows(0).start())
    when(has_above, lambda: mean_rows(1).start())
    for k in range(7, 0, -1):
        block_recv(k).wait_recv()
        when(has_below, functools.partial(lambda k: forward(k, 0).start(), k))
        when(has_above, functools.partial(lambda k: forward(k, 1).start(), k))
    own.wait()
    sums[10] = pan_stage(pe, consts, d_out, ts)
    early_compute(e, consts, ts, xs, xc, ys, vl, lvp, sums)
    for k in range(8):
        when(has_above, functools.partial(lambda k: forward(k, 0).wait_recv(), k))
        when(has_below, functools.partial(lambda k: forward(k, 1).wait_recv(), k))

    when(has_above, lambda: mean_rows(0).wait_recv())
    when(has_below, lambda: mean_rows(1).wait_recv())
    dd[0:8] = dup[...]
    dd[20:28] = ddn[...]
    front_compute(e, consts, sums, r, c, ts, dd, xs, xc, ys, lvs, vl, lvp, swu, dl, rl)

    me_two = 4 * y + z

    def sum_one(n):
        row, block = first[n]
        return remote(rl, g1.at[rl8], g1s.at[n], g1r.at[n], row, block)

    def sum_one_recv(n):
        dx, dc = ones[n]
        return remote(rl, g1.at[step_one(4 - dx, 2 - dc)], g1s.at[n], g1r.at[n], r, c)

    def sum_two(n):
        row, block = second[n]
        return remote(mid, g2.at[me_two], g2s.at[n], g2r.at[n], row, block)

    def sum_two_recv(n):
        dy, dz = twos[n]
        return remote(mid, g2.at[step_two(4 - dy, 4 - dz)], g2s.at[n], g2r.at[n], r, c)

    for n in range(7):
        sum_one(n).start()
    g1[rl8] = rl[...]
    for n in range(7):
        sum_one_recv(n).wait_recv()
    total = g1[0]
    for k in range(1, 8):
        total = total + g1[k]
    mid[...] = total
    for n in range(15):
        sum_two(n).start()
    g2[me_two] = total
    upsample(xs, consts, zs, up_out)

    for key in to:
        when(to[key], functools.partial(lambda key: pan_corner(*key).wait_send(), key))
    when(has_below, lambda: mean_rows(0).wait_send())
    when(has_above, lambda: mean_rows(1).wait_send())
    for k in range(1, 8):
        block_send(k).wait_send()
        sum_one(k - 1).wait_send()
    for n in range(15):
        sum_two(n).wait_send()
    when(has_right, lambda: pan_cols(0).wait_send())
    when(has_left, lambda: pan_cols(1).wait_send())
    for side, cond in ((0, has_below), (1, has_above)):
        when(cond, functools.partial(lambda side: pan_rows(side).wait_send(), side))
        for k in range(8):
            when(cond, functools.partial(lambda k, side: forward(k, side).wait_send(), k, side))

    for n in range(15):
        sum_two_recv(n).wait_recv()
    total = g2[0]
    for k in range(1, 16):
        total = total + g2[k]
    rt[...] = total


def front(pan, vnir, swir):
    return pl.pallas_call(
        front_kernel,
        name="front",
        out_shape=[
            VM((8, 128), F32),
            VM((384, 1536), F32),
            VM((48, 1536), F32),
            VM((12, 8, 384), F32),
            VM((96, 384), F32),
            VM((12, 384), F32),
        ],
        in_specs=[pl.BlockSpec(memory_space=pl.ANY)] * (3 + NUM_CONST),
        out_specs=[pl.BlockSpec(memory_space=VM)] * 6,
        scratch_shapes=[VM(k.shape, BF16 if k.dtype == ml_dtypes.bfloat16 else F32) for k in CONSTANTS]
        + [
            VM((384, 128), F32),
            VM((4, 1024), F32),
            VM((8, TILES, 8, 128), F32),
            VM((3, TILES, 64, 128), F32),
            VM((64, 1792), F32),
            VM((28, 8, 512), F32),
            VM((16, 8, 512), F32),
            VM((16, 8, 512), F32),
            VM((16, 512), F32),
            VM((32, 512), F32),
            VM((12, 8, 384), F32),
            VM((4, 384, 128), F32),
            VM((11, 8, 128), F32),
            VM((8, 128), F32),
            VM((8, 8, 128), F32),
            VM((8, 128), F32),
            VM((16, 8, 128), F32),
            VM((12, 8, 512), F32),
            VM((8, 512), F32),
            VM((8, 512), F32),
            VM((8, 512), F32),
            pltpu.SemaphoreType.DMA((NUM_CONST,)),
            pltpu.SemaphoreType.DMA((4,)),
            pltpu.SemaphoreType.DMA((8,)),
            pltpu.SemaphoreType.DMA((8,)),
            pltpu.SemaphoreType.DMA((2, 8)),
            pltpu.SemaphoreType.DMA((2, 8)),
            pltpu.SemaphoreType.DMA((8,)),
            pltpu.SemaphoreType.DMA((8,)),
            pltpu.SemaphoreType.DMA((8,)),
            pltpu.SemaphoreType.DMA((8,)),
            pltpu.SemaphoreType.DMA((16,)),
            pltpu.SemaphoreType.DMA((16,)),
            pltpu.SemaphoreType.DMA((4,)),
            pltpu.SemaphoreType.DMA((4,)),
        ],
        compiler_params=pltpu.CompilerParams(
            collective_id=0, has_side_effects=True, vmem_limit_bytes=56 << 20
        ),
    )(pan, vnir, swir, *[jnp.asarray(k) for k in CONSTANTS])


def solve_spd(a, b):
    a = [list(row) for row in a]
    inverse = []
    factor = [[None] * 8 for _ in range(8)]
    for j in range(8):
        inv = 1.0 / a[j][j]
        inverse.append(inv)
        for i in range(j + 1, 8):
            factor[i][j] = a[i][j] * inv
        for i in range(j + 1, 8):
            for k in range(j + 1, i + 1):
                a[i][k] = a[i][k] - factor[i][j] * a[k][j]
    z = list(b)
    for j in range(8):
        for i in range(j + 1, 8):
            z[i] = z[i] - factor[i][j] * z[j]
    z = [z[j] * inverse[j] for j in range(8)]
    for j in range(7, -1, -1):
        for i in range(j):
            z[i] = z[i] - factor[j][i] * z[j]
    return z


def solve_first(rt, cb):
    for k in range(11):
        cb[k] = jnp.broadcast_to(rt[:, k : k + 1], (8, 128))
    mean = [cb[9, i : i + 1, :] * (1.0 / N1) for i in range(8)]
    mean_p = jnp.sum(cb[10], axis=0, keepdims=True) * (1.0 / N1)
    a = [
        [
            (cb[j, i : i + 1, :] + cb[i, j : j + 1, :]) * (0.5 / N1) - mean[i] * mean[j]
            for j in range(i + 1)
        ]
        for i in range(8)
    ]
    b = [cb[8, i : i + 1, :] * (1.0 / N1) - mean[i] * mean_p for i in range(8)]
    w = solve_spd(a, b)
    scale = 1.0 / total_of([b[i] * w[i] for i in range(8)])
    return [b[i] * scale for i in range(8)]


def solve_second(rt, cb, gain):
    for k in range(16, 38):
        cb[k] = jnp.broadcast_to(rt[:, k : k + 1], (8, 128))

    def at(k, i):
        return cb[k, i : i + 1, :]

    sum_d = at(36, 0)
    sum_dd = at(37, 0)
    q = [at(32, i) for i in range(8)]
    mean2 = [(at(34, i) + gain[i] * sum_d) * (1.0 / N2) for i in range(8)]
    a2 = [
        [
            (at(16 + j, i) + gain[i] * q[j] + gain[j] * q[i] + gain[i] * gain[j] * sum_dd) * (1.0 / N2)
            - mean2[i] * mean2[j]
            for j in range(i + 1)
        ]
        for i in range(8)
    ]
    swir_mean = cb[35] * (1.0 / N2)
    cross = [
        (cb[24 + i] + gain[i] * cb[33]) * (1.0 / N2) - mean2[i] * swir_mean for i in range(8)
    ]
    y = [jnp.sum(cross[i], axis=0, keepdims=True) * 0.125 for i in range(8)]
    v = solve_spd(a2, y)
    share = total_of([v[i] * cross[i] for i in range(8)]) / total_of([v[i] * y[i] for i in range(8)])
    return v, share


def wide(x, copies):
    return jnp.concatenate([x] * copies, axis=1)


def back_kernel(rt, up, d, vl, swu, dl, joined, joined_swir, cb, gs, out, rows_out, sem):
    def half_copy(b, h):
        half = pl.ds(24 * h, 24)
        return pltpu.make_async_copy(out.at[b, half], joined.at[b, half], sem.at[b, h])

    gain = solve_first(rt, cb)
    for b in range(8):
        gs[b] = jnp.broadcast_to(gain[b], (8, 128))

    @pl.loop(0, BANDS)
    def _(b):
        g = wide(gs[b], 2)
        rows = pl.multiple_of(b * 48, 48)
        for h in range(2):
            for i in range(3 * h, 3 * h + 3):
                for t in range(6):
                    at = slice(256 * t, 256 * t + 256)
                    out[b, 8 * i : 8 * i + 8, at] = (
                        up[pl.ds(rows + 8 * i, 8), at] + g * d[8 * i : 8 * i + 8, at]
                    )
            half_copy(b, h).start()

    gain = [gs[b, 0:1, :] for b in range(8)]
    v, share = solve_second(rt, cb, gain)
    row8 = lax.broadcasted_iota(jnp.int32, (8, 128), 0)
    v8 = jnp.zeros((8, 128), F32)
    for b in range(8):
        v8 = jnp.where(row8 == b, jnp.broadcast_to(v[b], (8, 128)), v8)
    v8 = wide(v8, 3)
    vg = wide(total_of([v[b] * gain[b] for b in range(8)]), 3)
    share3 = wide(share, 3)
    for i in range(12):
        detail = jnp.sum(v8 * vl[i], axis=0, keepdims=True) + vg * dl[i : i + 1, :]
        rows_out[i] = swu[8 * i : 8 * i + 8, :] + share3 * detail
    last = pltpu.make_async_copy(rows_out, joined_swir, sem.at[8, 0])
    last.start()

    @pl.loop(0, BANDS)
    def _(b):
        half_copy(b, 0).wait()
        half_copy(b, 1).wait()

    last.wait()


def back(rt, up, d, vl, swu, dl):
    return pl.pallas_call(
        back_kernel,
        name="back",
        out_shape=[
            jax.ShapeDtypeStruct((8, 48, 1536), F32),
            jax.ShapeDtypeStruct((12, 8, 384), F32),
        ],
        in_specs=[pl.BlockSpec(memory_space=VM)] * 6,
        out_specs=[pl.BlockSpec(memory_space=pl.ANY)] * 2,
        scratch_shapes=[
            VM((38, 8, 128), F32),
            VM((8, 8, 128), F32),
            VM((8, 48, 1536), F32),
            VM((12, 8, 384), F32),
            pltpu.SemaphoreType.DMA((9, 2)),
        ],
        compiler_params=pltpu.CompilerParams(vmem_limit_bytes=32 << 20),
    )(rt, up, d, vl, swu, dl)


def local(pan, vnir, swir):
    joined, rows = back(*front(pan, vnir.reshape(288, 128), swir))
    return joined, jnp.swapaxes(rows, 0, 1)


def solution(mesh):
    return jax.shard_map(
        local,
        mesh=mesh,
        in_specs=(P("rows", "band"), P("band", "rows", None), P("band", "rows", None)),
        out_specs=(P(None, "rows", "band"), P(None, "rows", "band")),
        check_vma=False,
    )
```
